32 devices in a mesh: gx: 4 (over y, core), gy: 8 (over z, x).
Axes of the slice: x: 2, y: 2, z: 4, core: 2. Of those that a mesh axis runs over, the one named last changes fastest.
Arguments:
- source: float32 [256, 128, 128], P('gx', 'gy'), may hold values from -6 to 6
- diagonal: float32 [256, 128, 128], P('gx', 'gy'), may hold values from 6.05 to 7
- face_x: float32 [256, 128, 128], P('gx', 'gy'), may hold values from 0.1 to 1
- face_y: float32 [256, 128, 128], P('gx', 'gy'), may hold values from 0.1 to 1
- face_z: float32 [256, 128, 128], P('gx', 'gy'), may hold values from 0.1 to 1
- iterates: float32 [8, 256, 128, 128], P(None, 'gx', 'gy'), may hold values from -0.3 to 0.3
- labels: int32 [256, 128], P('gx', 'gy'), may hold values from 0 to 7
Outputs:
- new_iterates: float32 [8, 256, 128, 128], P(None, 'gx', 'gy')
- new_residual: float32 [256, 128, 128], P('gx', 'gy')
The draws below stay inside these ranges and needn't reach their ends.
All inputs are finite; a program needn't handle non-finite values.
Results may differ from the reference program's by a relative error of at most 0.0003.
Values sent between devices are 32-bit elements; how exact they have to be, the bound alone decides.
No kernel may reach another device: no remote copies, remote signals or barrier semaphores. Data moves between devices by JAX's collectives and lax.ppermute only.
A program may use at most 128 MiB of HBM per device.

```python
import math
import jax
import jax.numpy as jnp
from jax import lax

NZ = 128
ENLARGE = 8
NX = 256
NY = 128


def set_ends(entries, stream_key, least, top_value):
    longest = entries.shape.index(max(entries.shape))
    spots = []
    for shift in (0, 1):
        where = [jax.random.randint(jax.random.fold_in(stream_key, axis), (), 0, length) for axis, length in enumerate(entries.shape)]
        where[longest] = (where[longest] + shift) % entries.shape[longest]
        spots.append(tuple(where))
    return entries.at[spots[0]].set(least).at[spots[1]].set(top_value)


def steps_of(own_key, dims, pieces, least, largest):
    gain = 1.0
    for axis_at, shards_of in pieces:
        heights = jax.random.uniform(jax.random.fold_in(jax.random.fold_in(own_key, 6), axis_at), (shards_of,), jnp.float32, least / len(pieces), largest / len(pieces))
        gain = gain * jnp.repeat(jnp.exp(heights), dims[axis_at] // shards_of).reshape((-1,) + (1,) * (len(dims) - 1 - axis_at))
    return gain


def centred(stream_key, extent, spread, most, shards=(), kind=jnp.bfloat16):
    values = jax.random.normal(stream_key, extent, jnp.float32) * spread
    if len(shards) > 0:
        values = steps_of(stream_key, extent, shards, -0.22, 0.18) * values
    return jnp.clip(values, min=-most, max=most).astype(kind)


def setup_inputs(seed: int = 0) -> dict:
    streams_of = jax.random.split(jax.random.key(seed), 8)
    source = centred(streams_of[0], (NX, NY, NZ), 1.0, 6.0, ((0, 4), (1, 8)), jnp.float32)
    diagonal = jnp.clip(6.05 + 0.9499998 * jax.random.uniform(streams_of[1], (NX, NY, NZ), jnp.float32) ** steps_of(streams_of[1], (NX, NY, NZ), ((0, 4), (1, 8)), -0.2, 0.2), 6.05, 7.0)
    face_x = jnp.clip(jnp.exp(math.log(1.0) - 2.3025851 * jax.random.uniform(streams_of[2], (NX, NY, NZ), jnp.float32) ** steps_of(streams_of[2], (NX, NY, NZ), ((0, 4), (1, 8)), -0.2, 0.2)), 0.1, 1.0)
    face_y = jnp.clip(jnp.exp(math.log(1.0) - 2.3025851 * jax.random.uniform(streams_of[3], (NX, NY, NZ), jnp.float32) ** steps_of(streams_of[3], (NX, NY, NZ), ((0, 4), (1, 8)), -0.2, 0.2)), 0.1, 1.0)
    face_z = jnp.clip(jnp.exp(math.log(1.0) - 2.3025851 * jax.random.uniform(streams_of[4], (NX, NY, NZ), jnp.float32) ** steps_of(streams_of[4], (NX, NY, NZ), ((0, 4), (1, 8)), -0.2, 0.2)), 0.1, 1.0)
    iterates = centred(streams_of[5], (ENLARGE, NX, NY, NZ), 0.05, 0.3, ((1, 4), (2, 8)), jnp.float32)
    labels = set_ends(jax.random.randint(streams_of[6], (NX, NY), 0, ENLARGE), jax.random.fold_in(streams_of[6], 1), 0, ENLARGE - 1).astype(jnp.int32)
    return dict(source=source, diagonal=diagonal, face_x=face_x, face_y=face_y, face_z=face_z, iterates=iterates, labels=labels)


basis_shift = 6.5

def stencil(values, face_x, face_y, face_z, diagonal):
    centre = values[..., 1:-1, 1:-1, :]
    result = diagonal * centre
    result = result - face_x[1:-1, 1:-1, :] * values[..., 2:, 1:-1, :] - face_x[:-2, 1:-1, :] * values[..., :-2, 1:-1, :]
    result = result - face_y[1:-1, 1:-1, :] * values[..., 1:-1, 2:, :] - face_y[1:-1, :-2, :] * values[..., 1:-1, :-2, :]
    widths = [(0, 0)] * (centre.ndim - 1) + [(1, 1)]
    padded = jnp.pad(centre, widths)
    lower_face = jnp.pad(face_z[..., :-1], ((0, 0), (0, 0), (1, 0)))
    return result - face_z * padded[..., 2:] - lower_face * padded[..., :-2]

def extend(array):
    return jnp.pad(array, [(0, 0)] * (array.ndim - 3) + [(1, 1), (1, 1), (0, 0)])

def operate(values, face_x, face_y, face_z, diagonal):
    return stencil(extend(values), extend(face_x), extend(face_y), face_z, diagonal)

def finish(gram, project):
    highest = lax.Precision.HIGHEST
    lower = jnp.linalg.cholesky(gram)
    ident = jnp.eye(gram.shape[0], dtype=gram.dtype)
    inverse = lax.linalg.triangular_solve(lower, ident, left_side=True, lower=True)
    reduced = jnp.dot(jnp.dot(inverse, project, precision=highest), inverse.T, precision=highest)
    reduced = 0.5 * (reduced + reduced.T)
    target = jnp.dot(inverse, gram[:, :ENLARGE], precision=highest)
    factor = jnp.linalg.cholesky(reduced)
    middle = lax.linalg.triangular_solve(factor, target, left_side=True, lower=True)
    solved = lax.linalg.triangular_solve(factor, middle, left_side=True, lower=True, transpose_a=True)
    return jnp.dot(inverse.T, solved, precision=highest)

def reference(source, diagonal, face_x, face_y, face_z, iterates, labels):
    highest = lax.Precision.HIGHEST
    summed = jnp.sum(iterates, axis=0)
    residual = source - operate(summed, face_x, face_y, face_z, diagonal)
    onehot = (labels[None] == jnp.arange(ENLARGE)[:, None, None]).astype(residual.dtype)
    blocks = residual[None] * onehot[..., None]
    applied = operate(blocks, face_x, face_y, face_z, diagonal)
    powered = applied - basis_shift * blocks
    second = operate(powered, face_x, face_y, face_z, diagonal)
    basis = jnp.concatenate([blocks, powered], axis=0)
    image = jnp.concatenate([applied, second], axis=0)
    gram = jnp.einsum('aijk,bijk->ab', basis, basis, precision=highest)
    project = jnp.einsum('aijk,bijk->ab', basis, image, precision=highest)
    coeffs = finish(gram, project)
    new_iterates = iterates + jnp.einsum('ab,aijk->bijk', coeffs, basis, precision=highest)
    carried = jnp.sum(coeffs, axis=1)
    new_residual = residual - jnp.einsum('a,aijk->ijk', carried, image, precision=highest)
    return (new_iterates, new_residual)
```

```python
import functools

import jax
import jax.numpy as jnp
from jax import lax
from jax.experimental import pallas as pl
from jax.experimental.pallas import tpu as pltpu
from jax.sharding import PartitionSpec as P

ENLARGE = 8
SHIFT = 6.5
F32 = jnp.float32
HIGHEST = lax.Precision.HIGHEST
PAIRS = [(j, k) for j in range(ENLARGE) for k in range(j, ENLARGE)]
GHOST = 2
XROWS = 16
VMEM_LIMIT = 40 * 1024 * 1024


def iota(shape, dim):
    return lax.broadcasted_iota(jnp.int32, shape, dim)


def even_pairs(count):
    return [(i, i ^ 1) for i in range(count) if (i ^ 1) < count]


def odd_pairs(count):
    return [(i, ((i - 1) ^ 1) + 1) for i in range(1, count) if ((i - 1) ^ 1) + 1 < count]


def whole(count):
    return [pl.BlockSpec(memory_space=pltpu.VMEM)] * count


def params():
    return pltpu.CompilerParams(vmem_limit_bytes=VMEM_LIMIT)


def sum_kernel(steps, it_ref, *refs):
    lows, highs = refs[0:6], refs[6:12]
    s_ref, even_ref, odd_ref = refs[12:]
    step = pl.program_id(0)
    total = it_ref[0]
    for j in range(1, ENLARGE):
        total = total + it_ref[j]
    s_ref[...] = total
    width = total.shape[0]

    def pack(ref, at, values):
        ref[at : at + values.shape[0]] = values

    def put(dest, low):
        src, dg, fx, fy, fz, lb = lows if low else highs
        if low:
            take = lambda a, n: a[0:n]
        else:
            take = lambda a, n: a[width - n : width]
        pack(dest, 0, take(total, 3))
        pack(dest, 3, take(fx, 3))
        at = 6
        for field in (src, dg, fy, fz, lb):
            pack(dest, at, take(field, 2))
            at += 2

    parity = lax.rem(lax.axis_index("gx"), 2)

    @pl.when(jnp.logical_and(step == 0, parity == 0))
    def _():
        put(odd_ref, True)

    @pl.when(jnp.logical_and(step == 0, parity == 1))
    def _():
        put(even_ref, True)

    @pl.when(jnp.logical_and(step == steps - 1, parity == 0))
    def _():
        put(even_ref, False)

    @pl.when(jnp.logical_and(step == steps - 1, parity == 1))
    def _():
        put(odd_ref, False)


def sum_and_edges(iterates, fields):
    _, nx, ny, nz = iterates.shape
    width = 8
    steps = nx // width
    block = (width, ny, nz)
    low = pl.BlockSpec(block, lambda i: (0, 0, 0))
    high = pl.BlockSpec(block, lambda i: (steps - 1, 0, 0))
    edge = jax.ShapeDtypeStruct((XROWS, ny, nz), F32)
    edge_spec = pl.BlockSpec((XROWS, ny, nz), lambda i: (0, 0, 0))
    return pl.pallas_call(
        functools.partial(sum_kernel, steps),
        grid=(steps,),
        in_specs=[pl.BlockSpec((ENLARGE,) + block, lambda i: (0, i, 0, 0))] + [low] * 6 + [high] * 6,
        out_specs=[pl.BlockSpec(block, lambda i: (i, 0, 0)), edge_spec, edge_spec],
        out_shape=[jax.ShapeDtypeStruct((nx, ny, nz), F32), edge, edge],
        compiler_params=params(),
        name="sum_and_edges",
    )(iterates, *fields, *fields)


def partial_kernel(
    nx, ny, xpad, gx, gy,
    s_in, src_in, dg_in, fx_in, fy_in, fz_in, lb_in, xe_ref, xo_ref,
    t_out, s_out, fx_out, fy_out, dg_out, fz_out, lb_out, ye_ref, yo_ref,
    src_ext,
):
    g = GHOST
    nz = s_in.shape[-1]
    lane = iota((ny, nz), 1)
    row = iota((ny, nz), 0)
    even_x = lax.rem(lax.axis_index("gx"), 2) == 0
    last_x = lax.axis_index("gx") == gx - 1
    last_y = lax.axis_index("gy") == gy - 1

    def rows(i):
        return pl.ds(pl.multiple_of(i * ny, ny), ny)

    def low(r):
        return jnp.where(even_x, xo_ref[r], xe_ref[r])

    def high(r):
        return jnp.where(even_x, xe_ref[r], xo_ref[r])

    top = jnp.logical_and(last_y, row == ny - 1)

    def fy_of(values):
        return jnp.where(top, 0.0, values)

    def fz_of(values):
        return jnp.where(lane == nz - 1, 0.0, values)

    s_low = [low(r) for r in range(3)]
    s_high = [high(r) for r in range(3)]
    fx_low = [low(3 + r) for r in range(3)]
    fx_high = [high(3 + r) for r in range(3)]
    for e in range(2):
        for side, at, pick in ((0, e, low), (1, g + nx + e, high)):
            s_out[rows(at)] = s_low[1 + e] if side == 0 else s_high[e]
            fx_out[rows(at)] = fx_low[1 + e] if side == 0 else fx_high[e]
            src_ext[rows(at)] = pick(6 + e)
            dg_out[rows(at)] = pick(8 + e)
            fy_out[rows(at)] = fy_of(pick(10 + e))
            fz_out[rows(at)] = fz_of(pick(12 + e))
            lb_out[rows(at)] = pick(14 + e)
    zero = jnp.zeros((ny, nz), F32)
    for at in range(nx + 2 * g, xpad):
        for ref in (t_out, s_out, fx_out, fy_out, dg_out, fz_out, lb_out):
            ref[rows(at)] = zero

    def copy(i, carry):
        at = rows(i + g)
        s_out[at] = s_in[i]
        fx_out[at] = fx_in[i]
        dg_out[at] = dg_in[i]
        fy_out[at] = fy_of(fy_in[i])
        fz_out[at] = fz_of(fz_in[i])
        lb_out[at] = lb_in[i]
        src_ext[at] = src_in[i]
        return carry

    lax.fori_loop(0, nx, copy, 0, unroll=4)

    @pl.when(last_x)
    def _():
        fx_out[rows(g + nx - 1)] = zero

    def partial(at, s, sp, sm, fxp, fxm):
        fy = fy_out[at]
        fz = fz_out[at]
        fys = fy * s
        ys = jnp.where(row == ny - 1, 0.0, fy * pltpu.roll(s, ny - 1, 0))
        ys = ys + jnp.where(row == 0, 0.0, pltpu.roll(fys, 1, 0))
        zs = fz * pltpu.roll(s, nz - 1, 1) + pltpu.roll(fz * s, 1, 1)
        return src_ext[at] - (dg_out[at] * s - fxp * sp - fxm * sm - ys - zs)

    def body(i, carry):
        at = rows(i)
        t_out[at] = partial(
            at, s_out[at], s_out[rows(i + 1)], s_out[rows(i - 1)], fx_out[at], fx_out[rows(i - 1)]
        )
        return carry

    at = rows(0)
    t_out[at] = partial(at, s_out[at], s_out[rows(1)], s_low[0], fx_out[at], fx_low[0])
    end = nx + 2 * g - 1
    at = rows(end)
    t_out[at] = partial(at, s_out[at], s_high[2], s_out[rows(end - 1)], fx_out[at], fx_out[rows(end - 1)])
    lax.fori_loop(1, end, body, 0, unroll=2)

    even_y = lax.rem(lax.axis_index("gy"), 2) == 0

    def pack(dest, is_high):
        first = jnp.where(is_high, ny - 1, 0)
        second = jnp.where(is_high, ny - 2, 1)
        between = jnp.where(is_high, ny - 2, 0)

        def line(ref, y):
            return ref[pl.ds(y, xpad, stride=ny), :]

        blocks = (
            line(t_out, first),
            line(s_out, first),
            line(fy_out, first),
            line(fx_out, first),
            line(fy_out, between) * line(t_out, second),
            line(dg_out, first),
            line(fz_out, first),
        )
        for b, values in enumerate(blocks):
            dest[b * xpad : (b + 1) * xpad] = values
        spot = iota((xpad, nz), 0) == iota((xpad, nz), 1)
        one = jnp.sum(jnp.where(spot, line(lb_out, first), 0.0), axis=0, keepdims=True)
        two = jnp.sum(jnp.where(spot, line(lb_out, second), 0.0), axis=0, keepdims=True)
        which = iota((8, nz), 0)
        dest[7 * xpad : 7 * xpad + 8] = jnp.where(which == 0, one, jnp.where(which == 1, two, 0.0))

    pack(ye_ref, even_y)
    pack(yo_ref, jnp.logical_not(even_y))


def partial_and_edges(total, fields, xe, xo, xpad, gx, gy):
    nx, ny, nz = total.shape
    ext = jax.ShapeDtypeStruct((xpad * ny, nz), F32)
    pack = jax.ShapeDtypeStruct((7 * xpad + 8, nz), F32)
    return pl.pallas_call(
        functools.partial(partial_kernel, nx, ny, xpad, gx, gy),
        in_specs=whole(9),
        out_specs=whole(9),
        out_shape=[ext] * 7 + [pack] * 2,
        scratch_shapes=[pltpu.VMEM((xpad * ny, nz), F32)],
        compiler_params=params(),
        name="partial_and_edges",
    )(total, *fields, xe, xo)


def powers_kernel(
    nx, ny, xpad, devices,
    t_ref, s_ref, fx_ref, fy_ref, dg_ref, fz_ref, lb_ref, ye_ref, yo_ref,
    p_out, q_out, r_out, gram_out,
    rex, fyx, lbx, pex, rhalo, rin, lab1, lab2, labin, accs,
):
    g = GHOST
    nz = t_ref.shape[-1]
    ext = nx + 2 * g
    pitch = ny + 16
    even_y = lax.rem(lax.axis_index("gy"), 2) == 0

    def at16(i):
        return pl.ds(pl.multiple_of(i * ny, ny), ny)

    def copy(i, carry):
        base = pl.multiple_of(i * pitch + 8, 8)
        rex[pl.ds(base, ny)] = t_ref[at16(i)]
        fyx[pl.ds(base, ny)] = fy_ref[at16(i)]
        lbx[pl.ds(base, ny)] = lb_ref[at16(i)]
        return carry

    lax.fori_loop(0, xpad, copy, 0, unroll=4)

    def packed(side, b, start=0, count=None):
        count = xpad if count is None else count
        span = slice(b * xpad + start, b * xpad + start + count)
        e, o = ye_ref[span], yo_ref[span]
        return jnp.where(even_y, o, e) if side == 0 else jnp.where(even_y, e, o)

    for side in range(2):
        inner = 0 if side == 0 else ny - 1
        outer_at = 7 if side == 0 else 8 + ny
        t1, s1 = packed(side, 0), packed(side, 1)
        face = packed(side, 2) if side == 0 else fy_ref[pl.ds(ny - 1, xpad, stride=ny), :]
        s_in = s_ref[pl.ds(inner, xpad, stride=ny), :]
        t_in = t_ref[pl.ds(inner, xpad, stride=ny), :]
        outer = t1 + face * s_in
        inner_r = t_in + face * s1
        rhalo[side * xpad : (side + 1) * xpad] = outer
        rin[side * xpad : (side + 1) * xpad] = -face * inner_r
        rex[pl.ds(outer_at, xpad, stride=pitch), :] = outer
        rex[pl.ds(8 + inner, xpad, stride=pitch), :] = inner_r
        if side == 0:
            fyx[pl.ds(outer_at, xpad, stride=pitch), :] = face
        labels = packed(side, 7, 0, 8)
        spot = iota((xpad, nz), 0) == iota((xpad, nz), 1)
        for r, dest in ((0, lab1), (1, lab2)):
            column = jnp.sum(jnp.where(spot, labels[r : r + 1], 0.0), axis=1, keepdims=True)
            dest[side * xpad : (side + 1) * xpad] = jnp.broadcast_to(column, (xpad, nz))
        lbx[pl.ds(outer_at, xpad, stride=pitch), :] = lab1[side * xpad : (side + 1) * xpad]
        labin[side * xpad : (side + 1) * xpad] = lb_ref[pl.ds(inner, xpad, stride=ny), :]

    def spread(parts):
        fields = []
        for j in range(ENLARGE):
            total = None
            for values, label in parts:
                term = jnp.where(label == float(j), values, 0.0)
                total = term if total is None else total + term
            fields.append(total)
        return fields

    def centre(dg, fz, r):
        return (dg - SHIFT) * r - fz * pltpu.roll(r, nz - 1, 1) - pltpu.roll(fz * r, 1, 1)

    def first(i, carry):
        for h in range(0, ny, 8):
            base = pl.multiple_of(i * pitch + 8 + h, 8)
            flat = pl.multiple_of(i * ny + h, 8)
            mid = pl.ds(base, 8)
            r = rex[mid]
            parts = [
                (centre(dg_ref[pl.ds(flat, 8)], fz_ref[pl.ds(flat, 8)], r), lbx[mid]),
                (-fx_ref[pl.ds(flat, 8)] * rex[pl.ds(base + pitch, 8)], lbx[pl.ds(base + pitch, 8)]),
                (-fx_ref[pl.ds(flat - ny, 8)] * rex[pl.ds(base - pitch, 8)], lbx[pl.ds(base - pitch, 8)]),
                (-fyx[mid] * rex[pl.ds(base + 1, 8)], lbx[pl.ds(base + 1, 8)]),
                (-fyx[pl.ds(base - 1, 8)] * rex[pl.ds(base - 1, 8)], lbx[pl.ds(base - 1, 8)]),
            ]
            for j, values in enumerate(spread(parts)):
                pex[j, mid] = values
        return carry

    lax.fori_loop(1, ext - 1, first, 0)

    for side in range(2):
        outer_at = 7 if side == 0 else 8 + ny
        for c in range(0, nx, 8):
            lo = g + c
            here = slice(side * xpad + lo, side * xpad + lo + 8)
            up = slice(side * xpad + lo + 1, side * xpad + lo + 9)
            down = slice(side * xpad + lo - 1, side * xpad + lo + 7)
            parts = [
                (centre(packed(side, 5, lo, 8), packed(side, 6, lo, 8), rhalo[here]), lab1[here]),
                (-packed(side, 3, lo, 8) * rhalo[up], lab1[up]),
                (-packed(side, 3, lo - 1, 8) * rhalo[down], lab1[down]),
                (-packed(side, 4, lo, 8), lab2[here]),
                (rin[here], labin[here]),
            ]
            for j, values in enumerate(spread(parts)):
                pex[j, pl.ds(lo * pitch + outer_at, 8, stride=pitch), :] = values

    def second(i, carry):
        for h in range(0, ny, 8):
            base = pl.multiple_of((i + g) * pitch + 8 + h, 8)
            flat = pl.multiple_of((i + g) * ny + h, 8)
            out = pl.ds(pl.multiple_of(i * ny + h, 8), 8)
            mid = pl.ds(base, 8)
            dg, fz = dg_ref[pl.ds(flat, 8)], fz_ref[pl.ds(flat, 8)]
            fxp, fxm = fx_ref[pl.ds(flat, 8)], fx_ref[pl.ds(flat - ny, 8)]
            fyp, fym = fyx[mid], fyx[pl.ds(base - 1, 8)]
            r_out[out] = rex[mid]
            for j in range(ENLARGE):
                p = pex[j, mid]
                q = dg * p
                q = q - fxp * pex[j, pl.ds(base + pitch, 8)] - fxm * pex[j, pl.ds(base - pitch, 8)]
                q = q - fyp * pex[j, pl.ds(base + 1, 8)] - fym * pex[j, pl.ds(base - 1, 8)]
                q = q - fz * pltpu.roll(p, nz - 1, 1) - pltpu.roll(fz * p, 1, 1)
                p_out[j, out] = p
                q_out[j, out] = q
        return carry

    lax.fori_loop(0, nx, second, 0)

    zeros = tuple(jnp.zeros((8, nz), F32) for _ in PAIRS)

    def dots_pp(i, sums):
        at = pl.ds(pl.multiple_of(i * 8, 8), 8)
        p = [p_out[j, at] for j in range(ENLARGE)]
        return tuple(t + p[j] * p[k] for t, (j, k) in zip(sums, PAIRS))

    def dots_pq(i, sums):
        at = pl.ds(pl.multiple_of(i * 8, 8), 8)
        p = [p_out[j, at] for j in range(ENLARGE)]
        q = [q_out[j, at] for j in range(ENLARGE)]
        return tuple(t + p[j] * q[k] for t, (j, k) in zip(sums, PAIRS))

    def dots_bp(i, sums):
        at = pl.ds(pl.multiple_of(i * 8, 8), 8)
        flat = pl.ds(pl.multiple_of(i * 8 + g * ny, 8), 8)
        r = r_out[at]
        label = lb_ref[flat]
        b = [jnp.where(label == float(j), r, 0.0) for j in range(ENLARGE)]
        p = [p_out[j, at] for j in range(ENLARGE)]
        own = tuple(t + v * v for t, v in zip(sums[len(PAIRS) :], b))
        return tuple(t + b[j] * p[k] for t, (j, k) in zip(sums, PAIRS)) + own

    count = nx * ny // 8
    bp = lax.fori_loop(0, count, dots_bp, zeros + zeros[:ENLARGE])
    put = lambda slot, values: accs.__setitem__(
        (slice(slot, slot + 1),), jnp.sum(values, axis=0, keepdims=True)
    )
    accs[...] = jnp.zeros_like(accs)
    span = ENLARGE * ENLARGE
    for which, sums in ((0, bp[: len(PAIRS)]),):
        for (j, k), values in zip(PAIRS, sums):
            put(which * span + j * ENLARGE + k, values)
            if j != k:
                put(which * span + k * ENLARGE + j, values)
    for j in range(ENLARGE):
        put(3 * span + j * ENLARGE + j, bp[len(PAIRS) + j])
    for which, dots in ((1, dots_pp), (2, dots_pq)):
        sums = lax.fori_loop(0, count, dots, zeros)
        for (j, k), values in zip(PAIRS, sums):
            put(which * span + j * ENLARGE + k, values)
            if j != k:
                put(which * span + k * ENLARGE + j, values)
    ones = jnp.ones((8, nz), F32)
    flat = lax.dot_general(ones, accs[...], (((1,), (1,)), ((), ())), precision=HIGHEST, preferred_element_type=F32)
    half = 2 * span
    pair = jnp.where(iota((2, half), 0) == 0, flat[0:2, 0:half], flat[0:2, half : 2 * half])
    for d in range(devices):
        gram_out[d] = pair


def powers(ext_fields, ye, yo, nx, ny, xpad, devices):
    nz = ye.shape[-1]
    pitch = ny + 16
    half = 2 * ENLARGE * ENLARGE
    field = jax.ShapeDtypeStruct((nx * ny, nz), F32)
    fields = jax.ShapeDtypeStruct((ENLARGE, nx * ny, nz), F32)
    padded = pltpu.VMEM((xpad * pitch, nz), F32)
    edge = pltpu.VMEM((2 * xpad, nz), F32)
    return pl.pallas_call(
        functools.partial(powers_kernel, nx, ny, xpad, devices),
        in_specs=whole(9),
        out_specs=whole(4),
        out_shape=[fields, fields, field, jax.ShapeDtypeStruct((devices, 2, half), F32)],
        scratch_shapes=[
            padded, padded, padded, pltpu.VMEM((ENLARGE, xpad * pitch, nz), F32),
            edge, edge, edge, edge, edge,
            pltpu.VMEM((2 * half, nz), F32),
        ],
        compiler_params=params(),
        name="powers",
    )(*ext_fields, ye, yo)


def solve_columns(parts):
    nz = parts.shape[-1]
    span = ENLARGE * ENLARGE
    v = jnp.sum(parts, axis=0)
    lhs = jnp.concatenate([jnp.broadcast_to(v[0:1], (8, nz)), jnp.broadcast_to(v[1:2], (8, nz))], axis=1)
    source = iota((8, 2 * nz), 1)
    lhs = jnp.where(iota((8, 2 * nz), 0) == lax.rem(source, span) // ENLARGE, lhs, 0.0)
    k = iota((2 * nz, nz), 0)
    n = iota((2 * nz, nz), 1)
    which = k // span
    column = lax.rem(k, ENLARGE)

    def place(block, offset, scale):
        return jnp.where(jnp.logical_and(which == block, n == column + offset), scale, 0.0)

    upper = place(0, 0, 1.0) + place(3, 0, SHIFT) + place(1, 8, 1.0) + place(0, 8, SHIFT) + place(3, 16, 1.0)
    lower = place(1, 0, 1.0) + place(0, 0, SHIFT) + place(2, 8, 1.0) + place(0, 16, 1.0)
    dot = functools.partial(jnp.dot, precision=HIGHEST, preferred_element_type=F32)
    m = jnp.concatenate([dot(lhs, upper), dot(lhs, lower)], axis=0)
    row = iota(m.shape, 0)
    for i in range(2 * ENLARGE):
        pivot = m[i : i + 1] / m[i : i + 1, i : i + 1]
        m = jnp.where(row == i, pivot, m - m[:, i : i + 1] * pivot)
    return m


def update_kernel(ny, parts_ref, p_ref, q_ref, r_ref, lb_ref, it_ref, it_out, r_out, table, weights):
    nz = r_ref.shape[-1]
    two = 2 * ENLARGE

    @pl.when(pl.program_id(0) == 0)
    def _():
        m = solve_columns(parts_ref[...])
        lane = iota(m.shape, 1)
        inside = jnp.logical_and(lane >= two, lane < two + ENLARGE)
        carried = jnp.sum(jnp.where(inside, m, 0.0), axis=1, keepdims=True)
        for j in range(ENLARGE):
            for k in range(ENLARGE):
                value = m[ENLARGE + k : ENLARGE + k + 1, two + j : two + j + 1]
                table[j * ENLARGE + k] = jnp.broadcast_to(value, (8, nz))
        for k in range(two):
            table[ENLARGE * ENLARGE + k] = jnp.broadcast_to(carried[k : k + 1], (8, nz))
        own = pltpu.roll(m[0:ENLARGE], nz - two, 1)
        lane = iota(own.shape, 1)
        own = jnp.where(lane < ENLARGE, own, jnp.where(lane == ENLARGE, carried[0:ENLARGE], 0.0))
        high = own.astype(jnp.bfloat16).astype(F32)
        mid = (own - high).astype(jnp.bfloat16).astype(F32)
        rest = own - high - mid
        weights[...] = jnp.zeros_like(weights)
        weights[0:8] = high
        weights[8:16] = mid
        weights[16:24] = rest

    count = r_ref.shape[0]
    lane = iota((count, nz), 1)
    chosen = jnp.logical_and(lane < 3 * ENLARGE, lax.rem(lane, ENLARGE).astype(F32) == lb_ref[...])
    onehot = jnp.where(chosen, 1.0, 0.0).astype(jnp.bfloat16)
    own = jnp.dot(onehot, weights[...].astype(jnp.bfloat16), preferred_element_type=F32)
    for at in range(0, count, 8):
        here = slice(at, at + 8)
        r = r_ref[here]
        mine = own[here]
        p = [p_ref[k, here] for k in range(ENLARGE)]
        for j in range(ENLARGE):
            total = it_ref[j, here] + mine[:, j : j + 1] * r
            for k in range(ENLARGE):
                total = total + table[j * ENLARGE + k] * p[k]
            it_out[j, here] = total
        base = ENLARGE * ENLARGE
        total = r - (SHIFT * mine[:, ENLARGE : ENLARGE + 1]) * r
        for k in range(ENLARGE):
            total = total - table[base + k] * p[k] - table[base + ENLARGE + k] * q_ref[k, here]
        r_out[here] = total


def update(parts, p, q, r, labels_ext, iterates, ny):
    _, rows, nz = p.shape
    block = 4 * ny
    assert rows % block == 0
    many = pl.BlockSpec((ENLARGE, block, nz), lambda i: (0, i, 0))
    one = pl.BlockSpec((block, nz), lambda i: (i, 0))
    return pl.pallas_call(
        functools.partial(update_kernel, ny),
        grid=(rows // block,),
        in_specs=[pl.BlockSpec(parts.shape, lambda i: (0, 0, 0)), many, many, one, one, many],
        out_specs=[many, one],
        out_shape=[jax.ShapeDtypeStruct((ENLARGE, rows, nz), F32), jax.ShapeDtypeStruct((rows, nz), F32)],
        scratch_shapes=[
            pltpu.VMEM((ENLARGE * ENLARGE + 2 * ENLARGE, 8, nz), F32),
            pltpu.VMEM((nz, nz), F32),
        ],
        compiler_params=params(),
        name="update",
    )(parts, p, q, r, labels_ext, iterates)


def shards(gx, gy, source, diagonal, face_x, face_y, face_z, iterates, labels):
    _, nx, ny, nz = iterates.shape
    xpad = -(-(nx + 2 * GHOST) // 8) * 8
    spread = jnp.broadcast_to(labels.astype(F32)[:, :, None], (nx, ny, nz))
    fields = (source, diagonal, face_x, face_y, face_z, spread)
    total, xe, xo = sum_and_edges(iterates, fields)
    xe = lax.ppermute(xe, "gx", even_pairs(gx))
    xo = lax.ppermute(xo, "gx", odd_pairs(gx))
    *ext, ye, yo = partial_and_edges(total, fields, xe, xo, xpad, gx, gy)
    ye = lax.ppermute(ye, "gy", even_pairs(gy))
    yo = lax.ppermute(yo, "gy", odd_pairs(gy))
    p, q, r, gram = powers(ext, ye, yo, nx, ny, xpad, gx * gy)
    parts = lax.all_to_all(gram, ("gx", "gy"), 0, 0, tiled=True)
    flat = iterates.reshape(ENLARGE, nx * ny, nz)
    new_iterates, new_residual = update(parts, p, q, r, spread.reshape(nx * ny, nz), flat, ny)
    return new_iterates.reshape(iterates.shape), new_residual.reshape(source.shape)


def solution(mesh):
    placed = (
        P("gx", "gy", None),
        P("gx", "gy", None),
        P("gx", "gy", None),
        P("gx", "gy", None),
        P("gx", "gy", None),
        P(None, "gx", "gy", None),
        P("gx", "gy"),
    )
    return jax.shard_map(
        functools.partial(shards, mesh.shape["gx"], mesh.shape["gy"]),
        mesh=mesh,
        in_specs=placed,
        out_specs=(P(None, "gx", "gy", None), P("gx", "gy", None)),
        check_vma=False,
    )
```

```python
import functools

import jax
import jax.numpy as jnp
from jax import lax
from jax.experimental import pallas as pl
from jax.experimental.pallas import tpu as pltpu
from jax.sharding import PartitionSpec as P

ENLARGE = 8
SHIFT = 6.5
F32 = jnp.float32
HIGHEST = lax.Precision.HIGHEST
PAIRS = [(j, k) for j in range(ENLARGE) for k in range(j, ENLARGE)]
GHOST = 2
XROWS = 16
VMEM_LIMIT = 40 * 1024 * 1024


def iota(shape, dim):
    return lax.broadcasted_iota(jnp.int32, shape, dim)


def even_pairs(count):
    return [(i, i ^ 1) for i in range(count) if (i ^ 1) < count]


def odd_pairs(count):
    return [(i, ((i - 1) ^ 1) + 1) for i in range(1, count) if ((i - 1) ^ 1) + 1 < count]


def whole(count):
    return [pl.BlockSpec(memory_space=pltpu.VMEM)] * count


def params():
    return pltpu.CompilerParams(vmem_limit_bytes=VMEM_LIMIT)


def sum_kernel(steps, it_ref, *refs):
    lows, highs = refs[0:6], refs[6:12]
    s_ref, even_ref, odd_ref = refs[12:]
    step = pl.program_id(0)
    total = it_ref[0]
    for j in range(1, ENLARGE):
        total = total + it_ref[j]
    s_ref[...] = total
    width = total.shape[0]

    def pack(ref, at, values):
        ref[at : at + values.shape[0]] = values

    def put(dest, low):
        src, dg, fx, fy, fz, lb = lows if low else highs
        if low:
            take = lambda a, n: a[0:n]
        else:
            take = lambda a, n: a[width - n : width]
        pack(dest, 0, take(total, 3))
        pack(dest, 3, take(fx, 3))
        at = 6
        for field in (src, dg, fy, fz, lb):
            pack(dest, at, take(field, 2))
            at += 2

    parity = lax.rem(lax.axis_index("gx"), 2)

    @pl.when(jnp.logical_and(step == 0, parity == 0))
    def _():
        put(odd_ref, True)

    @pl.when(jnp.logical_and(step == 0, parity == 1))
    def _():
        put(even_ref, True)

    @pl.when(jnp.logical_and(step == steps - 1, parity == 0))
    def _():
        put(even_ref, False)

    @pl.when(jnp.logical_and(step == steps - 1, parity == 1))
    def _():
        put(odd_ref, False)


def sum_and_edges(iterates, fields):
    _, nx, ny, nz = iterates.shape
    width = 8
    steps = nx // width
    block = (width, ny, nz)
    low = pl.BlockSpec(block, lambda i: (0, 0, 0))
    high = pl.BlockSpec(block, lambda i: (steps - 1, 0, 0))
    edge = jax.ShapeDtypeStruct((XROWS, ny, nz), F32)
    edge_spec = pl.BlockSpec((XROWS, ny, nz), lambda i: (0, 0, 0))
    return pl.pallas_call(
        functools.partial(sum_kernel, steps),
        grid=(steps,),
        in_specs=[pl.BlockSpec((ENLARGE,) + block, lambda i: (0, i, 0, 0))] + [low] * 6 + [high] * 6,
        out_specs=[pl.BlockSpec(block, lambda i: (i, 0, 0)), edge_spec, edge_spec],
        out_shape=[jax.ShapeDtypeStruct((nx, ny, nz), F32), edge, edge],
        compiler_params=params(),
        name="sum_and_edges",
    )(iterates, *fields, *fields)


def partial_kernel(
    nx, ny, xpad, gx, gy,
    s_in, src_in, dg_in, fx_in, fy_in, fz_in, lb_in, xe_ref, xo_ref,
    t_out, s_out, fx_out, fy_out, dg_out, fz_out, lb_out, ye_ref, yo_ref,
    src_ext,
):
    g = GHOST
    nz = s_in.shape[-1]
    lane = iota((ny, nz), 1)
    row = iota((ny, nz), 0)
    even_x = lax.rem(lax.axis_index("gx"), 2) == 0
    last_x = lax.axis_index("gx") == gx - 1
    last_y = lax.axis_index("gy") == gy - 1

    def rows(i):
        return pl.ds(pl.multiple_of(i * ny, ny), ny)

    def low(r):
        return jnp.where(even_x, xo_ref[r], xe_ref[r])

    def high(r):
        return jnp.where(even_x, xe_ref[r], xo_ref[r])

    top = jnp.logical_and(last_y, row == ny - 1)

    def fy_of(values):
        return jnp.where(top, 0.0, values)

    def fz_of(values):
        return jnp.where(lane == nz - 1, 0.0, values)

    s_low = [low(r) for r in range(3)]
    s_high = [high(r) for r in range(3)]
    fx_low = [low(3 + r) for r in range(3)]
    fx_high = [high(3 + r) for r in range(3)]
    for e in range(2):
        for side, at, pick in ((0, e, low), (1, g + nx + e, high)):
            s_out[rows(at)] = s_low[1 + e] if side == 0 else s_high[e]
            fx_out[rows(at)] = fx_low[1 + e] if side == 0 else fx_high[e]
            src_ext[rows(at)] = pick(6 + e)
            dg_out[rows(at)] = pick(8 + e)
            fy_out[rows(at)] = fy_of(pick(10 + e))
            fz_out[rows(at)] = fz_of(pick(12 + e))
            lb_out[rows(at)] = pick(14 + e)
    zero = jnp.zeros((ny, nz), F32)
    for at in range(nx + 2 * g, xpad):
        for ref in (t_out, s_out, fx_out, fy_out, dg_out, fz_out, lb_out):
            ref[rows(at)] = zero

    def copy(i, carry):
        at = rows(i + g)
        s_out[at] = s_in[i]
        fx_out[at] = fx_in[i]
        dg_out[at] = dg_in[i]
        fy_out[at] = fy_of(fy_in[i])
        fz_out[at] = fz_of(fz_in[i])
        lb_out[at] = lb_in[i]
        src_ext[at] = src_in[i]
        return carry

    lax.fori_loop(0, nx, copy, 0, unroll=4)

    @pl.when(last_x)
    def _():
        fx_out[rows(g + nx - 1)] = zero

    def partial(at, s, sp, sm, fxp, fxm):
        fy = fy_out[at]
        fz = fz_out[at]
        fys = fy * s
        ys = jnp.where(row == ny - 1, 0.0, fy * pltpu.roll(s, ny - 1, 0))
        ys = ys + jnp.where(row == 0, 0.0, pltpu.roll(fys, 1, 0))
        zs = fz * pltpu.roll(s, nz - 1, 1) + pltpu.roll(fz * s, 1, 1)
        return src_ext[at] - (dg_out[at] * s - fxp * sp - fxm * sm - ys - zs)

    def body(i, carry):
        at = rows(i)
        t_out[at] = partial(
            at, s_out[at], s_out[rows(i + 1)], s_out[rows(i - 1)], fx_out[at], fx_out[rows(i - 1)]
        )
        return carry

    at = rows(0)
    t_out[at] = partial(at, s_out[at], s_out[rows(1)], s_low[0], fx_out[at], fx_low[0])
    end = nx + 2 * g - 1
    at = rows(end)
    t_out[at] = partial(at, s_out[at], s_high[2], s_out[rows(end - 1)], fx_out[at], fx_out[rows(end - 1)])
    lax.fori_loop(1, end, body, 0, unroll=2)

    even_y = lax.rem(lax.axis_index("gy"), 2) == 0

    def pack(dest, is_high):
        first = jnp.where(is_high, ny - 1, 0)
        second = jnp.where(is_high, ny - 2, 1)
        between = jnp.where(is_high, ny - 2, 0)

        def line(ref, y):
            return ref[pl.ds(y, xpad, stride=ny), :]

        blocks = (
            line(t_out, first),
            line(s_out, first),
            line(fy_out, first),
            line(fx_out, first),
            line(fy_out, between) * line(t_out, second),
            line(dg_out, first),
            line(fz_out, first),
        )
        for b, values in enumerate(blocks):
            dest[b * xpad : (b + 1) * xpad] = values
        spot = iota((xpad, nz), 0) == iota((xpad, nz), 1)
        one = jnp.sum(jnp.where(spot, line(lb_out, first), 0.0), axis=0, keepdims=True)
        two = jnp.sum(jnp.where(spot, line(lb_out, second), 0.0), axis=0, keepdims=True)
        which = iota((8, nz), 0)
        dest[7 * xpad : 7 * xpad + 8] = jnp.where(which == 0, one, jnp.where(which == 1, two, 0.0))

    pack(ye_ref, even_y)
    pack(yo_ref, jnp.logical_not(even_y))


def partial_and_edges(total, fields, xe, xo, xpad, gx, gy):
    nx, ny, nz = total.shape
    ext = jax.ShapeDtypeStruct((xpad * ny, nz), F32)
    pack = jax.ShapeDtypeStruct((7 * xpad + 8, nz), F32)
    return pl.pallas_call(
        functools.partial(partial_kernel, nx, ny, xpad, gx, gy),
        in_specs=whole(9),
        out_specs=whole(9),
        out_shape=[ext] * 7 + [pack] * 2,
        scratch_shapes=[pltpu.VMEM((xpad * ny, nz), F32)],
        compiler_params=params(),
        name="partial_and_edges",
    )(total, *fields, xe, xo)


def powers_kernel(
    nx, ny, xpad, devices,
    t_ref, s_ref, fx_ref, fy_ref, dg_ref, fz_ref, lb_ref, ye_ref, yo_ref,
    p_out, q_out, r_out, gram_out,
    rex, fyx, lbx, pex, rhalo, rin, lab1, lab2, labin, accs, packs,
):
    g = GHOST
    nz = t_ref.shape[-1]
    ext = nx + 2 * g
    pitch = ny + 16
    def at16(i):
        return pl.ds(pl.multiple_of(i * ny, ny), ny)

    def copy(i, carry):
        base = pl.multiple_of(i * pitch + 8, 8)
        rex[pl.ds(base, ny)] = t_ref[at16(i)]
        fyx[pl.ds(base, ny)] = fy_ref[at16(i)]
        lbx[pl.ds(base, ny)] = lb_ref[at16(i)]
        return carry

    lax.fori_loop(0, xpad, copy, 0, unroll=4)

    def packed(side, b, start=0, count=None):
        count = xpad if count is None else count
        return packs[side, b * xpad + start : b * xpad + start + count]

    odd = lax.rem(lax.axis_index("gy"), 2)
    packs[1 - odd] = ye_ref[...]
    packs[odd] = yo_ref[...]

    for side in range(2):
        inner = 0 if side == 0 else ny - 1
        outer_at = 7 if side == 0 else 8 + ny
        t1, s1 = packed(side, 0), packed(side, 1)
        face = packed(side, 2) if side == 0 else fy_ref[pl.ds(ny - 1, xpad, stride=ny), :]
        s_in = s_ref[pl.ds(inner, xpad, stride=ny), :]
        t_in = t_ref[pl.ds(inner, xpad, stride=ny), :]
        outer = t1 + face * s_in
        inner_r = t_in + face * s1
        rhalo[side * xpad : (side + 1) * xpad] = outer
        rin[side * xpad : (side + 1) * xpad] = -face * inner_r
        rex[pl.ds(outer_at, xpad, stride=pitch), :] = outer
        rex[pl.ds(8 + inner, xpad, stride=pitch), :] = inner_r
        if side == 0:
            fyx[pl.ds(outer_at, xpad, stride=pitch), :] = face
        labels = packed(side, 7, 0, 8)
        spot = iota((xpad, nz), 0) == iota((xpad, nz), 1)
        for r, dest in ((0, lab1), (1, lab2)):
            column = jnp.sum(jnp.where(spot, labels[r : r + 1], 0.0), axis=1, keepdims=True)
            dest[side * xpad : (side + 1) * xpad] = jnp.broadcast_to(column, (xpad, nz))
        lbx[pl.ds(outer_at, xpad, stride=pitch), :] = lab1[side * xpad : (side + 1) * xpad]
        labin[side * xpad : (side + 1) * xpad] = lb_ref[pl.ds(inner, xpad, stride=ny), :]

    def spread(parts):
        fields = []
        for j in range(ENLARGE):
            total = None
            for values, label in parts:
                term = jnp.where(label == float(j), values, 0.0)
                total = term if total is None else total + term
            fields.append(total)
        return fields

    def centre(dg, fz, r):
        return (dg - SHIFT) * r - fz * pltpu.roll(r, nz - 1, 1) - pltpu.roll(fz * r, 1, 1)

    def first(i, carry):
        for h in range(0, ny, 8):
            base = pl.multiple_of(i * pitch + 8 + h, 8)
            flat = pl.multiple_of(i * ny + h, 8)
            mid = pl.ds(base, 8)
            r = rex[mid]
            parts = [
                (centre(dg_ref[pl.ds(flat, 8)], fz_ref[pl.ds(flat, 8)], r), lbx[mid]),
                (-fx_ref[pl.ds(flat, 8)] * rex[pl.ds(base + pitch, 8)], lbx[pl.ds(base + pitch, 8)]),
                (-fx_ref[pl.ds(flat - ny, 8)] * rex[pl.ds(base - pitch, 8)], lbx[pl.ds(base - pitch, 8)]),
                (-fyx[mid] * rex[pl.ds(base + 1, 8)], lbx[pl.ds(base + 1, 8)]),
                (-fyx[pl.ds(base - 1, 8)] * rex[pl.ds(base - 1, 8)], lbx[pl.ds(base - 1, 8)]),
            ]
            for j, values in enumerate(spread(parts)):
                pex[j, mid] = values
        return carry

    lax.fori_loop(1, ext - 1, first, 0)

    for side in range(2):
        outer_at = 7 if side == 0 else 8 + ny
        for c in range(0, nx, 8):
            lo = g + c
            here = slice(side * xpad + lo, side * xpad + lo + 8)
            up = slice(side * xpad + lo + 1, side * xpad + lo + 9)
            down = slice(side * xpad + lo - 1, side * xpad + lo + 7)
            parts = [
                (centre(packed(side, 5, lo, 8), packed(side, 6, lo, 8), rhalo[here]), lab1[here]),
                (-packed(side, 3, lo, 8) * rhalo[up], lab1[up]),
                (-packed(side, 3, lo - 1, 8) * rhalo[down], lab1[down]),
                (-packed(side, 4, lo, 8), lab2[here]),
                (rin[here], labin[here]),
            ]
            for j, values in enumerate(spread(parts)):
                pex[j, pl.ds(lo * pitch + outer_at, 8, stride=pitch), :] = values

    def second(i, carry):
        for h in range(0, ny, 8):
            base = pl.multiple_of((i + g) * pitch + 8 + h, 8)
            flat = pl.multiple_of((i + g) * ny + h, 8)
            out = pl.ds(pl.multiple_of(i * ny + h, 8), 8)
            mid = pl.ds(base, 8)
            dg, fz = dg_ref[pl.ds(flat, 8)], fz_ref[pl.ds(flat, 8)]
            fxp, fxm = fx_ref[pl.ds(flat, 8)], fx_ref[pl.ds(flat - ny, 8)]
            fyp, fym = fyx[mid], fyx[pl.ds(base - 1, 8)]
            r_out[out] = rex[mid]
            for j in range(ENLARGE):
                p = pex[j, mid]
                q = dg * p
                q = q - fxp * pex[j, pl.ds(base + pitch, 8)] - fxm * pex[j, pl.ds(base - pitch, 8)]
                q = q - fyp * pex[j, pl.ds(base + 1, 8)] - fym * pex[j, pl.ds(base - 1, 8)]
                q = q - fz * pltpu.roll(p, nz - 1, 1) - pltpu.roll(fz * p, 1, 1)
                p_out[j, out] = p
                q_out[j, out] = q
        return carry

    lax.fori_loop(0, nx, second, 0, unroll=2)

    zeros = tuple(jnp.zeros((8, nz), F32) for _ in PAIRS)

    def dots_pp(i, sums):
        at = pl.ds(pl.multiple_of(i * 8, 8), 8)
        p = [p_out[j, at] for j in range(ENLARGE)]
        return tuple(t + p[j] * p[k] for t, (j, k) in zip(sums, PAIRS))

    def dots_pq(i, sums):
        at = pl.ds(pl.multiple_of(i * 8, 8), 8)
        p = [p_out[j, at] for j in range(ENLARGE)]
        q = [q_out[j, at] for j in range(ENLARGE)]
        return tuple(t + p[j] * q[k] for t, (j, k) in zip(sums, PAIRS))

    def dots_bp(i, sums):
        at = pl.ds(pl.multiple_of(i * 8, 8), 8)
        flat = pl.ds(pl.multiple_of(i * 8 + g * ny, 8), 8)
        r = r_out[at]
        label = lb_ref[flat]
        b = [jnp.where(label == float(j), r, 0.0) for j in range(ENLARGE)]
        p = [p_out[j, at] for j in range(ENLARGE)]
        own = tuple(t + v * v for t, v in zip(sums[len(PAIRS) :], b))
        return tuple(t + b[j] * p[k] for t, (j, k) in zip(sums, PAIRS)) + own

    count = nx * ny // 8
    bp = lax.fori_loop(0, count, dots_bp, zeros + zeros[:ENLARGE], unroll=4)
    put = lambda slot, values: accs.__setitem__(
        (slice(slot, slot + 1),), jnp.sum(values, axis=0, keepdims=True)
    )
    accs[...] = jnp.zeros_like(accs)
    span = ENLARGE * ENLARGE
    for which, sums in ((0, bp[: len(PAIRS)]),):
        for (j, k), values in zip(PAIRS, sums):
            put(which * span + j * ENLARGE + k, values)
            if j != k:
                put(which * span + k * ENLARGE + j, values)
    for j in range(ENLARGE):
        put(3 * span + j * ENLARGE + j, bp[len(PAIRS) + j])
    for which, dots in ((1, dots_pp), (2, dots_pq)):
        sums = lax.fori_loop(0, count, dots, zeros, unroll=4)
        for (j, k), values in zip(PAIRS, sums):
            put(which * span + j * ENLARGE + k, values)
            if j != k:
                put(which * span + k * ENLARGE + j, values)
    ones = jnp.ones((8, nz), F32)
    flat = lax.dot_general(ones, accs[...], (((1,), (1,)), ((), ())), precision=HIGHEST, preferred_element_type=F32)
    half = 2 * span
    pair = jnp.where(iota((2, half), 0) == 0, flat[0:2, 0:half], flat[0:2, half : 2 * half])
    for d in range(devices):
        gram_out[d] = pair


def powers(ext_fields, ye, yo, nx, ny, xpad, devices):
    nz = ye.shape[-1]
    pitch = ny + 16
    half = 2 * ENLARGE * ENLARGE
    field = jax.ShapeDtypeStruct((nx * ny, nz), F32)
    fields = jax.ShapeDtypeStruct((ENLARGE, nx * ny, nz), F32)
    padded = pltpu.VMEM((xpad * pitch, nz), F32)
    edge = pltpu.VMEM((2 * xpad, nz), F32)
    return pl.pallas_call(
        functools.partial(powers_kernel, nx, ny, xpad, devices),
        in_specs=whole(9),
        out_specs=whole(4),
        out_shape=[fields, fields, field, jax.ShapeDtypeStruct((devices, 2, half), F32)],
        scratch_shapes=[
            padded, padded, padded, pltpu.VMEM((ENLARGE, xpad * pitch, nz), F32),
            edge, edge, edge, edge, edge,
            pltpu.VMEM((2 * half, nz), F32),
            pltpu.VMEM((2,) + ye.shape, F32),
        ],
        compiler_params=params(),
        name="powers",
    )(*ext_fields, ye, yo)


def solve_columns(parts):
    nz = parts.shape[-1]
    span = ENLARGE * ENLARGE
    v = jnp.sum(parts, axis=0)
    lhs = jnp.concatenate([jnp.broadcast_to(v[0:1], (8, nz)), jnp.broadcast_to(v[1:2], (8, nz))], axis=1)
    source = iota((8, 2 * nz), 1)
    lhs = jnp.where(iota((8, 2 * nz), 0) == lax.rem(source, span) // ENLARGE, lhs, 0.0)
    k = iota((2 * nz, nz), 0)
    n = iota((2 * nz, nz), 1)
    which = k // span
    column = lax.rem(k, ENLARGE)

    def place(block, offset, scale):
        return jnp.where(jnp.logical_and(which == block, n == column + offset), scale, 0.0)

    upper = place(0, 0, 1.0) + place(3, 0, SHIFT) + place(1, 8, 1.0) + place(0, 8, SHIFT) + place(3, 16, 1.0)
    lower = place(1, 0, 1.0) + place(0, 0, SHIFT) + place(2, 8, 1.0) + place(0, 16, 1.0)
    dot = functools.partial(jnp.dot, precision=HIGHEST, preferred_element_type=F32)
    m = jnp.concatenate([dot(lhs, upper), dot(lhs, lower)], axis=0)
    row = iota(m.shape, 0)
    for i in range(2 * ENLARGE):
        pivot = m[i : i + 1] / m[i : i + 1, i : i + 1]
        m = jnp.where(row == i, pivot, m - m[:, i : i + 1] * pivot)
    return m


def update_kernel(
    offset, group, parts_ref, p_ref, q_ref, r_ref, lb_ref, it_hbm, it_out, r_out,
    table, weights, onehot, own, work, r_work, sem_in, sem_out, sem_r,
):
    rows, nz = r_ref.shape
    two = 2 * ENLARGE
    square = ENLARGE * ENLARGE
    groups = rows // group

    def span(c):
        return pl.ds(pl.multiple_of(c * group, group), group)

    def copy_in(c):
        return pltpu.make_async_copy(it_hbm.at[:, span(c)], work.at[:, span(c)], sem_in.at[c])

    def copy_out(c):
        return pltpu.make_async_copy(work.at[:, span(c)], it_out.at[:, span(c)], sem_out.at[c])

    def copy_r(c):
        return pltpu.make_async_copy(r_work.at[span(c)], r_out.at[span(c)], sem_r.at[c])

    def each(f):
        def body(c, carry):
            f(c)
            return carry

        lax.fori_loop(0, groups, body, 0)

    each(lambda c: copy_in(c).start())

    def mark(c):
        lane = iota((group, nz), 1)
        labels = lb_ref[pl.ds(pl.multiple_of(offset + c * group, 8), group)]
        chosen = jnp.logical_and(lane < 3 * ENLARGE, lax.rem(lane, ENLARGE).astype(F32) == labels)
        onehot[span(c)] = jnp.where(chosen, 1.0, 0.0).astype(jnp.bfloat16)

    each(mark)

    m = solve_columns(parts_ref[...])
    lane = iota(m.shape, 1)
    inside = jnp.logical_and(lane >= two, lane < two + ENLARGE)
    carried = jnp.sum(jnp.where(inside, m, 0.0), axis=1, keepdims=True)
    for j in range(ENLARGE):
        for k in range(ENLARGE):
            value = m[ENLARGE + k : ENLARGE + k + 1, two + j : two + j + 1]
            table[j * ENLARGE + k] = jnp.broadcast_to(value, (8, nz))
    for k in range(two):
        table[square + k] = jnp.broadcast_to(carried[k : k + 1], (8, nz))
    lane = iota((ENLARGE, nz), 1)
    mine = pltpu.roll(m[0:ENLARGE], nz - two, 1)
    mine = jnp.where(lane < ENLARGE, mine, jnp.where(lane == ENLARGE, carried[0:ENLARGE], 0.0))
    high = mine.astype(jnp.bfloat16).astype(F32)
    mid = (mine - high).astype(jnp.bfloat16).astype(F32)
    weights[...] = jnp.zeros_like(weights)
    weights[0:8] = high
    weights[8:16] = mid
    weights[16:24] = mine - high - mid
    own[...] = jnp.dot(onehot[...], weights[...].astype(jnp.bfloat16), preferred_element_type=F32)

    def body(c, carry):
        copy_in(c).wait()
        spots = [pl.ds(pl.multiple_of(c * group + h, 8), 8) for h in range(0, group, 8)]
        r = [r_ref[at] for at in spots]
        p = [[p_ref[k, at] for k in range(ENLARGE)] for at in spots]
        mine = [own[at] for at in spots]
        for j in range(ENLARGE):
            scale = [table[j * ENLARGE + k] for k in range(ENLARGE)]
            for h, at in enumerate(spots):
                total = work[j, at] + mine[h][:, j : j + 1] * r[h]
                for k in range(ENLARGE):
                    total = total + scale[k] * p[h][k]
                work[j, at] = total
        copy_out(c).start()
        scale = [table[square + k] for k in range(two)]
        for h, at in enumerate(spots):
            total = r[h] - (SHIFT * mine[h][:, ENLARGE : ENLARGE + 1]) * r[h]
            for k in range(ENLARGE):
                total = total - scale[k] * p[h][k] - scale[ENLARGE + k] * q_ref[k, at]
            r_work[at] = total
        copy_r(c).start()
        return carry

    lax.fori_loop(0, groups, body, 0)
    each(lambda c: copy_out(c).wait())
    each(lambda c: copy_r(c).wait())


def update(parts, p, q, r, labels_ext, iterates, ny):
    _, rows, nz = p.shape
    group = 2 * ny
    assert rows % group == 0
    groups = rows // group
    hbm = pl.BlockSpec(memory_space=pltpu.HBM)
    return pl.pallas_call(
        functools.partial(update_kernel, GHOST * ny, group),
        in_specs=whole(5) + [hbm],
        out_specs=[hbm, hbm],
        out_shape=[jax.ShapeDtypeStruct((ENLARGE, rows, nz), F32), jax.ShapeDtypeStruct((rows, nz), F32)],
        scratch_shapes=[
            pltpu.VMEM((ENLARGE * ENLARGE + 2 * ENLARGE, 8, nz), F32),
            pltpu.VMEM((nz, nz), F32),
            pltpu.VMEM((rows, nz), jnp.bfloat16),
            pltpu.VMEM((rows, nz), F32),
            pltpu.VMEM((ENLARGE, rows, nz), F32),
            pltpu.VMEM((rows, nz), F32),
            pltpu.SemaphoreType.DMA((groups,)),
            pltpu.SemaphoreType.DMA((groups,)),
            pltpu.SemaphoreType.DMA((groups,)),
        ],
        compiler_params=params(),
        name="update",
    )(parts, p, q, r, labels_ext, iterates)


def shards(gx, gy, source, diagonal, face_x, face_y, face_z, iterates, labels):
    _, nx, ny, nz = iterates.shape
    xpad = -(-(nx + 2 * GHOST) // 8) * 8
    spread = jnp.broadcast_to(labels.astype(F32)[:, :, None], (nx, ny, nz))
    fields = (source, diagonal, face_x, face_y, face_z, spread)
    total, xe, xo = sum_and_edges(iterates, fields)
    xe = lax.ppermute(xe, "gx", even_pairs(gx))
    xo = lax.ppermute(xo, "gx", odd_pairs(gx))
    *ext, ye, yo = partial_and_edges(total, fields, xe, xo, xpad, gx, gy)
    ye = lax.ppermute(ye, "gy", even_pairs(gy))
    yo = lax.ppermute(yo, "gy", odd_pairs(gy))
    p, q, r, gram = powers(ext, ye, yo, nx, ny, xpad, gx * gy)
    parts = lax.all_to_all(gram, ("gx", "gy"), 0, 0, tiled=True)
    flat = iterates.reshape(ENLARGE, nx * ny, nz)
    new_iterates, new_residual = update(parts, p, q, r, ext[-1], flat, ny)
    return new_iterates.reshape(iterates.shape), new_residual.reshape(source.shape)


def solution(mesh):
    placed = (
        P("gx", "gy", None),
        P("gx", "gy", None),
        P("gx", "gy", None),
        P("gx", "gy", None),
        P("gx", "gy", None),
        P(None, "gx", "gy", None),
        P("gx", "gy"),
    )
    return jax.shard_map(
        functools.partial(shards, mesh.shape["gx"], mesh.shape["gy"]),
        mesh=mesh,
        in_specs=placed,
        out_specs=(P(None, "gx", "gy", None), P("gx", "gy", None)),
        check_vma=False,
    )
```

```python
import functools

import jax
import jax.numpy as jnp
from jax import lax
from jax.experimental import pallas as pl
from jax.experimental.pallas import tpu as pltpu
from jax.sharding import PartitionSpec as P

ENLARGE = 8
SHIFT = 6.5
F32 = jnp.float32
HIGHEST = lax.Precision.HIGHEST
PAIRS = [(j, k) for j in range(ENLARGE) for k in range(j, ENLARGE)]
VMEM_LIMIT = 40 * 1024 * 1024
PAD = 8
SENT = 2


def iota(shape, dim):
    return lax.broadcasted_iota(jnp.int32, shape, dim)


def even_pairs(count):
    return [(i, i ^ 1) for i in range(count) if (i ^ 1) < count]


def odd_pairs(count):
    return [(i, ((i - 1) ^ 1) + 1) for i in range(1, count) if ((i - 1) ^ 1) + 1 < count]


def vmem(count):
    return [pl.BlockSpec(memory_space=pltpu.VMEM)] * count


def hbm(count):
    return [pl.BlockSpec(memory_space=pltpu.HBM)] * count


def pinned(value):
    return pltpu.with_memory_space_constraint(value, pltpu.HBM)


def array(*shape):
    return jax.ShapeDtypeStruct(shape, F32)


def params():
    return pltpu.CompilerParams(vmem_limit_bytes=VMEM_LIMIT)


def aligned(value):
    return value if isinstance(value, int) else pl.multiple_of(value, 8)


def eight(start):
    return pl.ds(aligned(start), 8)


def near(start):
    return pl.ds(start, 8)


def loop(count, body, **kw):
    def wrapped(i, carry):
        body(i)
        return carry

    lax.fori_loop(0, count, wrapped, 0, **kw)


def load_kernel(
    it_hbm, src_hbm, dg_hbm, fx_hbm, fy_hbm, fz_hbm, label_ref,
    s_out, src_out, dg_out, fx_out, fy_out, fz_out, lb_out, even_out, odd_out,
    work, sem_it, sem_field,
):
    ny, nx, nz = s_out.shape
    pairs = list(zip((src_hbm, dg_hbm, fx_hbm, fy_hbm, fz_hbm), (src_out, dg_out, fx_out, fy_out, fz_out)))

    def copy_it(y):
        return pltpu.make_async_copy(it_hbm.at[:, :, y], work.at[:, y], sem_it.at[y])

    def copy_field(f, y):
        return pltpu.make_async_copy(pairs[f][0].at[:, y], pairs[f][1].at[y], sem_field.at[f, y])

    def start(y):
        copy_it(y).start()
        for f in range(len(pairs)):
            copy_field(f, y).start()

    loop(ny, start)

    spot = iota((nx, nx), 0) == iota((nx, nx), 1)
    ones = jnp.ones((nx, nz), jnp.bfloat16)
    labels = label_ref[...].astype(F32)
    for y in range(ny):
        row = jnp.where(spot, labels[y : y + 1], 0.0).astype(jnp.bfloat16)
        lb_out[y] = jnp.dot(row, ones, preferred_element_type=F32)

    def add(y):
        copy_it(y).wait()
        for r in range(0, nx, 8):
            total = work[0, y, r : r + 8]
            for j in range(1, ENLARGE):
                total = total + work[j, y, r : r + 8]
            s_out[y, r : r + 8] = total

    loop(ny, add)

    def finish(y):
        for f in range(len(pairs)):
            copy_field(f, y).wait()

    loop(ny, finish)
    even = lax.rem(lax.axis_index("gx"), 2) == 0
    sub = iota((8, nz), 0)

    def pack(y):
        hi = slice(nx - 8, nx)
        lo = slice(0, 8)
        roll = lambda v, n: pltpu.roll(v, n, 0)
        high1 = jnp.where(sub >= 5, s_out[y, hi], jnp.where(sub < 2, roll(lb_out[y, hi], 2), roll(fx_out[y, hi], 5)))
        low1 = jnp.where(sub < 3, s_out[y, lo], jnp.where(sub >= 6, roll(lb_out[y, lo], 6), roll(fx_out[y, lo], 3)))

        def second(at, first):
            values = src_out[y, at]
            for n, ref in enumerate((dg_out, fy_out, fz_out)):
                begin = (first + 2 * n + 2) % 8
                inside = jnp.logical_or(sub == begin, sub == begin + 1)
                values = jnp.where(inside, roll(ref[y, at], 2 * n + 2), values)
            return values

        high2 = second(hi, 6)
        low2 = second(lo, 0)
        for part, high, low in ((0, high1, low1), (1, high2, low2)):
            even_out[part, y] = jnp.where(even, high, low)
            odd_out[part, y] = jnp.where(even, low, high)

    loop(ny, pack)


def load(iterates, fields, labels):
    _, nx, ny, nz = iterates.shape
    field = array(ny, nx, nz)
    edge = array(2, ny, 8, nz)
    return pl.pallas_call(
        load_kernel,
        in_specs=hbm(6) + vmem(1),
        out_specs=vmem(9),
        out_shape=[field] * 7 + [edge] * 2,
        scratch_shapes=[
            pltpu.VMEM((ENLARGE, ny, nx, nz), F32),
            pltpu.SemaphoreType.DMA((ny,)),
            pltpu.SemaphoreType.DMA((5, ny)),
        ],
        compiler_params=params(),
        name="load",
    )(*[pinned(a) for a in (iterates, *fields)], labels.T)


def blocks_of(nx):
    wide = nx + PAD
    sizes = (wide, wide, wide, wide, nx, nx, nx, 8)
    starts = [sum(sizes[:i]) for i in range(len(sizes) + 1)]
    return wide, starts


def partial_kernel(
    gx, gy,
    s_in, src_in, dg_in, fx_in, fy_in, fz_in, lb_in, xe_ref, xo_ref,
    t_out, s_out, fx_out, fy_out, dg_out, fz_out, lb_out, ye_ref, yo_ref,
    src_ext,
):
    ny, nx, nz = s_in.shape
    pitch = nx + 2 * PAD
    lane = iota((8, nz), 1)
    even_x = lax.rem(lax.axis_index("gx"), 2) == 0
    last_x = lax.axis_index("gx") == gx - 1
    last_y = lax.axis_index("gy") == gy - 1
    last_row = jnp.logical_and(iota((8, nz), 0) == 7, last_x)

    def fill(y):
        top = jnp.logical_and(last_y, y == ny - 1)
        fy_of = lambda v: jnp.where(top, 0.0, v)
        fz_of = lambda v: jnp.where(lane == nz - 1, 0.0, v)
        base = y * pitch
        roll = lambda v, n: pltpu.roll(v, n, 0)
        for at, is_low in ((0, True), (PAD + nx, False)):
            one, two = [
                jnp.where(even_x == is_low, xo_ref[part, y], xe_ref[part, y]) for part in range(2)
            ]
            here = eight(base + at)
            s_out[here] = one
            fx_out[here] = roll(one, 3 if is_low else 5)
            lb_out[here] = roll(one, 6 if is_low else 2)
            src_ext[here] = two
            dg_out[here] = roll(two, 6)
            fy_out[here] = fy_of(roll(two, 4))
            fz_out[here] = fz_of(roll(two, 2))
        for r in range(0, nx, 8):
            here = eight(base + PAD + r)
            span = slice(r, r + 8)
            s_out[here] = s_in[y, span]
            face = fx_in[y, span]
            fx_out[here] = jnp.where(last_row, 0.0, face) if r == nx - 8 else face
            lb_out[here] = lb_in[y, span]
            src_ext[here] = src_in[y, span]
            dg_out[here] = dg_in[y, span]
            fy_out[here] = fy_of(fy_in[y, span])
            fz_out[here] = fz_of(fz_in[y, span])

    loop(ny, fill)

    def layer(y, down=True, up=True):
        base = y * pitch
        for r in range(0, pitch, 8):
            at = base + r
            here = eight(at)
            s, fx, fz = s_out[here], fx_out[here], fz_out[here]
            if r == 0:
                sm, fxm = pltpu.roll(s, 1, 0), pltpu.roll(fx, 1, 0)
            else:
                sm, fxm = s_out[near(at - 1)], fx_out[near(at - 1)]
            sp = pltpu.roll(s, 7, 0) if r == pitch - 8 else s_out[near(at + 1)]
            total = dg_out[here] * s - fx * sp - fxm * sm
            if up:
                total = total - fy_out[here] * s_out[eight(at + pitch)]
            if down:
                total = total - fy_out[eight(at - pitch)] * s_out[eight(at - pitch)]
            total = total - fz * pltpu.roll(s, nz - 1, 1) - pltpu.roll(fz * s, 1, 1)
            t_out[here] = src_ext[here] - total

    layer(0, down=False)
    layer(ny - 1, up=False)
    loop(ny - 2, lambda i: layer(i + 1))

    even_y = lax.rem(lax.axis_index("gy"), 2) == 0
    wide, starts = blocks_of(nx)

    def pack(dest, is_high):
        first = jnp.where(is_high, ny - 1, 0) * pitch
        second = jnp.where(is_high, ny - 2, 1) * pitch
        between = jnp.where(is_high, ny - 2, 0) * pitch

        def line(ref, base):
            return ref[pl.ds(base + (PAD - SENT), wide)]

        def inner(ref, base):
            return ref[pl.ds(pl.multiple_of(base + PAD, 8), nx)]

        parts = (
            line(t_out, first),
            line(s_out, first),
            line(fy_out, first),
            line(fx_out, first),
            inner(fy_out, between) * inner(t_out, second),
            inner(dg_out, first),
            inner(fz_out, first),
        )
        for b, values in enumerate(parts):
            dest[starts[b] : starts[b + 1]] = values
        spot = iota((wide, nz), 0) == iota((wide, nz), 1)
        one = jnp.sum(jnp.where(spot, line(lb_out, first), 0.0), axis=0, keepdims=True)
        two = jnp.sum(jnp.where(spot, line(lb_out, second), 0.0), axis=0, keepdims=True)
        which = iota((8, nz), 0)
        dest[starts[7] : starts[8]] = jnp.where(which == 0, one, jnp.where(which == 1, two, 0.0))

    pack(ye_ref, even_y)
    pack(yo_ref, jnp.logical_not(even_y))


def partial_residual(fields, xe, xo, gx, gy):
    ny, nx, nz = fields[0].shape
    rows = ny * (nx + 2 * PAD)
    ext = array(rows, nz)
    pack = array(blocks_of(nx)[1][-1], nz)
    return pl.pallas_call(
        functools.partial(partial_kernel, gx, gy),
        in_specs=vmem(9),
        out_specs=vmem(9),
        out_shape=[ext] * 7 + [pack] * 2,
        scratch_shapes=[pltpu.VMEM((rows, nz), F32)],
        compiler_params=params(),
        name="partial_residual",
    )(*fields, xe, xo)


def spread(parts):
    fields = []
    for j in range(ENLARGE):
        total = None
        for values, label in parts:
            term = jnp.where(label == float(j), values, 0.0)
            total = term if total is None else total + term
        fields.append(total)
    return fields


def along_z(fz, values):
    nz = values.shape[-1]
    return fz * pltpu.roll(values, nz - 1, 1) + pltpu.roll(fz * values, 1, 1)


def edge_near(ref, at, shift, last):
    if last == shift:
        return pltpu.roll(ref[eight(at)], 1 if shift < 0 else 7, 0)
    return ref[near(at + shift)]


def zeros_like_pairs(nz, count):
    return tuple(jnp.zeros((8, nz), F32) for _ in range(count))


def dot_own(sums, r, label, p):
    b = [jnp.where(label == float(j), r, 0.0) for j in range(ENLARGE)]
    n = len(PAIRS)
    own = tuple(t + v * v for t, v in zip(sums[n:], b))
    return tuple(t + b[j] * p[k] for t, (j, k) in zip(sums, PAIRS)) + own


def dot_pairs(sums, p, q):
    return tuple(t + p[j] * q[k] for t, (j, k) in zip(sums, PAIRS))


def clean_kernel(
    ny, nx,
    t_ref, fx_ref, fy_ref, dg_ref, fz_ref, lb_ref,
    p_out, q_out, acc_out,
):
    nz = t_ref.shape[-1]
    pitch = nx + 2 * PAD
    chunks = nx // 8

    def first(i):
        layer = (i + 2) * pitch
        for r in range(0, pitch, 8):
            at = layer + r
            last = -1 if r == 0 else (1 if r == pitch - 8 else 0)
            here = eight(at)
            value = t_ref[here]
            below, above = eight(at - pitch), eight(at + pitch)
            parts = [
                ((dg_ref[here] - SHIFT) * value - along_z(fz_ref[here], value), lb_ref[here]),
                (-fx_ref[here] * edge_near(t_ref, at, 1, last), edge_near(lb_ref, at, 1, last)),
                (-edge_near(fx_ref, at, -1, last) * edge_near(t_ref, at, -1, last), edge_near(lb_ref, at, -1, last)),
                (-fy_ref[here] * t_ref[above], lb_ref[above]),
                (-fy_ref[below] * t_ref[below], lb_ref[below]),
            ]
            for j, values in enumerate(spread(parts)):
                p_out[j, eight(i * pitch + r)] = values

    loop(ny - 4, first)

    def second(n):
        i, c = n // (chunks // 2), lax.rem(n, chunks // 2)
        for h in range(2):
            r = c * 16 + h * 8
            at = (i + 3) * pitch + PAD + r
            own = (i + 1) * pitch + PAD + r
            here = eight(at)
            dg, fz, fxp, fxm = dg_ref[here], fz_ref[here], fx_ref[here], fx_ref[near(at - 1)]
            fyp, fym = fy_ref[here], fy_ref[eight(at - pitch)]
            for j in range(ENLARGE):
                p = p_out[j, eight(own)]
                q = dg * p - fxp * p_out[j, near(own + 1)] - fxm * p_out[j, near(own - 1)]
                q = q - fyp * p_out[j, eight(own + pitch)] - fym * p_out[j, eight(own - pitch)]
                q_out[j, eight(i * nx + r)] = q - along_z(fz, p)

    loop((ny - 6) * chunks // 2, second)

    def fields_at(ref, at):
        return [ref[j, eight(at)] for j in range(ENLARGE)]

    def own_dots(n, sums):
        row = (n // chunks) * pitch + PAD + lax.rem(n, chunks) * 8
        shifted = eight(row + 2 * pitch)
        return dot_own(sums, t_ref[shifted], lb_ref[shifted], fields_at(p_out, row))

    def p_dots(n, sums):
        row = (n // chunks) * pitch + PAD + lax.rem(n, chunks) * 8
        p = fields_at(p_out, row)
        return dot_pairs(sums, p, p)

    def q_dots(n, sums):
        row = (n // chunks + 1) * pitch + PAD + lax.rem(n, chunks) * 8
        return dot_pairs(sums, fields_at(p_out, row), fields_at(q_out, n * 8))

    slot = 0
    for dots, layers, count in (
        (own_dots, ny - 4, len(PAIRS) + ENLARGE), (p_dots, ny - 4, len(PAIRS)), (q_dots, ny - 6, len(PAIRS)),
    ):
        sums = lax.fori_loop(0, layers * chunks, dots, zeros_like_pairs(nz, count), unroll=4)
        for values in sums:
            acc_out[slot] = values
            slot += 1


def clean_powers(ext, ny, nx):
    t, _, fx, fy, dg, fz, lb = ext
    nz = t.shape[-1]
    pitch = nx + 2 * PAD
    return pl.pallas_call(
        functools.partial(clean_kernel, ny, nx),
        in_specs=vmem(6),
        out_specs=vmem(3),
        out_shape=[
            array(ENLARGE, (ny - 4) * pitch, nz),
            array(ENLARGE, (ny - 6) * nx, nz),
            array(3 * len(PAIRS) + ENLARGE, 8, nz),
        ],
        compiler_params=params(),
        cost_estimate=pl.CostEstimate(flops=60_000_000, bytes_accessed=12_000_000, transcendentals=0),
        name="clean_powers",
    )(t, fx, fy, dg, fz, lb)


def edge_kernel(
    ny, nx, devices,
    t_ref, s_ref, fx_ref, fy_ref, dg_ref, fz_ref, lb_ref, pc_ref, acc_ref, ye_ref, yo_ref,
    p_out, q_out, r_out, gram_out,
    packs, face_g, fx_g, lb_g, lb_g2, rows_acc,
):
    nz = t_ref.shape[-1]
    pitch = nx + 2 * PAD
    chunks = nx // 8
    wide, starts = blocks_of(nx)
    odd = lax.rem(lax.axis_index("gy"), 2)
    packs[1 - odd] = ye_ref[...]
    packs[odd] = yo_ref[...]
    p_layers = (-1, 0, 1, ny - 2, ny - 1, ny)
    q_layers = (0, 1, 2, ny - 3, ny - 2, ny - 1)
    r_layers = (-1, 0, ny - 1, ny)
    left = PAD - SENT

    def packed(side, b):
        return packs[side, starts[b] : starts[b + 1]]

    for side in range(2):
        inner, outer = (0, -1) if side == 0 else (ny - 1, ny)
        base = pl.ds(inner * pitch + left, wide)
        face = packed(side, 2) if side == 0 else fy_ref[base]
        at = lambda y: pl.ds(r_layers.index(y) * pitch + left, wide)
        r_out[at(outer)] = packed(side, 0) + face * s_ref[base]
        r_out[at(inner)] = t_ref[base] + face * packed(side, 1)
        if side == 0:
            face_g[pl.ds(left, wide)] = face
        ghost = pl.ds(side * pitch + left, wide)
        fx_g[ghost] = packed(side, 3)
        labels = packed(side, 7)
        spot = iota((wide, nz), 0) == iota((wide, nz), 1)
        for r, dest in ((0, lb_g), (1, lb_g2)):
            column = jnp.sum(jnp.where(spot, labels[r : r + 1], 0.0), axis=1, keepdims=True)
            dest[ghost] = jnp.broadcast_to(column, (wide, nz))

    def r_at(y):
        return (r_out, r_layers.index(y) * pitch) if y in r_layers else (t_ref, y * pitch)

    def label_at(y):
        if 0 <= y < ny:
            return lb_ref, y * pitch
        return lb_g, (0 if y < 0 else pitch)

    def face_at(y):
        return (face_g, 0) if y < 0 else (fy_ref, y * pitch)

    def p_at(y):
        return (p_out, p_layers.index(y) * pitch) if y in p_layers else (pc_ref, (y - 2) * pitch)

    def first(y, r, last=0):
        ref, base = r_at(y)
        labels, label_base = label_at(y)
        at = base + r
        mark = label_base + r
        value = ref[eight(at)]
        if 0 <= y < ny:
            dg, fz = dg_ref[eight(y * pitch + r)], fz_ref[eight(y * pitch + r)]
            fxs, fx_base = fx_ref, y * pitch
        else:
            side = 0 if y < 0 else 1
            dg, fz = [packs[side, eight(starts[b] + r - PAD)] for b in (5, 6)]
            fxs, fx_base = fx_g, side * pitch
        fx_row = fx_base + r
        parts = [
            ((dg - SHIFT) * value - along_z(fz, value), labels[eight(mark)]),
            (-fxs[eight(fx_row)] * edge_near(ref, at, 1, last), edge_near(labels, mark, 1, last)),
            (-edge_near(fxs, fx_row, -1, last) * edge_near(ref, at, -1, last), edge_near(labels, mark, -1, last)),
        ]
        for step in (-1, 1):
            if not -1 <= y + step <= ny:
                side = 0 if y < 0 else 1
                parts.append((-packs[side, eight(starts[4] + r - PAD)], lb_g2[eight(side * pitch + r)]))
                continue
            ref2, base2 = r_at(y + step)
            labels2, label_base2 = label_at(y + step)
            face, face_base = face_at(min(y, y + step))
            parts.append((-face[eight(face_base + r)] * ref2[eight(base2 + r)], labels2[eight(label_base2 + r)]))
        for j, values in enumerate(spread(parts)):
            p_out[j, eight(p_layers.index(y) * pitch + r)] = values

    for y in p_layers:
        if 0 <= y < ny:
            first(y, 0, -1)
            first(y, pitch - 8, 1)
        loop(chunks, lambda c, y=y: first(y, aligned(PAD + c * 8)), unroll=2)

    def second(y, c):
        r = aligned(PAD + c * 8)
        row = y * pitch + r
        here = eight(row)
        dg, fz, fxp, fxm = dg_ref[here], fz_ref[here], fx_ref[here], fx_ref[near(row - 1)]
        face, face_base = face_at(y - 1)
        fyp, fym = fy_ref[here], face[eight(face_base + r)]
        (mid, mid_base), (low, low_base), (high, high_base) = p_at(y), p_at(y - 1), p_at(y + 1)
        for j in range(ENLARGE):
            p = mid[j, eight(mid_base + r)]
            q = dg * p - fxp * mid[j, near(mid_base + r + 1)] - fxm * mid[j, near(mid_base + r - 1)]
            q = q - fyp * high[j, eight(high_base + r)] - fym * low[j, eight(low_base + r)]
            q_out[j, eight(q_layers.index(y) * nx + c * 8)] = q - along_z(fz, p)

    for y in q_layers:
        loop(chunks, lambda c, y=y: second(y, c), unroll=2)

    def fields_at(ref, at):
        return [ref[j, eight(at)] for j in range(ENLARGE)]

    n = len(PAIRS)
    stored = [acc_ref[i] for i in range(n + ENLARGE)]
    sums = tuple(stored)
    for y in (0, 1, ny - 2, ny - 1):

        def body(c, sums, y=y):
            r = PAD + c * 8
            ref, base = r_at(y)
            own = fields_at(p_out, p_layers.index(y) * pitch + r)
            return dot_own(sums, ref[eight(base + r)], lb_ref[eight(y * pitch + r)], own)

        sums = lax.fori_loop(0, chunks, body, sums, unroll=4)
    rows_acc[...] = jnp.zeros_like(rows_acc)
    span = ENLARGE * ENLARGE

    def put(slot, values):
        rows_acc[slot : slot + 1] = jnp.sum(values, axis=0, keepdims=True)

    def put_pairs(which, sums):
        for (j, k), values in zip(PAIRS, sums):
            put(which * span + j * ENLARGE + k, values)
            if j != k:
                put(which * span + k * ENLARGE + j, values)

    put_pairs(0, sums)
    for j in range(ENLARGE):
        put(3 * span + j * ENLARGE + j, sums[n + j])
    begin = n + ENLARGE
    for which, layers in ((1, (0, 1, ny - 2, ny - 1)), (2, q_layers)):
        sums = tuple(acc_ref[begin + i] for i in range(n))
        begin += n
        for y in layers:

            def body(c, sums, y=y, which=which):
                ref, base = p_at(y)
                p = fields_at(ref, base + PAD + c * 8)
                q = p if which == 1 else fields_at(q_out, q_layers.index(y) * nx + c * 8)
                return dot_pairs(sums, p, q)

            sums = lax.fori_loop(0, chunks, body, sums, unroll=4)
        put_pairs(which, sums)
    ones = jnp.ones((8, nz), F32)
    flat = lax.dot_general(
        ones, rows_acc[...], (((1,), (1,)), ((), ())), precision=HIGHEST, preferred_element_type=F32
    )
    half = 2 * span
    pair = jnp.where(iota((2, half), 0) == 0, flat[0:2, 0:half], flat[0:2, half : 2 * half])
    for d in range(devices):
        gram_out[d] = pair


def edge_powers(ext, pc, acc, ye, yo, ny, nx, devices):
    nz = pc.shape[-1]
    pitch = nx + 2 * PAD
    half = 2 * ENLARGE * ENLARGE
    return pl.pallas_call(
        functools.partial(edge_kernel, ny, nx, devices),
        in_specs=vmem(11),
        out_specs=vmem(4),
        out_shape=[
            array(ENLARGE, 6 * pitch, nz), array(ENLARGE, 6 * nx, nz), array(4 * pitch, nz), array(devices, 2, half),
        ],
        scratch_shapes=[
            pltpu.VMEM((2,) + ye.shape, F32),
            pltpu.VMEM((pitch, nz), F32),
            pltpu.VMEM((2 * pitch, nz), F32),
            pltpu.VMEM((2 * pitch, nz), F32),
            pltpu.VMEM((2 * pitch, nz), F32),
            pltpu.VMEM((2 * half, nz), F32),
        ],
        compiler_params=params(),
        name="edge_powers",
    )(*ext, pc, acc, ye, yo)


def solve_columns(parts):
    nz = parts.shape[-1]
    span = ENLARGE * ENLARGE
    v = jnp.sum(parts, axis=0)
    lhs = jnp.concatenate([jnp.broadcast_to(v[0:1], (8, nz)), jnp.broadcast_to(v[1:2], (8, nz))], axis=1)
    source = iota((8, 2 * nz), 1)
    lhs = jnp.where(iota((8, 2 * nz), 0) == lax.rem(source, span) // ENLARGE, lhs, 0.0)
    k = iota((2 * nz, nz), 0)
    n = iota((2 * nz, nz), 1)
    which = k // span
    column = lax.rem(k, ENLARGE)

    def place(block, offset, scale):
        return jnp.where(jnp.logical_and(which == block, n == column + offset), scale, 0.0)

    upper = place(0, 0, 1.0) + place(3, 0, SHIFT) + place(1, 8, 1.0) + place(0, 8, SHIFT) + place(3, 16, 1.0)
    lower = place(1, 0, 1.0) + place(0, 0, SHIFT) + place(2, 8, 1.0) + place(0, 16, 1.0)
    dot = functools.partial(jnp.dot, precision=HIGHEST, preferred_element_type=F32)
    m = jnp.concatenate([dot(lhs, upper), dot(lhs, lower)], axis=0)
    row = iota(m.shape, 0)
    for i in range(2 * ENLARGE):
        pivot = m[i : i + 1] / m[i : i + 1, i : i + 1]
        m = jnp.where(row == i, pivot, m - m[:, i : i + 1] * pivot)
    return m


def update_kernel(
    ny, nx, parts_ref, pc_ref, qc_ref, pd_ref, qd_ref, t_ref, rd_ref, lb_ref, it_hbm,
    it_out, r_out,
    table, weights, onehot, own, work, r_work, sem_in, sem_out, sem_r,
):
    nz = t_ref.shape[-1]
    pitch = nx + 2 * PAD
    two = 2 * ENLARGE
    square = ENLARGE * ENLARGE

    def copy_in(y):
        return pltpu.make_async_copy(it_hbm.at[:, :, y], work.at[:, y], sem_in.at[y])

    def copy_out(y):
        return pltpu.make_async_copy(work.at[:, y], it_out.at[:, :, y], sem_out.at[y])

    def copy_r(y):
        return pltpu.make_async_copy(r_work.at[y], r_out.at[:, y], sem_r.at[y])

    loop(ny, lambda y: copy_in(y).start())

    def mark(y):
        lane = iota((nx, nz), 1)
        labels = lb_ref[pl.ds(pl.multiple_of(y * pitch + PAD, 8), nx)]
        chosen = jnp.logical_and(lane < 3 * ENLARGE, lax.rem(lane, ENLARGE).astype(F32) == labels)
        onehot[pl.ds(pl.multiple_of(y * nx, nx), nx)] = jnp.where(chosen, 1.0, 0.0).astype(jnp.bfloat16)

    loop(ny, mark)

    m = solve_columns(parts_ref[...])
    lane = iota(m.shape, 1)
    inside = jnp.logical_and(lane >= two, lane < two + ENLARGE)
    carried = jnp.sum(jnp.where(inside, m, 0.0), axis=1, keepdims=True)
    for j in range(ENLARGE):
        for k in range(ENLARGE):
            value = m[ENLARGE + k : ENLARGE + k + 1, two + j : two + j + 1]
            table[j * ENLARGE + k] = jnp.broadcast_to(value, (8, nz))
    for k in range(two):
        table[square + k] = jnp.broadcast_to(carried[k : k + 1], (8, nz))
    lane = iota((ENLARGE, nz), 1)
    mine = pltpu.roll(m[0:ENLARGE], nz - two, 1)
    mine = jnp.where(lane < ENLARGE, mine, jnp.where(lane == ENLARGE, carried[0:ENLARGE], 0.0))
    high = mine.astype(jnp.bfloat16).astype(F32)
    mid = (mine - high).astype(jnp.bfloat16).astype(F32)
    weights[...] = jnp.zeros_like(weights)
    weights[0:8] = high
    weights[8:16] = mid
    weights[16:24] = mine - high - mid
    own[...] = jnp.dot(onehot[...], weights[...].astype(jnp.bfloat16), preferred_element_type=F32)

    def layer(y, p_ref, p_base, q_ref, q_base, r_ref, r_base):
        copy_in(y).wait()

        def body(c):
            x = [c * 16, c * 16 + 8]
            at = [eight(v) for v in x]
            r = [r_ref[eight(r_base + v)] for v in x]
            p = [[p_ref[k, eight(p_base + v)] for k in range(ENLARGE)] for v in x]
            mine = [own[eight(y * nx + v)] for v in x]
            for j in range(ENLARGE):
                scale = [table[j * ENLARGE + k] for k in range(ENLARGE)]
                for h in range(2):
                    total = work[j, y, at[h]] + mine[h][:, j : j + 1] * r[h]
                    for k in range(ENLARGE):
                        total = total + scale[k] * p[h][k]
                    work[j, y, at[h]] = total
            scale = [table[square + k] for k in range(two)]
            for h in range(2):
                total = r[h] - (SHIFT * mine[h][:, ENLARGE : ENLARGE + 1]) * r[h]
                for k in range(ENLARGE):
                    q = q_ref[k, eight(q_base + x[h])]
                    total = total - scale[k] * p[h][k] - scale[ENLARGE + k] * q
                r_work[y, at[h]] = total

        loop(nx // 16, body)
        copy_out(y).start()
        copy_r(y).start()

    def clean(i):
        y = i + 3
        layer(y, pc_ref, (i + 1) * pitch + PAD, qc_ref, i * nx, t_ref, y * pitch + PAD)

    loop(ny - 6, clean)
    p_layers = (-1, 0, 1, ny - 2, ny - 1, ny)
    q_layers = (0, 1, 2, ny - 3, ny - 2, ny - 1)
    r_layers = (-1, 0, ny - 1, ny)
    for i, y in enumerate(q_layers):
        p = (pd_ref, p_layers.index(y) * pitch + PAD) if y in p_layers else (pc_ref, (y - 2) * pitch + PAD)
        r = (rd_ref, r_layers.index(y) * pitch + PAD) if y in r_layers else (t_ref, y * pitch + PAD)
        layer(y, *p, qd_ref, i * nx, *r)
    loop(ny, lambda y: copy_out(y).wait())
    loop(ny, lambda y: copy_r(y).wait())


def update(parts, pc, qc, pd, qd, t, rd, labels, iterates):
    _, nx, ny, nz = iterates.shape
    return pl.pallas_call(
        functools.partial(update_kernel, ny, nx),
        in_specs=vmem(8) + hbm(1),
        out_specs=hbm(2),
        out_shape=[array(ENLARGE, nx, ny, nz), array(nx, ny, nz)],
        scratch_shapes=[
            pltpu.VMEM((ENLARGE * ENLARGE + 2 * ENLARGE, 8, nz), F32),
            pltpu.VMEM((nz, nz), F32),
            pltpu.VMEM((ny * nx, nz), jnp.bfloat16),
            pltpu.VMEM((ny * nx, nz), F32),
            pltpu.VMEM((ENLARGE, ny, nx, nz), F32),
            pltpu.VMEM((ny, nx, nz), F32),
            pltpu.SemaphoreType.DMA((ny,)),
            pltpu.SemaphoreType.DMA((ny,)),
            pltpu.SemaphoreType.DMA((ny,)),
        ],
        compiler_params=params(),
        name="update",
    )(parts, pc, qc, pd, qd, t, rd, labels, pinned(iterates))


def shards(gx, gy, source, diagonal, face_x, face_y, face_z, iterates, labels):
    _, nx, ny, nz = iterates.shape
    *fields, xe, xo = load(iterates, (source, diagonal, face_x, face_y, face_z), labels)
    xe = lax.ppermute(xe, "gx", even_pairs(gx))
    xo = lax.ppermute(xo, "gx", odd_pairs(gx))
    *ext, ye, yo = partial_residual(fields, xe, xo, gx, gy)
    ye = lax.ppermute(ye, "gy", even_pairs(gy))
    yo = lax.ppermute(yo, "gy", odd_pairs(gy))
    pc, qc, acc = clean_powers(ext, ny, nx)
    pd, qd, rd, gram = edge_powers(ext, pc, acc, ye, yo, ny, nx, gx * gy)
    parts = lax.all_to_all(gram, ("gx", "gy"), 0, 0, tiled=True)
    return update(parts, pc, qc, pd, qd, ext[0], rd, ext[-1], iterates)


def solution(mesh):
    placed = (
        P("gx", "gy", None),
        P("gx", "gy", None),
        P("gx", "gy", None),
        P("gx", "gy", None),
        P("gx", "gy", None),
        P(None, "gx", "gy", None),
        P("gx", "gy"),
    )
    return jax.shard_map(
        functools.partial(shards, mesh.shape["gx"], mesh.shape["gy"]),
        mesh=mesh,
        in_specs=placed,
        out_specs=(P(None, "gx", "gy", None), P("gx", "gy", None)),
        check_vma=False,
    )
```

```python
import functools

import jax
import jax.numpy as jnp
from jax import lax
from jax.experimental import pallas as pl
from jax.experimental.pallas import tpu as pltpu
from jax.sharding import PartitionSpec as P

ENLARGE = 8
SHIFT = 6.5
F32 = jnp.float32
HIGHEST = lax.Precision.HIGHEST
PAIRS = [(j, k) for j in range(ENLARGE) for k in range(j, ENLARGE)]
VMEM_LIMIT = 20 * 1024 * 1024
PAD = 8
SENT = 2


def iota(shape, dim):
    return lax.broadcasted_iota(jnp.int32, shape, dim)


def even_pairs(count):
    return [(i, i ^ 1) for i in range(count) if (i ^ 1) < count]


def odd_pairs(count):
    return [(i, ((i - 1) ^ 1) + 1) for i in range(1, count) if ((i - 1) ^ 1) + 1 < count]


def vmem(count):
    return [pl.BlockSpec(memory_space=pltpu.VMEM)] * count


def hbm(count):
    return [pl.BlockSpec(memory_space=pltpu.HBM)] * count


def pinned(value):
    return pltpu.with_memory_space_constraint(value, pltpu.HBM)


def array(*shape):
    return jax.ShapeDtypeStruct(shape, F32)


def params():
    return pltpu.CompilerParams(vmem_limit_bytes=VMEM_LIMIT)


def aligned(value):
    return value if isinstance(value, int) else pl.multiple_of(value, 8)


def eight(start):
    return pl.ds(aligned(start), 8)


def near(start):
    return pl.ds(start, 8)


def loop(count, body, **kw):
    def wrapped(i, carry):
        body(i)
        return carry

    lax.fori_loop(0, count, wrapped, 0, **kw)


def edges_kernel(
    it_hbm, src_hbm, dg_hbm, fx_hbm, fy_hbm, fz_hbm, label_hbm,
    even_out, odd_out,
    work, fields, labels, sem_it, sem_field, sem_label,
):
    _, nx, ny, nz = it_hbm.shape
    sources = (src_hbm, dg_hbm, fx_hbm, fy_hbm, fz_hbm)
    lines = [(x, x) for x in range(3)] + [(nx - 3 + x, 13 + x) for x in range(3)]
    copies = [pltpu.make_async_copy(label_hbm, labels, sem_label)]
    for n, (x, row) in enumerate(lines):
        copies.append(pltpu.make_async_copy(it_hbm.at[:, x], work.at[:, :, row], sem_it.at[n]))
        for f, ref in enumerate(sources):
            copies.append(pltpu.make_async_copy(ref.at[x], fields.at[f, :, row], sem_field.at[f, n]))
    for copy in copies:
        copy.start()
    copies[0].wait()
    spread_rows = iota((16, nx), 0)
    spot = jnp.where(spread_rows < 8, spread_rows, spread_rows + nx - 16) == iota((16, nx), 1)
    ones = jnp.ones((nx, nz), jnp.bfloat16)
    marks = labels[...].astype(F32)
    for copy in copies[1:]:
        copy.wait()
    even = lax.rem(lax.axis_index("gx"), 2) == 0
    sub = iota((8, nz), 0)
    roll = lambda v, n: pltpu.roll(v, n, 0)
    for y in range(ny):
        row = jnp.where(spot, marks[y : y + 1], 0.0).astype(jnp.bfloat16)
        lb = jnp.dot(row, ones, preferred_element_type=F32)
        total = work[0, y]
        for j in range(1, ENLARGE):
            total = total + work[j, y]
        src, dg, fx, fy, fz = [fields[f, y] for f in range(5)]

        def first(at, is_low):
            if is_low:
                return jnp.where(sub < 3, total[at], jnp.where(sub >= 6, roll(lb[at], 6), roll(fx[at], 3)))
            return jnp.where(sub >= 5, total[at], jnp.where(sub < 2, roll(lb[at], 2), roll(fx[at], 5)))

        def second(at, start):
            values = src[at]
            for n, field in enumerate((dg, fy, fz)):
                begin = (start + 2 * n + 2) % 8
                inside = jnp.logical_or(sub == begin, sub == begin + 1)
                values = jnp.where(inside, roll(field[at], 2 * n + 2), values)
            return values

        lo, hi = slice(0, 8), slice(8, 16)
        for part, high, low in ((0, first(hi, False), first(lo, True)), (1, second(hi, 6), second(lo, 0))):
            even_out[part, y] = jnp.where(even, high, low)
            odd_out[part, y] = jnp.where(even, low, high)


def x_edges(arrays):
    _, nx, ny, nz = arrays[0].shape
    edge = array(2, ny, 8, nz)
    return pl.pallas_call(
        edges_kernel,
        in_specs=hbm(7),
        out_specs=vmem(2),
        out_shape=[edge] * 2,
        scratch_shapes=[
            pltpu.VMEM((ENLARGE, ny, 16, nz), F32),
            pltpu.VMEM((5, ny, 16, nz), F32),
            pltpu.VMEM((ny, nx), jnp.int32),
            pltpu.SemaphoreType.DMA((6,)),
            pltpu.SemaphoreType.DMA((5, 6)),
            pltpu.SemaphoreType.DMA,
        ],
        compiler_params=params(),
        name="x_edges",
    )(*arrays)


def load_kernel(
    it_hbm, src_hbm, dg_hbm, fx_hbm, fy_hbm, fz_hbm, label_hbm,
    s_out, src_out, dg_out, fx_out, fy_out, fz_out, lb_out, work,
    label_ref, sem_it, sem_field, sem_label,
):
    ny, nx, nz = s_out.shape
    pairs = list(zip((src_hbm, dg_hbm, fx_hbm, fy_hbm, fz_hbm), (src_out, dg_out, fx_out, fy_out, fz_out)))
    label_copy = pltpu.make_async_copy(label_hbm, label_ref, sem_label)

    def copy_it(y):
        return pltpu.make_async_copy(it_hbm.at[:, :, y], work.at[:, y], sem_it.at[y])

    def copy_field(f, y):
        return pltpu.make_async_copy(pairs[f][0].at[:, y], pairs[f][1].at[y], sem_field.at[f, y])

    def start(y):
        copy_it(y).start()
        for f in range(len(pairs)):
            copy_field(f, y).start()

    label_copy.start()
    loop(ny, start)
    label_copy.wait()

    spot = iota((nx, nx), 0) == iota((nx, nx), 1)
    ones = jnp.ones((nx, nz), jnp.bfloat16)
    labels = label_ref[...].astype(F32)
    for y in range(ny):
        row = jnp.where(spot, labels[y : y + 1], 0.0).astype(jnp.bfloat16)
        lb_out[y] = jnp.dot(row, ones, preferred_element_type=F32)

    def add(y):
        copy_it(y).wait()
        for r in range(0, nx, 8):
            total = work[0, y, r : r + 8]
            for j in range(1, ENLARGE):
                total = total + work[j, y, r : r + 8]
            s_out[y, r : r + 8] = total

    loop(ny, add)

    def finish(y):
        for f in range(len(pairs)):
            copy_field(f, y).wait()

    loop(ny, finish)


def load(arrays):
    _, nx, ny, nz = arrays[0].shape
    field = array(ny, nx, nz)
    return pl.pallas_call(
        load_kernel,
        in_specs=hbm(7),
        out_specs=vmem(8),
        out_shape=[field] * 7 + [array(ENLARGE, ny, nx, nz)],
        scratch_shapes=[
            pltpu.VMEM((ny, nx), jnp.int32),
            pltpu.SemaphoreType.DMA((ny,)),
            pltpu.SemaphoreType.DMA((5, ny)),
            pltpu.SemaphoreType.DMA,
        ],
        compiler_params=params(),
        cost_estimate=pl.CostEstimate(flops=2_000_000, bytes_accessed=16_000_000, transcendentals=0),
        name="load",
    )(*arrays)


def blocks_of(nx):
    wide = nx + PAD
    sizes = (wide, wide, wide, wide, nx, nx, nx, 8)
    starts = [sum(sizes[:i]) for i in range(len(sizes) + 1)]
    return wide, starts


def pack_y_edge(ny, nx, dest, is_high, t, s, fy, fx, dg, fz, lb):
    pitch = nx + 2 * PAD
    nz = t.shape[-1]
    wide, starts = blocks_of(nx)
    first = jnp.where(is_high, ny - 1, 0) * pitch
    second = jnp.where(is_high, ny - 2, 1) * pitch
    between = jnp.where(is_high, ny - 2, 0) * pitch

    def line(ref, base):
        return ref[pl.ds(base + (PAD - SENT), wide)]

    def inner(ref, base):
        return ref[pl.ds(pl.multiple_of(base + PAD, 8), nx)]

    parts = (
        line(t, first),
        line(s, first),
        line(fy, first),
        line(fx, first),
        inner(fy, between) * inner(t, second),
        inner(dg, first),
        inner(fz, first),
    )
    for b, values in enumerate(parts):
        dest[starts[b] : starts[b + 1]] = values
    spot = iota((wide, nz), 0) == iota((wide, nz), 1)
    one = jnp.sum(jnp.where(spot, line(lb, first), 0.0), axis=0, keepdims=True)
    two = jnp.sum(jnp.where(spot, line(lb, second), 0.0), axis=0, keepdims=True)
    which = iota((8, nz), 0)
    dest[starts[7] : starts[8]] = jnp.where(which == 0, one, jnp.where(which == 1, two, 0.0))


def partial_kernel(
    gx, gy,
    s_in, src_in, dg_in, fx_in, fy_in, fz_in, lb_in, xe_ref, xo_ref,
    t_out, s_out, fx_out, fy_out, dg_out, fz_out, lb_out, ye_ref,
    src_ext,
):
    ny, nx, nz = s_in.shape
    pitch = nx + 2 * PAD
    lane = iota((8, nz), 1)
    even_x = lax.rem(lax.axis_index("gx"), 2) == 0
    last_x = lax.axis_index("gx") == gx - 1
    last_y = lax.axis_index("gy") == gy - 1
    last_row = jnp.logical_and(iota((8, nz), 0) == 7, last_x)

    def fill(y):
        top = jnp.logical_and(last_y, y == ny - 1)
        fy_of = lambda v: jnp.where(top, 0.0, v)
        fz_of = lambda v: jnp.where(lane == nz - 1, 0.0, v)
        base = y * pitch
        roll = lambda v, n: pltpu.roll(v, n, 0)
        for at, is_low in ((0, True), (PAD + nx, False)):
            one, two = [
                jnp.where(even_x == is_low, xo_ref[part, y], xe_ref[part, y]) for part in range(2)
            ]
            here = eight(base + at)
            s_out[here] = one
            fx_out[here] = roll(one, 3 if is_low else 5)
            lb_out[here] = roll(one, 6 if is_low else 2)
            src_ext[here] = two
            dg_out[here] = roll(two, 6)
            fy_out[here] = fy_of(roll(two, 4))
            fz_out[here] = fz_of(roll(two, 2))
        for r in range(0, nx, 8):
            here = eight(base + PAD + r)
            span = slice(r, r + 8)
            s_out[here] = s_in[y, span]
            face = fx_in[y, span]
            fx_out[here] = jnp.where(last_row, 0.0, face) if r == nx - 8 else face
            lb_out[here] = lb_in[y, span]
            src_ext[here] = src_in[y, span]
            dg_out[here] = dg_in[y, span]
            fy_out[here] = fy_of(fy_in[y, span])
            fz_out[here] = fz_of(fz_in[y, span])

    loop(ny, fill)

    def layer(y, down=True, up=True):
        base = y * pitch
        for r in range(0, pitch, 8):
            at = base + r
            here = eight(at)
            s, fx, fz = s_out[here], fx_out[here], fz_out[here]
            if r == 0:
                sm, fxm = pltpu.roll(s, 1, 0), pltpu.roll(fx, 1, 0)
            else:
                sm, fxm = s_out[near(at - 1)], fx_out[near(at - 1)]
            sp = pltpu.roll(s, 7, 0) if r == pitch - 8 else s_out[near(at + 1)]
            total = dg_out[here] * s - fx * sp - fxm * sm
            if up:
                total = total - fy_out[here] * s_out[eight(at + pitch)]
            if down:
                total = total - fy_out[eight(at - pitch)] * s_out[eight(at - pitch)]
            total = total - fz * pltpu.roll(s, nz - 1, 1) - pltpu.roll(fz * s, 1, 1)
            t_out[here] = src_ext[here] - total

    layer(0, down=False)
    layer(ny - 1, up=False)
    loop(ny - 2, lambda i: layer(i + 1))

    even_y = lax.rem(lax.axis_index("gy"), 2) == 0
    pack_y_edge(ny, nx, ye_ref, even_y, t_out, s_out, fy_out, fx_out, dg_out, fz_out, lb_out)


def partial_residual(fields, xe, xo, gx, gy):
    ny, nx, nz = fields[0].shape
    rows = ny * (nx + 2 * PAD)
    ext = array(rows, nz)
    pack = array(blocks_of(nx)[1][-1], nz)
    return pl.pallas_call(
        functools.partial(partial_kernel, gx, gy),
        in_specs=vmem(9),
        out_specs=vmem(8),
        out_shape=[ext] * 7 + [pack],
        scratch_shapes=[pltpu.VMEM((rows, nz), F32)],
        compiler_params=params(),
        name="partial_residual",
    )(*fields, xe, xo)


def spread(parts):
    fields = []
    for j in range(ENLARGE):
        total = None
        for values, label in parts:
            term = jnp.where(label == float(j), values, 0.0)
            total = term if total is None else total + term
        fields.append(total)
    return fields


def along_z(fz, values):
    nz = values.shape[-1]
    return fz * pltpu.roll(values, nz - 1, 1) + pltpu.roll(fz * values, 1, 1)


def edge_near(ref, at, shift, last):
    if last == shift:
        return pltpu.roll(ref[eight(at)], 1 if shift < 0 else 7, 0)
    return ref[near(at + shift)]


def zeros_like_pairs(nz, count):
    return tuple(jnp.zeros((8, nz), F32) for _ in range(count))


def dot_own(sums, r, label, p):
    b = [jnp.where(label == float(j), r, 0.0) for j in range(ENLARGE)]
    n = len(PAIRS)
    own = tuple(t + v * v for t, v in zip(sums[n:], b))
    return tuple(t + b[j] * p[k] for t, (j, k) in zip(sums, PAIRS)) + own


def dot_pairs(sums, p, q):
    return tuple(t + p[j] * q[k] for t, (j, k) in zip(sums, PAIRS))


def clean_first_kernel(
    ny, nx,
    t_ref, s_ref, fx_ref, fy_ref, dg_ref, fz_ref, lb_ref,
    p_out, yo_ref,
):
    pitch = nx + 2 * PAD

    def first(i):
        layer = (i + 2) * pitch
        for r in range(0, pitch, 8):
            at = layer + r
            last = -1 if r == 0 else (1 if r == pitch - 8 else 0)
            here = eight(at)
            value = t_ref[here]
            below, above = eight(at - pitch), eight(at + pitch)
            parts = [
                ((dg_ref[here] - SHIFT) * value - along_z(fz_ref[here], value), lb_ref[here]),
                (-fx_ref[here] * edge_near(t_ref, at, 1, last), edge_near(lb_ref, at, 1, last)),
                (-edge_near(fx_ref, at, -1, last) * edge_near(t_ref, at, -1, last), edge_near(lb_ref, at, -1, last)),
                (-fy_ref[here] * t_ref[above], lb_ref[above]),
                (-fy_ref[below] * t_ref[below], lb_ref[below]),
            ]
            for j, values in enumerate(spread(parts)):
                p_out[j, eight(i * pitch + r)] = values

    loop(ny - 4, first)
    odd_y = lax.rem(lax.axis_index("gy"), 2) == 1
    pack_y_edge(ny, nx, yo_ref, odd_y, t_ref, s_ref, fy_ref, fx_ref, dg_ref, fz_ref, lb_ref)


def clean_second_kernel(
    ny, nx,
    t_ref, fx_ref, fy_ref, dg_ref, fz_ref, lb_ref, p_out,
    q_out, acc_out,
):
    nz = t_ref.shape[-1]
    pitch = nx + 2 * PAD
    chunks = nx // 8

    def second(i):
        for c in range(chunks):
            at = (i + 3) * pitch + PAD + c * 8
            own = (i + 1) * pitch + PAD + c * 8
            here = eight(at)
            dg, fz, fxp, fxm = dg_ref[here], fz_ref[here], fx_ref[here], fx_ref[near(at - 1)]
            fyp, fym = fy_ref[here], fy_ref[eight(at - pitch)]
            for j in range(ENLARGE):
                p = p_out[j, eight(own)]
                q = dg * p - fxp * p_out[j, near(own + 1)] - fxm * p_out[j, near(own - 1)]
                q = q - fyp * p_out[j, eight(own + pitch)] - fym * p_out[j, eight(own - pitch)]
                q_out[j, eight(i * nx + c * 8)] = q - along_z(fz, p)

    loop(ny - 6, second)

    def fields_at(ref, at):
        return [ref[j, eight(at)] for j in range(ENLARGE)]

    def own_dots(i, sums):
        for c in range(chunks):
            row = i * pitch + PAD + c * 8
            shifted = eight(row + 2 * pitch)
            sums = dot_own(sums, t_ref[shifted], lb_ref[shifted], fields_at(p_out, row))
        return sums

    def p_dots(i, sums):
        for c in range(chunks):
            p = fields_at(p_out, i * pitch + PAD + c * 8)
            sums = dot_pairs(sums, p, p)
        return sums

    def q_dots(i, sums):
        for c in range(chunks):
            p = fields_at(p_out, (i + 1) * pitch + PAD + c * 8)
            sums = dot_pairs(sums, p, fields_at(q_out, i * nx + c * 8))
        return sums

    slot = 0
    for dots, layers, count in (
        (own_dots, ny - 4, len(PAIRS) + ENLARGE), (p_dots, ny - 4, len(PAIRS)), (q_dots, ny - 6, len(PAIRS)),
    ):
        sums = lax.fori_loop(0, layers, dots, zeros_like_pairs(nz, count))
        for values in sums:
            acc_out[slot] = values
            slot += 1


def clean_first(ext, ny, nx):
    nz = ext[0].shape[-1]
    return pl.pallas_call(
        functools.partial(clean_first_kernel, ny, nx),
        in_specs=vmem(7),
        out_specs=vmem(2),
        out_shape=[array(ENLARGE, (ny - 4) * (nx + 2 * PAD), nz), array(blocks_of(nx)[1][-1], nz)],
        compiler_params=params(),
        cost_estimate=pl.CostEstimate(flops=20_000_000, bytes_accessed=8_000_000, transcendentals=0),
        name="clean_first",
    )(*ext)


def clean_second(ext, pc, ny, nx):
    t, _, fx, fy, dg, fz, lb = ext
    nz = t.shape[-1]
    return pl.pallas_call(
        functools.partial(clean_second_kernel, ny, nx),
        in_specs=vmem(7),
        out_specs=vmem(2),
        out_shape=[array(ENLARGE, (ny - 6) * nx, nz), array(3 * len(PAIRS) + ENLARGE, 8, nz)],
        compiler_params=params(),
        cost_estimate=pl.CostEstimate(flops=40_000_000, bytes_accessed=12_000_000, transcendentals=0),
        name="clean_second",
    )(t, fx, fy, dg, fz, lb, pc)


def edge_slot(y, ny):
    return y + 2 if y < 4 else y - (ny - 4) + 6


def edge_kernel(
    ny, nx, devices,
    t_ref, s_ref, fx_ref, fy_ref, dg_ref, fz_ref, lb_ref, pc_ref, acc_ref, ye_ref, yo_ref,
    p_out, q_out, r_out, lb_out, gram_out,
    packs, fx, fy, dg, fz, rows_acc,
):
    nz = t_ref.shape[-1]
    pitch = nx + 2 * PAD
    chunks = nx // 8
    wide, starts = blocks_of(nx)
    left = PAD - SENT
    odd = lax.rem(lax.axis_index("gy"), 2)
    packs[1 - odd] = ye_ref[...]
    packs[odd] = yo_ref[...]

    def packed(side, b):
        return packs[side, starts[b] : starts[b + 1]]

    for side in range(2):
        for i in range(4):
            source = ((side * (ny - 4)) + i) * pitch
            dest = (side * 4 + i + 2) * pitch
            for ref, out in ((t_ref, r_out), (lb_ref, lb_out), (fx_ref, fx), (fy_ref, fy), (dg_ref, dg), (fz_ref, fz)):
                out[dest : dest + pitch] = ref[source : source + pitch]
        for i in range(2):
            source = (side * (ny - 6) + i) * pitch
            dest = (side * 2 + i + 4) * pitch
            p_out[:, dest : dest + pitch] = pc_ref[:, source : source + pitch]
    for side in range(2):
        inner, ghost, far = (0, -1, -2) if side == 0 else (ny - 1, ny, ny + 1)
        at = lambda y, start=left, size=wide: pl.ds(edge_slot(y, ny) * pitch + start, size)
        base = pl.ds(inner * pitch + left, wide)
        face = packed(side, 2) if side == 0 else fy_ref[base]
        r_out[at(ghost)] = packed(side, 0) + face * s_ref[base]
        r_out[at(inner)] = t_ref[base] + face * packed(side, 1)
        if side == 0:
            fy[at(ghost)] = face
        fy[at(far if side == 0 else ghost)] = jnp.ones((wide, nz), F32)
        r_out[at(far, PAD, nx)] = packed(side, 4)
        fx[at(ghost)] = packed(side, 3)
        dg[at(ghost, PAD, nx)] = packed(side, 5)
        fz[at(ghost, PAD, nx)] = packed(side, 6)
        labels = packed(side, 7)
        spot = iota((wide, nz), 0) == iota((wide, nz), 1)
        for r, y in ((0, ghost), (1, far)):
            column = jnp.sum(jnp.where(spot, labels[r : r + 1], 0.0), axis=1, keepdims=True)
            lb_out[at(y)] = jnp.broadcast_to(column, (wide, nz))

    def first(i):
        base = (i + 1 + jnp.where(i >= 3, 4, 0)) * pitch
        for r in range(0, pitch, 8):
            at = base + r
            here, below, above = eight(at), eight(at - pitch), eight(at + pitch)
            value = r_out[here]
            parts = [
                ((dg[here] - SHIFT) * value - along_z(fz[here], value), lb_out[here]),
                (-fx[here] * r_out[near(at + 1)], lb_out[near(at + 1)]),
                (-fx[near(at - 1)] * r_out[near(at - 1)], lb_out[near(at - 1)]),
                (-fy[here] * r_out[above], lb_out[above]),
                (-fy[below] * r_out[below], lb_out[below]),
            ]
            for j, values in enumerate(spread(parts)):
                p_out[j, here] = values

    loop(6, first)

    def q_slot(i):
        return i + 2 + jnp.where(i >= 3, 2, 0)

    def second(i):
        for c in range(chunks):
            at = q_slot(i) * pitch + PAD + c * 8
            here, below, above = eight(at), eight(at - pitch), eight(at + pitch)
            d, z, fxp, fxm, fyp, fym = dg[here], fz[here], fx[here], fx[near(at - 1)], fy[here], fy[below]
            for j in range(ENLARGE):
                p = p_out[j, here]
                q = d * p - fxp * p_out[j, near(at + 1)] - fxm * p_out[j, near(at - 1)]
                q = q - fyp * p_out[j, above] - fym * p_out[j, below]
                q_out[j, eight(i * nx + c * 8)] = q - along_z(z, p)

    loop(6, second)

    def fields_at(ref, at):
        return [ref[j, eight(at)] for j in range(ENLARGE)]

    def own_dots(i, sums):
        base = (i + 2 + jnp.where(i >= 2, 4, 0)) * pitch + PAD
        for c in range(chunks):
            at = base + c * 8
            sums = dot_own(sums, r_out[eight(at)], lb_out[eight(at)], fields_at(p_out, at))
        return sums

    def p_dots(i, sums):
        base = (i + 2 + jnp.where(i >= 2, 4, 0)) * pitch + PAD
        for c in range(chunks):
            p = fields_at(p_out, base + c * 8)
            sums = dot_pairs(sums, p, p)
        return sums

    def q_dots(i, sums):
        base = q_slot(i) * pitch + PAD
        for c in range(chunks):
            sums = dot_pairs(sums, fields_at(p_out, base + c * 8), fields_at(q_out, i * nx + c * 8))
        return sums

    rows_acc[...] = jnp.zeros_like(rows_acc)
    span = ENLARGE * ENLARGE

    def put(slot, values):
        rows_acc[slot : slot + 1] = jnp.sum(values, axis=0, keepdims=True)

    pairs = len(PAIRS)
    begin = 0
    for which, dots, layers, count in (
        (0, own_dots, 4, pairs + ENLARGE), (1, p_dots, 4, pairs), (2, q_dots, 6, pairs),
    ):
        sums = tuple(acc_ref[begin + i] for i in range(count))
        begin += count
        sums = lax.fori_loop(0, layers, dots, sums)
        for (j, k), values in zip(PAIRS, sums):
            put(which * span + j * ENLARGE + k, values)
            if j != k:
                put(which * span + k * ENLARGE + j, values)
        for j, values in enumerate(sums[pairs:]):
            put(3 * span + j * ENLARGE + j, values)
    ones = jnp.ones((8, nz), F32)
    flat = lax.dot_general(
        ones, rows_acc[...], (((1,), (1,)), ((), ())), precision=HIGHEST, preferred_element_type=F32
    )
    half = 2 * span
    pair = jnp.where(iota((2, half), 0) == 0, flat[0:2, 0:half], flat[0:2, half : 2 * half])
    for d in range(devices):
        gram_out[d] = pair


def edge_powers(ext, pc, acc, ye, yo, ny, nx, devices):
    nz = pc.shape[-1]
    rows = 12 * (nx + 2 * PAD)
    half = 2 * ENLARGE * ENLARGE
    return pl.pallas_call(
        functools.partial(edge_kernel, ny, nx, devices),
        in_specs=vmem(11),
        out_specs=vmem(5),
        out_shape=[
            array(ENLARGE, rows, nz), array(ENLARGE, 6 * nx, nz), array(rows, nz), array(rows, nz),
            array(devices, 2, half),
        ],
        scratch_shapes=[
            pltpu.VMEM((2,) + ye.shape, F32),
            pltpu.VMEM((rows, nz), F32),
            pltpu.VMEM((rows, nz), F32),
            pltpu.VMEM((rows, nz), F32),
            pltpu.VMEM((rows, nz), F32),
            pltpu.VMEM((2 * half, nz), F32),
        ],
        compiler_params=params(),
        name="edge_powers",
    )(*ext, pc, acc, ye, yo)


def solve_columns(parts):
    nz = parts.shape[-1]
    span = ENLARGE * ENLARGE
    v = jnp.sum(parts, axis=0)
    lhs = jnp.concatenate([jnp.broadcast_to(v[0:1], (8, nz)), jnp.broadcast_to(v[1:2], (8, nz))], axis=1)
    source = iota((8, 2 * nz), 1)
    lhs = jnp.where(iota((8, 2 * nz), 0) == lax.rem(source, span) // ENLARGE, lhs, 0.0)
    k = iota((2 * nz, nz), 0)
    n = iota((2 * nz, nz), 1)
    which = k // span
    column = lax.rem(k, ENLARGE)

    def place(block, offset, scale):
        return jnp.where(jnp.logical_and(which == block, n == column + offset), scale, 0.0)

    upper = place(0, 0, 1.0) + place(3, 0, SHIFT) + place(1, 8, 1.0) + place(0, 8, SHIFT) + place(3, 16, 1.0)
    lower = place(1, 0, 1.0) + place(0, 0, SHIFT) + place(2, 8, 1.0) + place(0, 16, 1.0)
    dot = functools.partial(jnp.dot, precision=HIGHEST, preferred_element_type=F32)
    m = jnp.concatenate([dot(lhs, upper), dot(lhs, lower)], axis=0)
    row = iota(m.shape, 0)
    for i in range(2 * ENLARGE):
        pivot = m[i : i + 1] / m[i : i + 1, i : i + 1]
        m = jnp.where(row == i, pivot, m - m[:, i : i + 1] * pivot)
    return m


def update_kernel(
    parts_ref, pc_ref, qc_ref, pd_ref, qd_ref, t_ref, rd_ref, lb_ref, it_ref,
    it_out, r_out,
    table, weights, onehot, own, work, r_work, sem_out, sem_r,
):
    _, ny, nx, nz = it_ref.shape
    pitch = nx + 2 * PAD
    two = 2 * ENLARGE
    square = ENLARGE * ENLARGE
    chunks = nx // 8

    def copy_out(half, c):
        span, rows = pl.ds(half * 4, 4), pl.ds(pl.multiple_of(c * 8 * ny, 8 * ny), 8 * ny)
        return pltpu.make_async_copy(work.at[span, rows], it_out.at[span, rows], sem_out.at[half, c])

    def copy_r(c):
        rows = pl.ds(pl.multiple_of(c * 8 * ny, 8 * ny), 8 * ny)
        return pltpu.make_async_copy(r_work.at[rows], r_out.at[rows], sem_r.at[c])

    def mark(y):
        lane = iota((nx, nz), 1)
        labels = lb_ref[pl.ds(pl.multiple_of(y * pitch + PAD, 8), nx)]
        chosen = jnp.logical_and(lane < 3 * ENLARGE, lax.rem(lane, ENLARGE).astype(F32) == labels)
        onehot[pl.ds(pl.multiple_of(y * nx, nx), nx)] = jnp.where(chosen, 1.0, 0.0).astype(jnp.bfloat16)

    loop(ny, mark)

    m = solve_columns(parts_ref[...])
    columns = [jnp.broadcast_to(m[:, two + j : two + j + 1], (two, nz)) for j in range(ENLARGE)]
    carried = columns[0]
    for column in columns[1:]:
        carried = carried + column
    weights[...] = jnp.zeros_like(weights)
    for j, column in enumerate(columns + [carried]):
        for k in range(two):
            if j < ENLARGE and k < ENLARGE:
                continue
            slot = j * ENLARGE + k - ENLARGE if j < ENLARGE else square + k
            table[slot] = jnp.broadcast_to(column[k : k + 1], (8, nz))
        mine = column[0:ENLARGE]
        high = mine.astype(jnp.bfloat16).astype(F32)
        mid = (mine - high).astype(jnp.bfloat16).astype(F32)
        at = slice(j * nz, (j + 1) * nz)
        weights[0:8, at] = high
        weights[8:16, at] = mid
        weights[16:24, at] = mine - high - mid
    spread_weights = weights[...].astype(jnp.bfloat16)

    def coefficients(n):
        here = pl.ds(pl.multiple_of(n * 128, 128), 128)
        own[here] = jnp.dot(onehot[here], spread_weights, preferred_element_type=F32)

    loop(ny * nx // 128, coefficients, unroll=2)

    def spots(c, visit):
        def clean(i):
            x = PAD + c * 8
            visit(i + 3, pc_ref, (i + 1) * pitch + x, qc_ref, i * nx + c * 8, t_ref, (i + 3) * pitch + x)

        loop(ny - 6, clean, unroll=2)

        def edge(i):
            at = (i + 2 + jnp.where(i >= 3, 2, 0)) * pitch + PAD + c * 8
            y = i + jnp.where(i >= 3, ny - 6, 0)
            visit(y, pd_ref, at, qd_ref, i * nx + c * 8, rd_ref, at)

        loop(6, edge, unroll=2)

    def place(c, y):
        return pl.ds(c * 8 * ny + y, 8, stride=ny)

    def updates(half):
        js = range(half * 4, half * 4 + 4)
        scales = [[table[j * ENLARGE + k] for k in range(ENLARGE)] for j in js]

        def block(c):
            def visit(y, p_ref, p_at, q_ref, q_at, r_ref, r_at):
                r = r_ref[eight(r_at)]
                at = eight(y * nx + c * 8)
                totals = [it_ref[j, y, eight(c * 8)] + own[at, j * nz : (j + 1) * nz] * r for j in js]
                for k in range(ENLARGE):
                    p = p_ref[k, eight(p_at)]
                    totals = [t + scale[k] * p for t, scale in zip(totals, scales)]
                for j, t in zip(js, totals):
                    work[j, place(c, y), :] = t

            spots(c, visit)
            copy_out(half, c).start()

        loop(chunks, block)

    def residuals():
        scales = [table[square + k] for k in range(two)]

        def block(c):
            def visit(y, p_ref, p_at, q_ref, q_at, r_ref, r_at):
                r = r_ref[eight(r_at)]
                total = r - (SHIFT * own[eight(y * nx + c * 8), ENLARGE * nz : (ENLARGE + 1) * nz]) * r
                for k in range(ENLARGE):
                    total = total - scales[k] * p_ref[k, eight(p_at)]
                    total = total - scales[ENLARGE + k] * q_ref[k, eight(q_at)]
                r_work[place(c, y), :] = total

            spots(c, visit)
            copy_r(c).start()

        loop(chunks, block)

    updates(0)
    updates(1)
    residuals()
    for half in range(2):
        loop(chunks, lambda c, half=half: copy_out(half, c).wait())
    loop(chunks, lambda c: copy_r(c).wait())


def update(parts, pc, qc, pd, qd, t, rd, labels, held):
    _, ny, nx, nz = held.shape
    rows = nx * ny
    return pl.pallas_call(
        update_kernel,
        in_specs=vmem(9),
        out_specs=hbm(2),
        out_shape=[array(ENLARGE, rows, nz), array(rows, nz)],
        scratch_shapes=[
            pltpu.VMEM((ENLARGE * ENLARGE + 2 * ENLARGE, 8, nz), F32),
            pltpu.VMEM((nz, (ENLARGE + 1) * nz), F32),
            pltpu.VMEM((rows, nz), jnp.bfloat16),
            pltpu.VMEM((rows, (ENLARGE + 1) * nz), F32),
            pltpu.VMEM((ENLARGE, rows, nz), F32),
            pltpu.VMEM((rows, nz), F32),
            pltpu.SemaphoreType.DMA((2, nx // 8)),
            pltpu.SemaphoreType.DMA((nx // 8,)),
        ],
        compiler_params=params(),
        name="update",
    )(parts, pc, qc, pd, qd, t, rd, labels, held)


def shards(gx, gy, source, diagonal, face_x, face_y, face_z, iterates, labels):
    _, nx, ny, nz = iterates.shape
    arrays = [pinned(a) for a in (iterates, source, diagonal, face_x, face_y, face_z, labels.T)]
    xe, xo = x_edges(arrays)
    xo = lax.ppermute(xo, "gx", odd_pairs(gx))
    xe = lax.ppermute(xe, "gx", even_pairs(gx))
    *fields, held = load(arrays)
    *ext, ye = partial_residual(fields, xe, xo, gx, gy)
    ye = lax.ppermute(ye, "gy", even_pairs(gy))
    pc, yo = clean_first(ext, ny, nx)
    yo = lax.ppermute(yo, "gy", odd_pairs(gy))
    qc, acc = clean_second(ext, pc, ny, nx)
    pd, qd, rd, _, gram = edge_powers(ext, pc, acc, ye, yo, ny, nx, gx * gy)
    parts = lax.all_to_all(gram, ("gx", "gy"), 0, 0, tiled=True)
    new_iterates, new_residual = update(parts, pc, qc, pd, qd, ext[0], rd, ext[-1], held)
    return new_iterates.reshape(iterates.shape), new_residual.reshape(source.shape)


def solution(mesh):
    placed = (
        P("gx", "gy", None),
        P("gx", "gy", None),
        P("gx", "gy", None),
        P("gx", "gy", None),
        P("gx", "gy", None),
        P(None, "gx", "gy", None),
        P("gx", "gy"),
    )
    return jax.shard_map(
        functools.partial(shards, mesh.shape["gx"], mesh.shape["gy"]),
        mesh=mesh,
        in_specs=placed,
        out_specs=(P(None, "gx", "gy", None), P("gx", "gy", None)),
        check_vma=False,
    )
```

```python
import functools

import jax
import jax.numpy as jnp
from jax import lax
from jax.experimental import pallas as pl
from jax.experimental.pallas import tpu as pltpu
from jax.sharding import PartitionSpec as P

ENLARGE = 8
SHIFT = 6.5
F32 = jnp.float32
HIGHEST = lax.Precision.HIGHEST
PAIRS = [(j, k) for j in range(ENLARGE) for k in range(j, ENLARGE)]
VMEM_LIMIT = 20 * 1024 * 1024
PAD = 8
SENT = 2


def iota(shape, dim):
    return lax.broadcasted_iota(jnp.int32, shape, dim)


def even_pairs(count):
    return [(i, i ^ 1) for i in range(count) if (i ^ 1) < count]


def odd_pairs(count):
    return [(i, ((i - 1) ^ 1) + 1) for i in range(1, count) if ((i - 1) ^ 1) + 1 < count]


def vmem(count):
    return [pl.BlockSpec(memory_space=pltpu.VMEM)] * count


def hbm(count):
    return [pl.BlockSpec(memory_space=pltpu.HBM)] * count


def pinned(value):
    return pltpu.with_memory_space_constraint(value, pltpu.HBM)


def array(*shape):
    return jax.ShapeDtypeStruct(shape, F32)


def params():
    return pltpu.CompilerParams(vmem_limit_bytes=VMEM_LIMIT)


def aligned(value):
    return value if isinstance(value, int) else pl.multiple_of(value, 8)


def eight(start):
    return pl.ds(aligned(start), 8)


def near(start):
    return pl.ds(start, 8)


def loop(count, body, **kw):
    def wrapped(i, carry):
        body(i)
        return carry

    lax.fori_loop(0, count, wrapped, 0, **kw)


def edges_kernel(
    it_hbm, src_hbm, dg_hbm, fx_hbm, fy_hbm, fz_hbm, label_hbm,
    even_out, odd_out,
    work, fields, labels, sem_it, sem_field, sem_label,
):
    _, nx, ny, nz = it_hbm.shape
    sources = (src_hbm, dg_hbm, fx_hbm, fy_hbm, fz_hbm)
    lines = [(x, x) for x in range(3)] + [(nx - 3 + x, 13 + x) for x in range(3)]
    copies = [pltpu.make_async_copy(label_hbm, labels, sem_label)]
    for n, (x, row) in enumerate(lines):
        copies.append(pltpu.make_async_copy(it_hbm.at[:, x], work.at[:, :, row], sem_it.at[n]))
        for f, ref in enumerate(sources):
            copies.append(pltpu.make_async_copy(ref.at[x], fields.at[f, :, row], sem_field.at[f, n]))
    for copy in copies:
        copy.start()
    copies[0].wait()
    spread_rows = iota((16, nx), 0)
    spot = jnp.where(spread_rows < 8, spread_rows, spread_rows + nx - 16) == iota((16, nx), 1)
    ones = jnp.ones((nx, nz), jnp.bfloat16)
    marks = labels[...].astype(F32)
    for copy in copies[1:]:
        copy.wait()
    even = lax.rem(lax.axis_index("gx"), 2) == 0
    sub = iota((8, nz), 0)
    roll = lambda v, n: pltpu.roll(v, n, 0)
    for y in range(ny):
        row = jnp.where(spot, marks[y : y + 1], 0.0).astype(jnp.bfloat16)
        lb = jnp.dot(row, ones, preferred_element_type=F32)
        total = work[0, y]
        for j in range(1, ENLARGE):
            total = total + work[j, y]
        src, dg, fx, fy, fz = [fields[f, y] for f in range(5)]

        def first(at, is_low):
            if is_low:
                return jnp.where(sub < 3, total[at], jnp.where(sub >= 6, roll(lb[at], 6), roll(fx[at], 3)))
            return jnp.where(sub >= 5, total[at], jnp.where(sub < 2, roll(lb[at], 2), roll(fx[at], 5)))

        def second(at, start):
            values = src[at]
            for n, field in enumerate((dg, fy, fz)):
                begin = (start + 2 * n + 2) % 8
                inside = jnp.logical_or(sub == begin, sub == begin + 1)
                values = jnp.where(inside, roll(field[at], 2 * n + 2), values)
            return values

        lo, hi = slice(0, 8), slice(8, 16)
        for part, high, low in ((0, first(hi, False), first(lo, True)), (1, second(hi, 6), second(lo, 0))):
            even_out[part, y] = jnp.where(even, high, low)
            odd_out[part, y] = jnp.where(even, low, high)


def x_edges(arrays):
    _, nx, ny, nz = arrays[0].shape
    edge = array(2, ny, 8, nz)
    return pl.pallas_call(
        edges_kernel,
        in_specs=hbm(7),
        out_specs=vmem(2),
        out_shape=[edge] * 2,
        scratch_shapes=[
            pltpu.VMEM((ENLARGE, ny, 16, nz), F32),
            pltpu.VMEM((5, ny, 16, nz), F32),
            pltpu.VMEM((ny, nx), jnp.int32),
            pltpu.SemaphoreType.DMA((6,)),
            pltpu.SemaphoreType.DMA((5, 6)),
            pltpu.SemaphoreType.DMA,
        ],
        compiler_params=params(),
        name="x_edges",
    )(*arrays)


def load_kernel(
    it_hbm, src_hbm, dg_hbm, fx_hbm, fy_hbm, fz_hbm, label_hbm,
    s_out, src_out, dg_out, fx_out, fy_out, fz_out, lb_out, work,
    label_ref, sem_it, sem_field, sem_label,
):
    ny, nx, nz = s_out.shape
    pairs = list(zip((src_hbm, dg_hbm, fx_hbm, fy_hbm, fz_hbm), (src_out, dg_out, fx_out, fy_out, fz_out)))
    label_copy = pltpu.make_async_copy(label_hbm, label_ref, sem_label)

    def copy_it(y):
        return pltpu.make_async_copy(it_hbm.at[:, :, y], work.at[:, y], sem_it.at[y])

    def copy_field(f, y):
        return pltpu.make_async_copy(pairs[f][0].at[:, y], pairs[f][1].at[y], sem_field.at[f, y])

    def start(y):
        copy_it(y).start()
        for f in range(len(pairs)):
            copy_field(f, y).start()

    label_copy.start()
    loop(ny, start)
    label_copy.wait()

    spot = iota((nx, nx), 0) == iota((nx, nx), 1)
    ones = jnp.ones((nx, nz), jnp.bfloat16)
    labels = label_ref[...].astype(F32)
    for y in range(ny):
        row = jnp.where(spot, labels[y : y + 1], 0.0).astype(jnp.bfloat16)
        lb_out[y] = jnp.dot(row, ones, preferred_element_type=F32)

    def add(y):
        copy_it(y).wait()
        for r in range(0, nx, 8):
            total = work[0, y, r : r + 8]
            for j in range(1, ENLARGE):
                total = total + work[j, y, r : r + 8]
            s_out[y, r : r + 8] = total

    loop(ny, add)

    def finish(y):
        for f in range(len(pairs)):
            copy_field(f, y).wait()

    loop(ny, finish)


def load(arrays):
    _, nx, ny, nz = arrays[0].shape
    field = array(ny, nx, nz)
    return pl.pallas_call(
        load_kernel,
        in_specs=hbm(7),
        out_specs=vmem(8),
        out_shape=[field] * 7 + [array(ENLARGE, ny, nx, nz)],
        scratch_shapes=[
            pltpu.VMEM((ny, nx), jnp.int32),
            pltpu.SemaphoreType.DMA((ny,)),
            pltpu.SemaphoreType.DMA((5, ny)),
            pltpu.SemaphoreType.DMA,
        ],
        compiler_params=params(),
        cost_estimate=pl.CostEstimate(flops=2_000_000, bytes_accessed=16_000_000, transcendentals=0),
        name="load",
    )(*arrays)


def blocks_of(nx):
    wide = nx + PAD
    sizes = (wide, wide, wide, wide, nx, nx, nx, 8)
    starts = [sum(sizes[:i]) for i in range(len(sizes) + 1)]
    return wide, starts


def pack_y_edge(ny, nx, dest, is_high, t, s, fy, fx, dg, fz, lb):
    pitch = nx + 2 * PAD
    nz = t.shape[-1]
    wide, starts = blocks_of(nx)
    first = jnp.where(is_high, ny - 1, 0) * pitch
    second = jnp.where(is_high, ny - 2, 1) * pitch
    between = jnp.where(is_high, ny - 2, 0) * pitch

    def line(ref, base):
        return ref[pl.ds(base + (PAD - SENT), wide)]

    def inner(ref, base):
        return ref[pl.ds(pl.multiple_of(base + PAD, 8), nx)]

    parts = (
        line(t, first),
        line(s, first),
        line(fy, first),
        line(fx, first),
        inner(fy, between) * inner(t, second),
        inner(dg, first),
        inner(fz, first),
    )
    for b, values in enumerate(parts):
        dest[starts[b] : starts[b + 1]] = values
    spot = iota((wide, nz), 0) == iota((wide, nz), 1)
    one = jnp.sum(jnp.where(spot, line(lb, first), 0.0), axis=0, keepdims=True)
    two = jnp.sum(jnp.where(spot, line(lb, second), 0.0), axis=0, keepdims=True)
    which = iota((8, nz), 0)
    dest[starts[7] : starts[8]] = jnp.where(which == 0, one, jnp.where(which == 1, two, 0.0))


def partial_kernel(
    gx, gy,
    s_in, src_in, dg_in, fx_in, fy_in, fz_in, lb_in, xe_ref, xo_ref,
    t_out, s_out, fx_out, fy_out, dg_out, fz_out, lb_out, ye_ref,
    src_ext,
):
    ny, nx, nz = s_in.shape
    pitch = nx + 2 * PAD
    lane = iota((8, nz), 1)
    even_x = lax.rem(lax.axis_index("gx"), 2) == 0
    last_x = lax.axis_index("gx") == gx - 1
    last_y = lax.axis_index("gy") == gy - 1
    last_row = jnp.logical_and(iota((8, nz), 0) == 7, last_x)

    def fill(y):
        top = jnp.logical_and(last_y, y == ny - 1)
        fy_of = lambda v: jnp.where(top, 0.0, v)
        fz_of = lambda v: jnp.where(lane == nz - 1, 0.0, v)
        base = y * pitch
        roll = lambda v, n: pltpu.roll(v, n, 0)
        for at, is_low in ((0, True), (PAD + nx, False)):
            one, two = [
                jnp.where(even_x == is_low, xo_ref[part, y], xe_ref[part, y]) for part in range(2)
            ]
            here = eight(base + at)
            s_out[here] = one
            fx_out[here] = roll(one, 3 if is_low else 5)
            lb_out[here] = roll(one, 6 if is_low else 2)
            src_ext[here] = two
            dg_out[here] = roll(two, 6)
            fy_out[here] = fy_of(roll(two, 4))
            fz_out[here] = fz_of(roll(two, 2))
        for r in range(0, nx, 8):
            here = eight(base + PAD + r)
            span = slice(r, r + 8)
            s_out[here] = s_in[y, span]
            face = fx_in[y, span]
            fx_out[here] = jnp.where(last_row, 0.0, face) if r == nx - 8 else face
            lb_out[here] = lb_in[y, span]
            src_ext[here] = src_in[y, span]
            dg_out[here] = dg_in[y, span]
            fy_out[here] = fy_of(fy_in[y, span])
            fz_out[here] = fz_of(fz_in[y, span])

    loop(ny, fill)

    def layer(y, down=True, up=True):
        base = y * pitch
        for r in range(0, pitch, 8):
            at = base + r
            here = eight(at)
            s, fx, fz = s_out[here], fx_out[here], fz_out[here]
            if r == 0:
                sm, fxm = pltpu.roll(s, 1, 0), pltpu.roll(fx, 1, 0)
            else:
                sm, fxm = s_out[near(at - 1)], fx_out[near(at - 1)]
            sp = pltpu.roll(s, 7, 0) if r == pitch - 8 else s_out[near(at + 1)]
            total = dg_out[here] * s - fx * sp - fxm * sm
            if up:
                total = total - fy_out[here] * s_out[eight(at + pitch)]
            if down:
                total = total - fy_out[eight(at - pitch)] * s_out[eight(at - pitch)]
            total = total - fz * pltpu.roll(s, nz - 1, 1) - pltpu.roll(fz * s, 1, 1)
            t_out[here] = src_ext[here] - total

    layer(0, down=False)
    layer(ny - 1, up=False)
    loop(ny - 2, lambda i: layer(i + 1))

    even_y = lax.rem(lax.axis_index("gy"), 2) == 0
    pack_y_edge(ny, nx, ye_ref, even_y, t_out, s_out, fy_out, fx_out, dg_out, fz_out, lb_out)


def partial_residual(fields, xe, xo, gx, gy):
    ny, nx, nz = fields[0].shape
    rows = ny * (nx + 2 * PAD)
    ext = array(rows, nz)
    pack = array(blocks_of(nx)[1][-1], nz)
    return pl.pallas_call(
        functools.partial(partial_kernel, gx, gy),
        in_specs=vmem(9),
        out_specs=vmem(8),
        out_shape=[ext] * 7 + [pack],
        scratch_shapes=[pltpu.VMEM((rows, nz), F32)],
        compiler_params=params(),
        name="partial_residual",
    )(*fields, xe, xo)


def spread(parts):
    fields = []
    for j in range(ENLARGE):
        total = None
        for values, label in parts:
            term = jnp.where(label == float(j), values, 0.0)
            total = term if total is None else total + term
        fields.append(total)
    return fields


def along_z(fz, values):
    nz = values.shape[-1]
    return fz * pltpu.roll(values, nz - 1, 1) + pltpu.roll(fz * values, 1, 1)


def edge_near(ref, at, shift, last):
    if last == shift:
        return pltpu.roll(ref[eight(at)], 1 if shift < 0 else 7, 0)
    return ref[near(at + shift)]


def zeros_like_pairs(nz, count):
    return tuple(jnp.zeros((8, nz), F32) for _ in range(count))


def dot_own(sums, r, label, p):
    b = [jnp.where(label == float(j), r, 0.0) for j in range(ENLARGE)]
    n = len(PAIRS)
    own = tuple(t + v * v for t, v in zip(sums[n:], b))
    return tuple(t + b[j] * p[k] for t, (j, k) in zip(sums, PAIRS)) + own


def dot_pairs(sums, p, q):
    return tuple(t + p[j] * q[k] for t, (j, k) in zip(sums, PAIRS))


def clean_first_kernel(
    ny, nx,
    t_ref, s_ref, fx_ref, fy_ref, dg_ref, fz_ref, lb_ref,
    p_out, yo_ref,
):
    pitch = nx + 2 * PAD

    def first(i):
        layer = (i + 2) * pitch
        for r in range(0, pitch, 8):
            at = layer + r
            last = -1 if r == 0 else (1 if r == pitch - 8 else 0)
            here = eight(at)
            value = t_ref[here]
            below, above = eight(at - pitch), eight(at + pitch)
            parts = [
                ((dg_ref[here] - SHIFT) * value - along_z(fz_ref[here], value), lb_ref[here]),
                (-fx_ref[here] * edge_near(t_ref, at, 1, last), edge_near(lb_ref, at, 1, last)),
                (-edge_near(fx_ref, at, -1, last) * edge_near(t_ref, at, -1, last), edge_near(lb_ref, at, -1, last)),
                (-fy_ref[here] * t_ref[above], lb_ref[above]),
                (-fy_ref[below] * t_ref[below], lb_ref[below]),
            ]
            for j, values in enumerate(spread(parts)):
                p_out[j, eight(i * pitch + r)] = values

    loop(ny - 4, first)
    odd_y = lax.rem(lax.axis_index("gy"), 2) == 1
    pack_y_edge(ny, nx, yo_ref, odd_y, t_ref, s_ref, fy_ref, fx_ref, dg_ref, fz_ref, lb_ref)


def clean_second_kernel(
    ny, nx,
    t_ref, fx_ref, fy_ref, dg_ref, fz_ref, lb_ref, p_out,
    q_out, acc_out,
):
    nz = t_ref.shape[-1]
    pitch = nx + 2 * PAD
    chunks = nx // 8

    def second(i):
        for c in range(chunks):
            at = (i + 3) * pitch + PAD + c * 8
            own = (i + 1) * pitch + PAD + c * 8
            here = eight(at)
            dg, fz, fxp, fxm = dg_ref[here], fz_ref[here], fx_ref[here], fx_ref[near(at - 1)]
            fyp, fym = fy_ref[here], fy_ref[eight(at - pitch)]
            for j in range(ENLARGE):
                p = p_out[j, eight(own)]
                q = dg * p - fxp * p_out[j, near(own + 1)] - fxm * p_out[j, near(own - 1)]
                q = q - fyp * p_out[j, eight(own + pitch)] - fym * p_out[j, eight(own - pitch)]
                q_out[j, eight(i * nx + c * 8)] = q - along_z(fz, p)

    loop(ny - 6, second)

    def fields_at(ref, at):
        return [ref[j, eight(at)] for j in range(ENLARGE)]

    def own_dots(i, sums):
        for c in range(chunks):
            row = i * pitch + PAD + c * 8
            shifted = eight(row + 2 * pitch)
            sums = dot_own(sums, t_ref[shifted], lb_ref[shifted], fields_at(p_out, row))
        return sums

    def p_dots(i, sums):
        for c in range(chunks):
            p = fields_at(p_out, i * pitch + PAD + c * 8)
            sums = dot_pairs(sums, p, p)
        return sums

    def q_dots(i, sums):
        for c in range(chunks):
            p = fields_at(p_out, (i + 1) * pitch + PAD + c * 8)
            sums = dot_pairs(sums, p, fields_at(q_out, i * nx + c * 8))
        return sums

    slot = 0
    for dots, layers, count in (
        (own_dots, ny - 4, len(PAIRS) + ENLARGE), (p_dots, ny - 4, len(PAIRS)), (q_dots, ny - 6, len(PAIRS)),
    ):
        sums = lax.fori_loop(0, layers, dots, zeros_like_pairs(nz, count))
        for values in sums:
            acc_out[slot] = values
            slot += 1


def clean_first(ext, ny, nx):
    nz = ext[0].shape[-1]
    return pl.pallas_call(
        functools.partial(clean_first_kernel, ny, nx),
        in_specs=vmem(7),
        out_specs=vmem(2),
        out_shape=[array(ENLARGE, (ny - 4) * (nx + 2 * PAD), nz), array(blocks_of(nx)[1][-1], nz)],
        compiler_params=params(),
        cost_estimate=pl.CostEstimate(flops=20_000_000, bytes_accessed=8_000_000, transcendentals=0),
        name="clean_first",
    )(*ext)


def clean_second(ext, pc, ny, nx):
    t, _, fx, fy, dg, fz, lb = ext
    nz = t.shape[-1]
    return pl.pallas_call(
        functools.partial(clean_second_kernel, ny, nx),
        in_specs=vmem(7),
        out_specs=vmem(2),
        out_shape=[array(ENLARGE, (ny - 6) * nx, nz), array(3 * len(PAIRS) + ENLARGE, 8, nz)],
        compiler_params=params(),
        cost_estimate=pl.CostEstimate(flops=40_000_000, bytes_accessed=12_000_000, transcendentals=0),
        name="clean_second",
    )(t, fx, fy, dg, fz, lb, pc)


def edge_slot(y, ny):
    return y + 2 if y < 4 else y - (ny - 4) + 6


def edge_kernel(
    ny, nx, devices,
    t_ref, s_ref, fx_ref, fy_ref, dg_ref, fz_ref, lb_ref, pc_ref, acc_ref, ye_ref, yo_ref,
    p_out, q_out, r_out, lb_out, gram_out,
    packs, fx, fy, dg, fz, rows_acc,
):
    nz = t_ref.shape[-1]
    pitch = nx + 2 * PAD
    chunks = nx // 8
    wide, starts = blocks_of(nx)
    left = PAD - SENT
    odd = lax.rem(lax.axis_index("gy"), 2)
    packs[1 - odd] = ye_ref[...]
    packs[odd] = yo_ref[...]

    def packed(side, b):
        return packs[side, starts[b] : starts[b + 1]]

    for side in range(2):
        for i in range(4):
            source = ((side * (ny - 4)) + i) * pitch
            dest = (side * 4 + i + 2) * pitch
            for ref, out in ((t_ref, r_out), (lb_ref, lb_out), (fx_ref, fx), (fy_ref, fy), (dg_ref, dg), (fz_ref, fz)):
                out[dest : dest + pitch] = ref[source : source + pitch]
        for i in range(2):
            source = (side * (ny - 6) + i) * pitch
            dest = (side * 2 + i + 4) * pitch
            p_out[:, dest : dest + pitch] = pc_ref[:, source : source + pitch]
    for side in range(2):
        inner, ghost, far = (0, -1, -2) if side == 0 else (ny - 1, ny, ny + 1)
        at = lambda y, start=left, size=wide: pl.ds(edge_slot(y, ny) * pitch + start, size)
        base = pl.ds(inner * pitch + left, wide)
        face = packed(side, 2) if side == 0 else fy_ref[base]
        r_out[at(ghost)] = packed(side, 0) + face * s_ref[base]
        r_out[at(inner)] = t_ref[base] + face * packed(side, 1)
        if side == 0:
            fy[at(ghost)] = face
        fy[at(far if side == 0 else ghost)] = jnp.ones((wide, nz), F32)
        r_out[at(far, PAD, nx)] = packed(side, 4)
        fx[at(ghost)] = packed(side, 3)
        dg[at(ghost, PAD, nx)] = packed(side, 5)
        fz[at(ghost, PAD, nx)] = packed(side, 6)
        labels = packed(side, 7)
        spot = iota((wide, nz), 0) == iota((wide, nz), 1)
        for r, y in ((0, ghost), (1, far)):
            column = jnp.sum(jnp.where(spot, labels[r : r + 1], 0.0), axis=1, keepdims=True)
            lb_out[at(y)] = jnp.broadcast_to(column, (wide, nz))

    def first(i):
        base = (i + 1 + jnp.where(i >= 3, 4, 0)) * pitch
        for r in range(0, pitch, 8):
            at = base + r
            here, below, above = eight(at), eight(at - pitch), eight(at + pitch)
            value = r_out[here]
            parts = [
                ((dg[here] - SHIFT) * value - along_z(fz[here], value), lb_out[here]),
                (-fx[here] * r_out[near(at + 1)], lb_out[near(at + 1)]),
                (-fx[near(at - 1)] * r_out[near(at - 1)], lb_out[near(at - 1)]),
                (-fy[here] * r_out[above], lb_out[above]),
                (-fy[below] * r_out[below], lb_out[below]),
            ]
            for j, values in enumerate(spread(parts)):
                p_out[j, here] = values

    loop(6, first)

    def q_slot(i):
        return i + 2 + jnp.where(i >= 3, 2, 0)

    def second(i):
        for c in range(chunks):
            at = q_slot(i) * pitch + PAD + c * 8
            here, below, above = eight(at), eight(at - pitch), eight(at + pitch)
            d, z, fxp, fxm, fyp, fym = dg[here], fz[here], fx[here], fx[near(at - 1)], fy[here], fy[below]
            for j in range(ENLARGE):
                p = p_out[j, here]
                q = d * p - fxp * p_out[j, near(at + 1)] - fxm * p_out[j, near(at - 1)]
                q = q - fyp * p_out[j, above] - fym * p_out[j, below]
                q_out[j, eight(i * nx + c * 8)] = q - along_z(z, p)

    loop(6, second)

    def fields_at(ref, at):
        return [ref[j, eight(at)] for j in range(ENLARGE)]

    def own_dots(i, sums):
        base = (i + 2 + jnp.where(i >= 2, 4, 0)) * pitch + PAD
        for c in range(chunks):
            at = base + c * 8
            sums = dot_own(sums, r_out[eight(at)], lb_out[eight(at)], fields_at(p_out, at))
        return sums

    def p_dots(i, sums):
        base = (i + 2 + jnp.where(i >= 2, 4, 0)) * pitch + PAD
        for c in range(chunks):
            p = fields_at(p_out, base + c * 8)
            sums = dot_pairs(sums, p, p)
        return sums

    def q_dots(i, sums):
        base = q_slot(i) * pitch + PAD
        for c in range(chunks):
            sums = dot_pairs(sums, fields_at(p_out, base + c * 8), fields_at(q_out, i * nx + c * 8))
        return sums

    rows_acc[...] = jnp.zeros_like(rows_acc)
    span = ENLARGE * ENLARGE

    def put(slot, values):
        rows_acc[slot : slot + 1] = jnp.sum(values, axis=0, keepdims=True)

    pairs = len(PAIRS)
    begin = 0
    for which, dots, layers, count in (
        (0, own_dots, 4, pairs + ENLARGE), (1, p_dots, 4, pairs), (2, q_dots, 6, pairs),
    ):
        sums = tuple(acc_ref[begin + i] for i in range(count))
        begin += count
        sums = lax.fori_loop(0, layers, dots, sums)
        for (j, k), values in zip(PAIRS, sums):
            put(which * span + j * ENLARGE + k, values)
            if j != k:
                put(which * span + k * ENLARGE + j, values)
        for j, values in enumerate(sums[pairs:]):
            put(3 * span + j * ENLARGE + j, values)
    ones = jnp.ones((8, nz), F32)
    flat = lax.dot_general(
        ones, rows_acc[...], (((1,), (1,)), ((), ())), precision=HIGHEST, preferred_element_type=F32
    )
    half = 2 * span
    pair = jnp.where(iota((2, half), 0) == 0, flat[0:2, 0:half], flat[0:2, half : 2 * half])
    for d in range(devices):
        gram_out[d] = pair


def edge_powers(ext, pc, acc, ye, yo, ny, nx, devices):
    nz = pc.shape[-1]
    rows = 12 * (nx + 2 * PAD)
    half = 2 * ENLARGE * ENLARGE
    return pl.pallas_call(
        functools.partial(edge_kernel, ny, nx, devices),
        in_specs=vmem(11),
        out_specs=vmem(5),
        out_shape=[
            array(ENLARGE, rows, nz), array(ENLARGE, 6 * nx, nz), array(rows, nz), array(rows, nz),
            array(devices, 2, half),
        ],
        scratch_shapes=[
            pltpu.VMEM((2,) + ye.shape, F32),
            pltpu.VMEM((rows, nz), F32),
            pltpu.VMEM((rows, nz), F32),
            pltpu.VMEM((rows, nz), F32),
            pltpu.VMEM((rows, nz), F32),
            pltpu.VMEM((2 * half, nz), F32),
        ],
        compiler_params=params(),
        name="edge_powers",
    )(*ext, pc, acc, ye, yo)


def solve_columns(parts):
    nz = parts.shape[-1]
    span = ENLARGE * ENLARGE
    v = jnp.sum(parts, axis=0)
    lhs = jnp.concatenate([jnp.broadcast_to(v[0:1], (8, nz)), jnp.broadcast_to(v[1:2], (8, nz))], axis=1)
    source = iota((8, 2 * nz), 1)
    lhs = jnp.where(iota((8, 2 * nz), 0) == lax.rem(source, span) // ENLARGE, lhs, 0.0)
    k = iota((2 * nz, nz), 0)
    n = iota((2 * nz, nz), 1)
    which = k // span
    column = lax.rem(k, ENLARGE)

    def place(block, offset, scale):
        return jnp.where(jnp.logical_and(which == block, n == column + offset), scale, 0.0)

    upper = place(0, 0, 1.0) + place(3, 0, SHIFT) + place(1, 8, 1.0) + place(0, 8, SHIFT) + place(3, 16, 1.0)
    lower = place(1, 0, 1.0) + place(0, 0, SHIFT) + place(2, 8, 1.0) + place(0, 16, 1.0)
    dot = functools.partial(jnp.dot, precision=HIGHEST, preferred_element_type=F32)
    m = jnp.concatenate([dot(lhs, upper), dot(lhs, lower)], axis=0)
    row = iota(m.shape, 0)
    for i in range(2 * ENLARGE):
        column = jnp.broadcast_to(m[:, i : i + 1], m.shape)
        pivot = m[i : i + 1] / column[i : i + 1]
        m = jnp.where(row == i, pivot, m - column * pivot)
    return m


def update_kernel(
    parts_ref, pc_ref, qc_ref, pd_ref, qd_ref, t_ref, rd_ref, lb_ref, it_ref,
    it_out, r_out,
    table, weights, onehot, own, work, r_work, sem_out, sem_r,
):
    _, ny, nx, nz = it_ref.shape
    pitch = nx + 2 * PAD
    two = 2 * ENLARGE
    square = ENLARGE * ENLARGE
    chunks = nx // 8

    def copy_out(half, c):
        span, rows = pl.ds(half * 4, 4), pl.ds(pl.multiple_of(c * 8 * ny, 8 * ny), 8 * ny)
        return pltpu.make_async_copy(work.at[span, rows], it_out.at[span, rows], sem_out.at[half, c])

    def copy_r(c):
        rows = pl.ds(pl.multiple_of(c * 8 * ny, 8 * ny), 8 * ny)
        return pltpu.make_async_copy(r_work.at[rows], r_out.at[rows], sem_r.at[c])

    def mark(y):
        lane = iota((nx, nz), 1)
        labels = lb_ref[pl.ds(pl.multiple_of(y * pitch + PAD, 8), nx)]
        chosen = jnp.logical_and(lane < 3 * ENLARGE, lax.rem(lane, ENLARGE).astype(F32) == labels)
        onehot[pl.ds(pl.multiple_of(y * nx, nx), nx)] = jnp.where(chosen, 1.0, 0.0).astype(jnp.bfloat16)

    loop(ny, mark)

    m = solve_columns(parts_ref[...])
    columns = [jnp.broadcast_to(m[:, two + j : two + j + 1], (two, nz)) for j in range(ENLARGE)]
    carried = columns[0]
    for column in columns[1:]:
        carried = carried + column
    weights[...] = jnp.zeros_like(weights)
    for j, column in enumerate(columns + [carried]):
        for k in range(two):
            if j < ENLARGE and k < ENLARGE:
                continue
            slot = j * ENLARGE + k - ENLARGE if j < ENLARGE else square + k
            table[slot] = jnp.broadcast_to(column[k : k + 1], (8, nz))
        mine = column[0:ENLARGE]
        high = mine.astype(jnp.bfloat16).astype(F32)
        mid = (mine - high).astype(jnp.bfloat16).astype(F32)
        at = slice(j * nz, (j + 1) * nz)
        weights[0:8, at] = high
        weights[8:16, at] = mid
        weights[16:24, at] = mine - high - mid
    spread_weights = weights[...].astype(jnp.bfloat16)

    def coefficients(n):
        here = pl.ds(pl.multiple_of(n * 128, 128), 128)
        own[here] = jnp.dot(onehot[here], spread_weights, preferred_element_type=F32)

    loop(ny * nx // 128, coefficients, unroll=2)

    def spots(c, visit):
        x = PAD + c * 8
        for i in range(ny - 6):
            visit(i + 3, pc_ref, (i + 1) * pitch + x, qc_ref, i * nx + c * 8, t_ref, (i + 3) * pitch + x)
        for i in range(6):
            at = (i + 2 + (2 if i >= 3 else 0)) * pitch + x
            y = i + (ny - 6 if i >= 3 else 0)
            visit(y, pd_ref, at, qd_ref, i * nx + c * 8, rd_ref, at)

    def place(c, y):
        return pl.ds(c * 8 * ny + y, 8, stride=ny)

    def updates(half):
        js = range(half * 4, half * 4 + 4)
        scales = [[table[j * ENLARGE + k] for k in range(ENLARGE)] for j in js]

        def block(c):
            def visit(y, p_ref, p_at, q_ref, q_at, r_ref, r_at):
                r = r_ref[eight(r_at)]
                at = eight(y * nx + c * 8)
                totals = [it_ref[j, y, eight(c * 8)] + own[at, j * nz : (j + 1) * nz] * r for j in js]
                for k in range(ENLARGE):
                    p = p_ref[k, eight(p_at)]
                    totals = [t + scale[k] * p for t, scale in zip(totals, scales)]
                for j, t in zip(js, totals):
                    work[j, place(c, y), :] = t

            spots(c, visit)
            copy_out(half, c).start()

        loop(chunks, block)

    def residuals():
        scales = [table[square + k] for k in range(two)]

        def block(c):
            def visit(y, p_ref, p_at, q_ref, q_at, r_ref, r_at):
                r = r_ref[eight(r_at)]
                total = r - (SHIFT * own[eight(y * nx + c * 8), ENLARGE * nz : (ENLARGE + 1) * nz]) * r
                for k in range(ENLARGE):
                    total = total - scales[k] * p_ref[k, eight(p_at)]
                    total = total - scales[ENLARGE + k] * q_ref[k, eight(q_at)]
                r_work[place(c, y), :] = total

            spots(c, visit)
            copy_r(c).start()

        loop(chunks, block)

    updates(0)
    updates(1)
    residuals()
    for half in range(2):
        loop(chunks, lambda c, half=half: copy_out(half, c).wait())
    loop(chunks, lambda c: copy_r(c).wait())


def update(parts, pc, qc, pd, qd, t, rd, labels, held):
    _, ny, nx, nz = held.shape
    rows = nx * ny
    return pl.pallas_call(
        update_kernel,
        in_specs=vmem(9),
        out_specs=hbm(2),
        out_shape=[array(ENLARGE, rows, nz), array(rows, nz)],
        scratch_shapes=[
            pltpu.VMEM((ENLARGE * ENLARGE + 2 * ENLARGE, 8, nz), F32),
            pltpu.VMEM((nz, (ENLARGE + 1) * nz), F32),
            pltpu.VMEM((rows, nz), jnp.bfloat16),
            pltpu.VMEM((rows, (ENLARGE + 1) * nz), F32),
            pltpu.VMEM((ENLARGE, rows, nz), F32),
            pltpu.VMEM((rows, nz), F32),
            pltpu.SemaphoreType.DMA((2, nx // 8)),
            pltpu.SemaphoreType.DMA((nx // 8,)),
        ],
        compiler_params=params(),
        name="update",
    )(parts, pc, qc, pd, qd, t, rd, labels, held)


def shards(gx, gy, source, diagonal, face_x, face_y, face_z, iterates, labels):
    _, nx, ny, nz = iterates.shape
    arrays = [pinned(a) for a in (iterates, source, diagonal, face_x, face_y, face_z, labels.T)]
    xe, xo = x_edges(arrays)
    xo = lax.ppermute(xo, "gx", odd_pairs(gx))
    xe = lax.ppermute(xe, "gx", even_pairs(gx))
    *fields, held = load(arrays)
    *ext, ye = partial_residual(fields, xe, xo, gx, gy)
    ye = lax.ppermute(ye, "gy", even_pairs(gy))
    pc, yo = clean_first(ext, ny, nx)
    yo = lax.ppermute(yo, "gy", odd_pairs(gy))
    qc, acc = clean_second(ext, pc, ny, nx)
    pd, qd, rd, _, gram = edge_powers(ext, pc, acc, ye, yo, ny, nx, gx * gy)
    parts = lax.all_to_all(gram, ("gx", "gy"), 0, 0, tiled=True)
    new_iterates, new_residual = update(parts, pc, qc, pd, qd, ext[0], rd, ext[-1], held)
    return new_iterates.reshape(iterates.shape), new_residual.reshape(source.shape)


def solution(mesh):
    placed = (
        P("gx", "gy", None),
        P("gx", "gy", None),
        P("gx", "gy", None),
        P("gx", "gy", None),
        P("gx", "gy", None),
        P(None, "gx", "gy", None),
        P("gx", "gy"),
    )
    return jax.shard_map(
        functools.partial(shards, mesh.shape["gx"], mesh.shape["gy"]),
        mesh=mesh,
        in_specs=placed,
        out_specs=(P(None, "gx", "gy", None), P("gx", "gy", None)),
        check_vma=False,
    )
```

```python
import functools

import jax
import jax.numpy as jnp
from jax import lax
from jax.experimental import pallas as pl
from jax.experimental.pallas import tpu as pltpu
from jax.sharding import PartitionSpec as P

ENLARGE = 8
SHIFT = 6.5
F32 = jnp.float32
HIGHEST = lax.Precision.HIGHEST
PAIRS = [(j, k) for j in range(ENLARGE) for k in range(j, ENLARGE)]
VMEM_LIMIT = 20 * 1024 * 1024
PAD = 8
SENT = 2


def iota(shape, dim):
    return lax.broadcasted_iota(jnp.int32, shape, dim)


def even_pairs(count):
    return [(i, i ^ 1) for i in range(count) if (i ^ 1) < count]


def odd_pairs(count):
    return [(i, ((i - 1) ^ 1) + 1) for i in range(1, count) if ((i - 1) ^ 1) + 1 < count]


def vmem(count):
    return [pl.BlockSpec(memory_space=pltpu.VMEM)] * count


def hbm(count):
    return [pl.BlockSpec(memory_space=pltpu.HBM)] * count


def pinned(value):
    return pltpu.with_memory_space_constraint(value, pltpu.HBM)


def array(*shape):
    return jax.ShapeDtypeStruct(shape, F32)


def params():
    return pltpu.CompilerParams(vmem_limit_bytes=VMEM_LIMIT)


def aligned(value):
    return value if isinstance(value, int) else pl.multiple_of(value, 8)


def eight(start):
    return pl.ds(aligned(start), 8)


def near(start):
    return pl.ds(start, 8)


def loop(count, body, **kw):
    def wrapped(i, carry):
        body(i)
        return carry

    lax.fori_loop(0, count, wrapped, 0, **kw)


def edges_kernel(
    it_hbm, src_hbm, dg_hbm, fx_hbm, fy_hbm, fz_hbm, label_hbm,
    even_out, odd_out,
    work, fields, labels, sem_it, sem_field, sem_label,
):
    _, nx, ny, nz = it_hbm.shape
    sources = (src_hbm, dg_hbm, fx_hbm, fy_hbm, fz_hbm)
    lines = [(x, x) for x in range(3)] + [(nx - 3 + x, 13 + x) for x in range(3)]
    copies = [pltpu.make_async_copy(label_hbm, labels, sem_label)]
    for n, (x, row) in enumerate(lines):
        copies.append(pltpu.make_async_copy(it_hbm.at[:, x], work.at[:, :, row], sem_it.at[n]))
        for f, ref in enumerate(sources):
            copies.append(pltpu.make_async_copy(ref.at[x], fields.at[f, :, row], sem_field.at[f, n]))
    for copy in copies:
        copy.start()
    copies[0].wait()
    spread_rows = iota((16, nx), 0)
    spot = jnp.where(spread_rows < 8, spread_rows, spread_rows + nx - 16) == iota((16, nx), 1)
    ones = jnp.ones((nx, nz), jnp.bfloat16)
    marks = labels[...].astype(F32)
    for copy in copies[1:]:
        copy.wait()
    even = lax.rem(lax.axis_index("gx"), 2) == 0
    sub = iota((8, nz), 0)
    roll = lambda v, n: pltpu.roll(v, n, 0)
    for y in range(ny):
        row = jnp.where(spot, marks[y : y + 1], 0.0).astype(jnp.bfloat16)
        lb = jnp.dot(row, ones, preferred_element_type=F32)
        total = work[0, y]
        for j in range(1, ENLARGE):
            total = total + work[j, y]
        src, dg, fx, fy, fz = [fields[f, y] for f in range(5)]

        def first(at, is_low):
            if is_low:
                return jnp.where(sub < 3, total[at], jnp.where(sub >= 6, roll(lb[at], 6), roll(fx[at], 3)))
            return jnp.where(sub >= 5, total[at], jnp.where(sub < 2, roll(lb[at], 2), roll(fx[at], 5)))

        def second(at, start):
            values = src[at]
            for n, field in enumerate((dg, fy, fz)):
                begin = (start + 2 * n + 2) % 8
                inside = jnp.logical_or(sub == begin, sub == begin + 1)
                values = jnp.where(inside, roll(field[at], 2 * n + 2), values)
            return values

        lo, hi = slice(0, 8), slice(8, 16)
        for part, high, low in ((0, first(hi, False), first(lo, True)), (1, second(hi, 6), second(lo, 0))):
            even_out[part, y] = jnp.where(even, high, low)
            odd_out[part, y] = jnp.where(even, low, high)


def x_edges(arrays):
    _, nx, ny, nz = arrays[0].shape
    edge = array(2, ny, 8, nz)
    return pl.pallas_call(
        edges_kernel,
        in_specs=hbm(7),
        out_specs=vmem(2),
        out_shape=[edge] * 2,
        scratch_shapes=[
            pltpu.VMEM((ENLARGE, ny, 16, nz), F32),
            pltpu.VMEM((5, ny, 16, nz), F32),
            pltpu.VMEM((ny, nx), jnp.int32),
            pltpu.SemaphoreType.DMA((6,)),
            pltpu.SemaphoreType.DMA((5, 6)),
            pltpu.SemaphoreType.DMA,
        ],
        compiler_params=params(),
        name="x_edges",
    )(*arrays)


def load_kernel(
    it_hbm, src_hbm, dg_hbm, fx_hbm, fy_hbm, fz_hbm, label_hbm,
    s_out, src_out, dg_out, fx_out, fy_out, fz_out, lb_out, work,
    label_ref, sem_it, sem_field, sem_label,
):
    ny, nx, nz = s_out.shape
    pairs = list(zip((src_hbm, dg_hbm, fx_hbm, fy_hbm, fz_hbm), (src_out, dg_out, fx_out, fy_out, fz_out)))
    label_copy = pltpu.make_async_copy(label_hbm, label_ref, sem_label)

    def copy_it(y):
        return pltpu.make_async_copy(it_hbm.at[:, :, y], work.at[:, y], sem_it.at[y])

    def copy_field(f, y):
        return pltpu.make_async_copy(pairs[f][0].at[:, y], pairs[f][1].at[y], sem_field.at[f, y])

    def start(y):
        copy_it(y).start()
        for f in range(len(pairs)):
            copy_field(f, y).start()

    label_copy.start()
    loop(ny, start)
    label_copy.wait()

    spot = iota((nx, nx), 0) == iota((nx, nx), 1)
    ones = jnp.ones((nx, nz), jnp.bfloat16)
    labels = label_ref[...].astype(F32)
    for y in range(ny):
        row = jnp.where(spot, labels[y : y + 1], 0.0).astype(jnp.bfloat16)
        lb_out[y] = jnp.dot(row, ones, preferred_element_type=F32)

    def add(y):
        copy_it(y).wait()
        for r in range(0, nx, 8):
            total = work[0, y, r : r + 8]
            for j in range(1, ENLARGE):
                total = total + work[j, y, r : r + 8]
            s_out[y, r : r + 8] = total

    loop(ny, add)

    def finish(y):
        for f in range(len(pairs)):
            copy_field(f, y).wait()

    loop(ny, finish)


def load(arrays):
    _, nx, ny, nz = arrays[0].shape
    field = array(ny, nx, nz)
    return pl.pallas_call(
        load_kernel,
        in_specs=hbm(7),
        out_specs=vmem(8),
        out_shape=[field] * 7 + [array(ENLARGE, ny, nx, nz)],
        scratch_shapes=[
            pltpu.VMEM((ny, nx), jnp.int32),
            pltpu.SemaphoreType.DMA((ny,)),
            pltpu.SemaphoreType.DMA((5, ny)),
            pltpu.SemaphoreType.DMA,
        ],
        compiler_params=params(),
        cost_estimate=pl.CostEstimate(flops=2_000_000, bytes_accessed=16_000_000, transcendentals=0),
        name="load",
    )(*arrays)


def blocks_of(nx):
    wide = nx + PAD
    sizes = (wide, wide, wide, wide, nx, nx, nx, 8)
    starts = [sum(sizes[:i]) for i in range(len(sizes) + 1)]
    return wide, starts


def pack_y_edge(ny, nx, dest, is_high, t, s, fy, fx, dg, fz, lb):
    pitch = nx + 2 * PAD
    nz = t.shape[-1]
    wide, starts = blocks_of(nx)
    first = jnp.where(is_high, ny - 1, 0) * pitch
    second = jnp.where(is_high, ny - 2, 1) * pitch
    between = jnp.where(is_high, ny - 2, 0) * pitch

    def line(ref, base):
        return ref[pl.ds(base + (PAD - SENT), wide)]

    def inner(ref, base):
        return ref[pl.ds(pl.multiple_of(base + PAD, 8), nx)]

    parts = (
        line(t, first),
        line(s, first),
        line(fy, first),
        line(fx, first),
        inner(fy, between) * inner(t, second),
        inner(dg, first),
        inner(fz, first),
    )
    for b, values in enumerate(parts):
        dest[starts[b] : starts[b + 1]] = values
    spot = iota((wide, nz), 0) == iota((wide, nz), 1)
    one = jnp.sum(jnp.where(spot, line(lb, first), 0.0), axis=0, keepdims=True)
    two = jnp.sum(jnp.where(spot, line(lb, second), 0.0), axis=0, keepdims=True)
    which = iota((8, nz), 0)
    dest[starts[7] : starts[8]] = jnp.where(which == 0, one, jnp.where(which == 1, two, 0.0))


def partial_kernel(
    gx, gy,
    s_in, src_in, dg_in, fx_in, fy_in, fz_in, lb_in, xe_ref, xo_ref,
    t_out, s_out, fx_out, fy_out, dg_out, fz_out, lb_out, ye_ref,
    src_ext,
):
    ny, nx, nz = s_in.shape
    pitch = nx + 2 * PAD
    lane = iota((8, nz), 1)
    even_x = lax.rem(lax.axis_index("gx"), 2) == 0
    last_x = lax.axis_index("gx") == gx - 1
    last_y = lax.axis_index("gy") == gy - 1
    last_row = jnp.logical_and(iota((8, nz), 0) == 7, last_x)

    def fill(y):
        top = jnp.logical_and(last_y, y == ny - 1)
        fy_of = lambda v: jnp.where(top, 0.0, v)
        fz_of = lambda v: jnp.where(lane == nz - 1, 0.0, v)
        base = y * pitch
        roll = lambda v, n: pltpu.roll(v, n, 0)
        for at, is_low in ((0, True), (PAD + nx, False)):
            one, two = [
                jnp.where(even_x == is_low, xo_ref[part, y], xe_ref[part, y]) for part in range(2)
            ]
            here = eight(base + at)
            s_out[here] = one
            fx_out[here] = roll(one, 3 if is_low else 5)
            lb_out[here] = roll(one, 6 if is_low else 2)
            src_ext[here] = two
            dg_out[here] = roll(two, 6)
            fy_out[here] = fy_of(roll(two, 4))
            fz_out[here] = fz_of(roll(two, 2))
        for r in range(0, nx, 8):
            here = eight(base + PAD + r)
            span = slice(r, r + 8)
            s_out[here] = s_in[y, span]
            face = fx_in[y, span]
            fx_out[here] = jnp.where(last_row, 0.0, face) if r == nx - 8 else face
            lb_out[here] = lb_in[y, span]
            src_ext[here] = src_in[y, span]
            dg_out[here] = dg_in[y, span]
            fy_out[here] = fy_of(fy_in[y, span])
            fz_out[here] = fz_of(fz_in[y, span])

    loop(ny, fill)

    def layer(y, down=True, up=True):
        base = y * pitch
        for r in range(0, pitch, 8):
            at = base + r
            here = eight(at)
            s, fx, fz = s_out[here], fx_out[here], fz_out[here]
            if r == 0:
                sm, fxm = pltpu.roll(s, 1, 0), pltpu.roll(fx, 1, 0)
            else:
                sm, fxm = s_out[near(at - 1)], fx_out[near(at - 1)]
            sp = pltpu.roll(s, 7, 0) if r == pitch - 8 else s_out[near(at + 1)]
            total = dg_out[here] * s - fx * sp - fxm * sm
            if up:
                total = total - fy_out[here] * s_out[eight(at + pitch)]
            if down:
                total = total - fy_out[eight(at - pitch)] * s_out[eight(at - pitch)]
            total = total - fz * pltpu.roll(s, nz - 1, 1) - pltpu.roll(fz * s, 1, 1)
            t_out[here] = src_ext[here] - total

    layer(0, down=False)
    layer(ny - 1, up=False)
    loop(ny - 2, lambda i: layer(i + 1))

    even_y = lax.rem(lax.axis_index("gy"), 2) == 0
    pack_y_edge(ny, nx, ye_ref, even_y, t_out, s_out, fy_out, fx_out, dg_out, fz_out, lb_out)


def partial_residual(fields, xe, xo, gx, gy):
    ny, nx, nz = fields[0].shape
    rows = ny * (nx + 2 * PAD)
    ext = array(rows, nz)
    pack = array(blocks_of(nx)[1][-1], nz)
    return pl.pallas_call(
        functools.partial(partial_kernel, gx, gy),
        in_specs=vmem(9),
        out_specs=vmem(8),
        out_shape=[ext] * 7 + [pack],
        scratch_shapes=[pltpu.VMEM((rows, nz), F32)],
        compiler_params=params(),
        name="partial_residual",
    )(*fields, xe, xo)


def spread(parts):
    fields = []
    for j in range(ENLARGE):
        total = None
        for values, label in parts:
            term = jnp.where(label == float(j), values, 0.0)
            total = term if total is None else total + term
        fields.append(total)
    return fields


def along_z(fz, values):
    nz = values.shape[-1]
    return fz * pltpu.roll(values, nz - 1, 1) + pltpu.roll(fz * values, 1, 1)


def edge_near(ref, at, shift, last):
    if last == shift:
        return pltpu.roll(ref[eight(at)], 1 if shift < 0 else 7, 0)
    return ref[near(at + shift)]


def zeros_like_pairs(nz, count):
    return tuple(jnp.zeros((8, nz), F32) for _ in range(count))


def dot_own(sums, r, label, p):
    b = [jnp.where(label == float(j), r, 0.0) for j in range(ENLARGE)]
    n = len(PAIRS)
    own = tuple(t + v * v for t, v in zip(sums[n:], b))
    return tuple(t + b[j] * p[k] for t, (j, k) in zip(sums, PAIRS)) + own


def dot_pairs(sums, p, q):
    return tuple(t + p[j] * q[k] for t, (j, k) in zip(sums, PAIRS))


def clean_first_kernel(
    ny, nx,
    t_ref, s_ref, fx_ref, fy_ref, dg_ref, fz_ref, lb_ref,
    p_out, acc_out, yo_ref,
):
    nz = t_ref.shape[-1]
    pitch = nx + 2 * PAD

    def first(i):
        layer = (i + 2) * pitch
        for r in range(0, pitch, 8):
            at = layer + r
            last = -1 if r == 0 else (1 if r == pitch - 8 else 0)
            here = eight(at)
            value = t_ref[here]
            below, above = eight(at - pitch), eight(at + pitch)
            parts = [
                ((dg_ref[here] - SHIFT) * value - along_z(fz_ref[here], value), lb_ref[here]),
                (-fx_ref[here] * edge_near(t_ref, at, 1, last), edge_near(lb_ref, at, 1, last)),
                (-edge_near(fx_ref, at, -1, last) * edge_near(t_ref, at, -1, last), edge_near(lb_ref, at, -1, last)),
                (-fy_ref[here] * t_ref[above], lb_ref[above]),
                (-fy_ref[below] * t_ref[below], lb_ref[below]),
            ]
            for j, values in enumerate(spread(parts)):
                p_out[j, eight(i * pitch + r)] = values

    loop(ny - 4, first)

    def p_dots(i, sums):
        for r in range(PAD, PAD + nx, 8):
            p = [p_out[j, eight(i * pitch + r)] for j in range(ENLARGE)]
            sums = dot_pairs(sums, p, p)
        return sums

    sums = lax.fori_loop(0, ny - 4, p_dots, zeros_like_pairs(nz, len(PAIRS)))
    for n, values in enumerate(sums):
        acc_out[n] = values
    odd_y = lax.rem(lax.axis_index("gy"), 2) == 1
    pack_y_edge(ny, nx, yo_ref, odd_y, t_ref, s_ref, fy_ref, fx_ref, dg_ref, fz_ref, lb_ref)


def clean_second_kernel(
    ny, nx,
    t_ref, fx_ref, fy_ref, dg_ref, fz_ref, lb_ref, p_out,
    q_out, acc_out,
):
    nz = t_ref.shape[-1]
    pitch = nx + 2 * PAD
    chunks = nx // 8

    def second(i):
        for c in range(chunks):
            at = (i + 3) * pitch + PAD + c * 8
            own = (i + 1) * pitch + PAD + c * 8
            here = eight(at)
            dg, fz, fxp, fxm = dg_ref[here], fz_ref[here], fx_ref[here], fx_ref[near(at - 1)]
            fyp, fym = fy_ref[here], fy_ref[eight(at - pitch)]
            for j in range(ENLARGE):
                p = p_out[j, eight(own)]
                q = dg * p - fxp * p_out[j, near(own + 1)] - fxm * p_out[j, near(own - 1)]
                q = q - fyp * p_out[j, eight(own + pitch)] - fym * p_out[j, eight(own - pitch)]
                q_out[j, eight(i * nx + c * 8)] = q - along_z(fz, p)

    loop(ny - 6, second)

    def fields_at(ref, at):
        return [ref[j, eight(at)] for j in range(ENLARGE)]

    def own_dots(i, sums):
        for c in range(chunks):
            row = i * pitch + PAD + c * 8
            shifted = eight(row + 2 * pitch)
            sums = dot_own(sums, t_ref[shifted], lb_ref[shifted], fields_at(p_out, row))
        return sums

    def q_dots(i, sums):
        for c in range(chunks):
            p = fields_at(p_out, (i + 1) * pitch + PAD + c * 8)
            sums = dot_pairs(sums, p, fields_at(q_out, i * nx + c * 8))
        return sums

    slot = 0
    for dots, layers, count in ((own_dots, ny - 4, len(PAIRS) + ENLARGE), (q_dots, ny - 6, len(PAIRS))):
        sums = lax.fori_loop(0, layers, dots, zeros_like_pairs(nz, count))
        for values in sums:
            acc_out[slot] = values
            slot += 1


def clean_first(ext, ny, nx):
    nz = ext[0].shape[-1]
    return pl.pallas_call(
        functools.partial(clean_first_kernel, ny, nx),
        in_specs=vmem(7),
        out_specs=vmem(3),
        out_shape=[
            array(ENLARGE, (ny - 4) * (nx + 2 * PAD), nz),
            array(len(PAIRS), 8, nz),
            array(blocks_of(nx)[1][-1], nz),
        ],
        compiler_params=params(),
        cost_estimate=pl.CostEstimate(flops=20_000_000, bytes_accessed=8_000_000, transcendentals=0),
        name="clean_first",
    )(*ext)


def clean_second(ext, pc, ny, nx):
    t, _, fx, fy, dg, fz, lb = ext
    nz = t.shape[-1]
    return pl.pallas_call(
        functools.partial(clean_second_kernel, ny, nx),
        in_specs=vmem(7),
        out_specs=vmem(2),
        out_shape=[array(ENLARGE, (ny - 6) * nx, nz), array(2 * len(PAIRS) + ENLARGE, 8, nz)],
        compiler_params=params(),
        cost_estimate=pl.CostEstimate(flops=40_000_000, bytes_accessed=12_000_000, transcendentals=0),
        name="clean_second",
    )(t, fx, fy, dg, fz, lb, pc)


def side_of(phase):
    odd = lax.rem(lax.axis_index("gy"), 2)
    return odd if phase else 1 - odd


def edge_kernel(
    ny, nx, phase, devices,
    t_ref, s_ref, fx_ref, fy_ref, dg_ref, fz_ref, lb_ref, pc_ref, acc_pp, acc_ref, pack,
    p_out, q_out, r_out, *rest,
):
    outs, (lb, fx, fy, dg, fz, rows_acc) = rest[:-6], rest[-6:]
    nz = t_ref.shape[-1]
    pitch = nx + 2 * PAD
    chunks = nx // 8
    wide, starts = blocks_of(nx)
    left = PAD - SENT
    side = side_of(phase)

    def packed(b):
        return pack[starts[b] : starts[b + 1]]

    def setup(which):
        first, skip = (0, 2) if which == 0 else (ny - 4, 0)
        for i in range(4):
            source, dest = (first + i) * pitch, (skip + i) * pitch
            for ref, out in ((t_ref, r_out), (lb_ref, lb), (fx_ref, fx), (fy_ref, fy), (dg_ref, dg), (fz_ref, fz)):
                out[dest : dest + pitch] = ref[source : source + pitch]
        first, skip = (0, 4) if which == 0 else (ny - 6, 0)
        for i in range(2):
            source, dest = (first + i) * pitch, (skip + i) * pitch
            p_out[:, dest : dest + pitch] = pc_ref[:, source : source + pitch]
        inner, ghost, far = (2, 1, 0) if which == 0 else (3, 4, 5)
        at = lambda slot, start=left, size=wide: pl.ds(slot * pitch + start, size)
        base = pl.ds((0 if which == 0 else ny - 1) * pitch + left, wide)
        face = packed(2) if which == 0 else fy_ref[base]
        r_out[at(ghost)] = packed(0) + face * s_ref[base]
        r_out[at(inner)] = t_ref[base] + face * packed(1)
        if which == 0:
            fy[at(ghost)] = face
        fy[at(far if which == 0 else ghost)] = jnp.ones((wide, nz), F32)
        r_out[at(far, PAD, nx)] = packed(4)
        fx[at(ghost)] = packed(3)
        dg[at(ghost, PAD, nx)] = packed(5)
        fz[at(ghost, PAD, nx)] = packed(6)
        labels = packed(7)
        spot = iota((wide, nz), 0) == iota((wide, nz), 1)
        for r, slot in ((0, ghost), (1, far)):
            column = jnp.sum(jnp.where(spot, labels[r : r + 1], 0.0), axis=1, keepdims=True)
            lb[at(slot)] = jnp.broadcast_to(column, (wide, nz))

    for which in range(2):
        pl.when(side == which)(functools.partial(setup, which))

    def first(i):
        base = (i + 1 + side) * pitch
        for r in range(0, pitch, 8):
            at = base + r
            here, below, above = eight(at), eight(at - pitch), eight(at + pitch)
            value = r_out[here]
            parts = [
                ((dg[here] - SHIFT) * value - along_z(fz[here], value), lb[here]),
                (-fx[here] * r_out[near(at + 1)], lb[near(at + 1)]),
                (-fx[near(at - 1)] * r_out[near(at - 1)], lb[near(at - 1)]),
                (-fy[here] * r_out[above], lb[above]),
                (-fy[below] * r_out[below], lb[below]),
            ]
            for j, values in enumerate(spread(parts)):
                p_out[j, here] = values

    loop(3, first)

    def second(i):
        for c in range(chunks):
            at = (i + 2 - side) * pitch + PAD + c * 8
            here, below, above = eight(at), eight(at - pitch), eight(at + pitch)
            d, z, fxp, fxm, fyp, fym = dg[here], fz[here], fx[here], fx[near(at - 1)], fy[here], fy[below]
            for j in range(ENLARGE):
                p = p_out[j, here]
                q = d * p - fxp * p_out[j, near(at + 1)] - fxm * p_out[j, near(at - 1)]
                q = q - fyp * p_out[j, above] - fym * p_out[j, below]
                q_out[j, eight(i * nx + c * 8)] = q - along_z(z, p)

    loop(3, second)

    def fields_at(ref, at):
        return [ref[j, eight(at)] for j in range(ENLARGE)]

    def own_dots(i, sums):
        for c in range(chunks):
            at = (i + 2) * pitch + PAD + c * 8
            sums = dot_own(sums, r_out[eight(at)], lb[eight(at)], fields_at(p_out, at))
        return sums

    def p_dots(i, sums):
        for c in range(chunks):
            p = fields_at(p_out, (i + 2) * pitch + PAD + c * 8)
            sums = dot_pairs(sums, p, p)
        return sums

    def q_dots(i, sums):
        for c in range(chunks):
            p = fields_at(p_out, (i + 2 - side) * pitch + PAD + c * 8)
            sums = dot_pairs(sums, p, fields_at(q_out, i * nx + c * 8))
        return sums

    pairs = len(PAIRS)
    span = ENLARGE * ENLARGE
    groups = (
        (0, own_dots, 2, [(acc_ref, i) for i in range(pairs + ENLARGE)]),
        (1, p_dots, 2, [(acc_pp, i) for i in range(pairs)]),
        (2, q_dots, 3, [(acc_ref, pairs + ENLARGE + i) for i in range(pairs)]),
    )
    if phase:
        rows_acc[...] = jnp.zeros_like(rows_acc)

    def put(slot, values):
        rows_acc[slot : slot + 1] = jnp.sum(values, axis=0, keepdims=True)

    for which, dots, layers, stored in groups:
        sums = tuple(ref[i] for ref, i in stored)
        sums = lax.fori_loop(0, layers, dots, sums)
        if not phase:
            out = outs[0] if which == 1 else outs[1]
            for (_, i), values in zip(stored, sums):
                out[i] = values
            continue
        for (j, k), values in zip(PAIRS, sums):
            put(which * span + j * ENLARGE + k, values)
            if j != k:
                put(which * span + k * ENLARGE + j, values)
        for j, values in enumerate(sums[pairs:]):
            put(3 * span + j * ENLARGE + j, values)
    if phase:
        ones = jnp.ones((8, nz), F32)
        flat = lax.dot_general(
            ones, rows_acc[...], (((1,), (1,)), ((), ())), precision=HIGHEST, preferred_element_type=F32
        )
        half = 2 * span
        pair = jnp.where(iota((2, half), 0) == 0, flat[0:2, 0:half], flat[0:2, half : 2 * half])
        for d in range(devices):
            outs[0][d] = pair


def edge_powers(phase, ext, pc, acc_pp, acc, pack, ny, nx, devices):
    nz = pc.shape[-1]
    rows = 6 * (nx + 2 * PAD)
    half = 2 * ENLARGE * ENLARGE
    result = [array(devices, 2, half)] if phase else [array(*acc_pp.shape), array(*acc.shape)]
    return pl.pallas_call(
        functools.partial(edge_kernel, ny, nx, phase, devices),
        in_specs=vmem(11),
        out_specs=vmem(3 + len(result)),
        out_shape=[array(ENLARGE, rows, nz), array(ENLARGE, 3 * nx, nz), array(rows, nz)] + result,
        scratch_shapes=[pltpu.VMEM((rows, nz), F32)] * 5 + [pltpu.VMEM((2 * half, nz), F32)],
        compiler_params=params(),
        cost_estimate=pl.CostEstimate(flops=20_000_000, bytes_accessed=8_000_000, transcendentals=0),
        name=f"edge_powers_{phase}",
    )(*ext, pc, acc_pp, acc, pack)


def solve_columns(parts):
    nz = parts.shape[-1]
    span = ENLARGE * ENLARGE
    v = jnp.sum(parts, axis=0)
    lhs = jnp.concatenate([jnp.broadcast_to(v[0:1], (8, nz)), jnp.broadcast_to(v[1:2], (8, nz))], axis=1)
    source = iota((8, 2 * nz), 1)
    lhs = jnp.where(iota((8, 2 * nz), 0) == lax.rem(source, span) // ENLARGE, lhs, 0.0)
    k = iota((2 * nz, nz), 0)
    n = iota((2 * nz, nz), 1)
    which = k // span
    column = lax.rem(k, ENLARGE)

    def place(block, offset, scale):
        return jnp.where(jnp.logical_and(which == block, n == column + offset), scale, 0.0)

    upper = place(0, 0, 1.0) + place(3, 0, SHIFT) + place(1, 8, 1.0) + place(0, 8, SHIFT) + place(3, 16, 1.0)
    lower = place(1, 0, 1.0) + place(0, 0, SHIFT) + place(2, 8, 1.0) + place(0, 16, 1.0)
    dot = functools.partial(jnp.dot, precision=HIGHEST, preferred_element_type=F32)
    m = jnp.concatenate([dot(lhs, upper), dot(lhs, lower)], axis=0)
    row = iota(m.shape, 0)
    two = 2 * ENLARGE
    columns = [jnp.broadcast_to(m[:, i : i + 1], m.shape) for i in range(two + ENLARGE)]
    for i in range(two):
        inverse = 1.0 / columns[i][i : i + 1]
        for n in range(i + 1, two + ENLARGE):
            scaled = jnp.broadcast_to(columns[n][i : i + 1] * inverse, m.shape)
            columns[n] = jnp.where(row == i, scaled, columns[n] - columns[i] * scaled)
    return columns[two:]


def update_kernel(
    parts_ref, pc_ref, qc_ref, p0_ref, q0_ref, r0_ref, p1_ref, q1_ref, r1_ref, t_ref, lb_ref, it_ref,
    it_out, r_out,
    table, weights, onehot, own, work, r_work, sem_out, sem_r,
):
    _, ny, nx, nz = it_ref.shape
    pitch = nx + 2 * PAD
    two = 2 * ENLARGE
    square = ENLARGE * ENLARGE
    chunks = nx // 8

    def copy_out(half, c):
        span, rows = pl.ds(half * 4, 4), pl.ds(pl.multiple_of(c * 8 * ny, 8 * ny), 8 * ny)
        return pltpu.make_async_copy(work.at[span, rows], it_out.at[span, rows], sem_out.at[half, c])

    def copy_r(c):
        rows = pl.ds(pl.multiple_of(c * 8 * ny, 8 * ny), 8 * ny)
        return pltpu.make_async_copy(r_work.at[rows], r_out.at[rows], sem_r.at[c])

    def mark(y):
        lane = iota((nx, nz), 1)
        labels = lb_ref[pl.ds(pl.multiple_of(y * pitch + PAD, 8), nx)]
        chosen = jnp.logical_and(lane < 3 * ENLARGE, lax.rem(lane, ENLARGE).astype(F32) == labels)
        onehot[pl.ds(pl.multiple_of(y * nx, nx), nx)] = jnp.where(chosen, 1.0, 0.0).astype(jnp.bfloat16)

    loop(ny, mark)

    columns = solve_columns(parts_ref[...])
    carried = columns[0]
    for column in columns[1:]:
        carried = carried + column
    weights[...] = jnp.zeros_like(weights)
    for j, column in enumerate(columns + [carried]):
        for k in range(two):
            if j < ENLARGE and k < ENLARGE:
                continue
            slot = j * ENLARGE + k - ENLARGE if j < ENLARGE else square + k
            table[slot] = jnp.broadcast_to(column[k : k + 1], (8, nz))
        mine = column[0:ENLARGE]
        high = mine.astype(jnp.bfloat16).astype(F32)
        mid = (mine - high).astype(jnp.bfloat16).astype(F32)
        at = slice(j * nz, (j + 1) * nz)
        weights[0:8, at] = high
        weights[8:16, at] = mid
        weights[16:24, at] = mine - high - mid
    spread_weights = weights[...].astype(jnp.bfloat16)

    def coefficients(n):
        here = pl.ds(pl.multiple_of(n * 128, 128), 128)
        own[here] = jnp.dot(onehot[here], spread_weights, preferred_element_type=F32)

    loop(ny * nx // 128, coefficients, unroll=2)

    def spots(c, visit):
        x = PAD + c * 8
        for i in range(ny - 6):
            visit(i + 3, pc_ref, (i + 1) * pitch + x, qc_ref, i * nx + c * 8, t_ref, (i + 3) * pitch + x)
        for phase, p_ref, q_ref, r_ref in ((0, p0_ref, q0_ref, r0_ref), (1, p1_ref, q1_ref, r1_ref)):
            for side in range(2):

                def visit_side(side=side, p_ref=p_ref, q_ref=q_ref, r_ref=r_ref):
                    for i in range(3):
                        at = (i + 2 - side) * pitch + x
                        visit(i + side * (ny - 3), p_ref, at, q_ref, i * nx + c * 8, r_ref, at)

                pl.when(side_of(phase) == side)(visit_side)

    def place(c, y):
        return pl.ds(c * 8 * ny + y, 8, stride=ny)

    def updates(half):
        js = range(half * 4, half * 4 + 4)
        scales = [[table[j * ENLARGE + k] for k in range(ENLARGE)] for j in js]

        def block(c):
            def visit(y, p_ref, p_at, q_ref, q_at, r_ref, r_at):
                r = r_ref[eight(r_at)]
                at = eight(y * nx + c * 8)
                totals = [it_ref[j, y, eight(c * 8)] + own[at, j * nz : (j + 1) * nz] * r for j in js]
                for k in range(ENLARGE):
                    p = p_ref[k, eight(p_at)]
                    totals = [t + scale[k] * p for t, scale in zip(totals, scales)]
                for j, t in zip(js, totals):
                    work[j, place(c, y), :] = t

            spots(c, visit)
            copy_out(half, c).start()

        loop(chunks, block)

    def residuals():
        scales = [table[square + k] for k in range(two)]

        def block(c):
            def visit(y, p_ref, p_at, q_ref, q_at, r_ref, r_at):
                r = r_ref[eight(r_at)]
                total = r - (SHIFT * own[eight(y * nx + c * 8), ENLARGE * nz : (ENLARGE + 1) * nz]) * r
                for k in range(ENLARGE):
                    total = total - scales[k] * p_ref[k, eight(p_at)]
                    total = total - scales[ENLARGE + k] * q_ref[k, eight(q_at)]
                r_work[place(c, y), :] = total

            spots(c, visit)
            copy_r(c).start()

        loop(chunks, block)

    updates(0)
    updates(1)
    residuals()
    for half in range(2):
        loop(chunks, lambda c, half=half: copy_out(half, c).wait())
    loop(chunks, lambda c: copy_r(c).wait())


def update(parts, pc, qc, edges, t, labels, held):
    _, ny, nx, nz = held.shape
    rows = nx * ny
    return pl.pallas_call(
        update_kernel,
        in_specs=vmem(12),
        out_specs=hbm(2),
        out_shape=[array(ENLARGE, rows, nz), array(rows, nz)],
        scratch_shapes=[
            pltpu.VMEM((ENLARGE * ENLARGE + 2 * ENLARGE, 8, nz), F32),
            pltpu.VMEM((nz, (ENLARGE + 1) * nz), F32),
            pltpu.VMEM((rows, nz), jnp.bfloat16),
            pltpu.VMEM((rows, (ENLARGE + 1) * nz), F32),
            pltpu.VMEM((ENLARGE, rows, nz), F32),
            pltpu.VMEM((rows, nz), F32),
            pltpu.SemaphoreType.DMA((2, nx // 8)),
            pltpu.SemaphoreType.DMA((nx // 8,)),
        ],
        compiler_params=params(),
        name="update",
    )(parts, pc, qc, *edges, t, labels, held)


def shards(gx, gy, source, diagonal, face_x, face_y, face_z, iterates, labels):
    _, nx, ny, nz = iterates.shape
    arrays = [pinned(a) for a in (iterates, source, diagonal, face_x, face_y, face_z, labels.T)]
    xe, xo = x_edges(arrays)
    xo = lax.ppermute(xo, "gx", odd_pairs(gx))
    xe = lax.ppermute(xe, "gx", even_pairs(gx))
    *fields, held = load(arrays)
    *ext, ye = partial_residual(fields, xe, xo, gx, gy)
    ye = lax.ppermute(ye, "gy", even_pairs(gy))
    pc, acc_pp, yo = clean_first(ext, ny, nx)
    yo = lax.ppermute(yo, "gy", odd_pairs(gy))
    qc, acc = clean_second(ext, pc, ny, nx)
    p0, q0, r0, acc_pp, acc = edge_powers(0, ext, pc, acc_pp, acc, ye, ny, nx, gx * gy)
    p1, q1, r1, gram = edge_powers(1, ext, pc, acc_pp, acc, yo, ny, nx, gx * gy)
    parts = lax.all_to_all(gram, ("gx", "gy"), 0, 0, tiled=True)
    edges = (p0, q0, r0, p1, q1, r1)
    new_iterates, new_residual = update(parts, pc, qc, edges, ext[0], ext[-1], held)
    return new_iterates.reshape(iterates.shape), new_residual.reshape(source.shape)


def solution(mesh):
    placed = (
        P("gx", "gy", None),
        P("gx", "gy", None),
        P("gx", "gy", None),
        P("gx", "gy", None),
        P("gx", "gy", None),
        P(None, "gx", "gy", None),
        P("gx", "gy"),
    )
    return jax.shard_map(
        functools.partial(shards, mesh.shape["gx"], mesh.shape["gy"]),
        mesh=mesh,
        in_specs=placed,
        out_specs=(P(None, "gx", "gy", None), P("gx", "gy", None)),
        check_vma=False,
    )
```

```python
import functools

import jax
import jax.numpy as jnp
from jax import lax
from jax.experimental import pallas as pl
from jax.experimental.pallas import tpu as pltpu
from jax.sharding import PartitionSpec as P

ENLARGE = 8
SHIFT = 6.5
F32 = jnp.float32
HIGHEST = lax.Precision.HIGHEST
PAIRS = [(j, k) for j in range(ENLARGE) for k in range(j, ENLARGE)]
VMEM_LIMIT = 20 * 1024 * 1024
PAD = 8
SENT = 2


def iota(shape, dim):
    return lax.broadcasted_iota(jnp.int32, shape, dim)


def even_pairs(count):
    return [(i, i ^ 1) for i in range(count) if (i ^ 1) < count]


def odd_pairs(count):
    return [(i, ((i - 1) ^ 1) + 1) for i in range(1, count) if ((i - 1) ^ 1) + 1 < count]


def vmem(count):
    return [pl.BlockSpec(memory_space=pltpu.VMEM)] * count


def hbm(count):
    return [pl.BlockSpec(memory_space=pltpu.HBM)] * count


def pinned(value):
    return pltpu.with_memory_space_constraint(value, pltpu.HBM)


def array(*shape):
    return jax.ShapeDtypeStruct(shape, F32)


def params():
    return pltpu.CompilerParams(vmem_limit_bytes=VMEM_LIMIT)


def aligned(value):
    return value if isinstance(value, int) else pl.multiple_of(value, 8)


def eight(start):
    return pl.ds(aligned(start), 8)


def near(start):
    return pl.ds(start, 8)


def loop(count, body, **kw):
    def wrapped(i, carry):
        body(i)
        return carry

    lax.fori_loop(0, count, wrapped, 0, **kw)


def edges_kernel(
    it_hbm, src_hbm, dg_hbm, fx_hbm, fy_hbm, fz_hbm, label_hbm,
    even_out, odd_out,
    work, fields, labels, sem_it, sem_field, sem_label,
):
    _, nx, ny, nz = it_hbm.shape
    sources = (src_hbm, dg_hbm, fx_hbm, fy_hbm, fz_hbm)
    lines = [(x, x) for x in range(3)] + [(nx - 3 + x, 13 + x) for x in range(3)]
    copies = [pltpu.make_async_copy(label_hbm, labels, sem_label)]
    for n, (x, row) in enumerate(lines):
        copies.append(pltpu.make_async_copy(it_hbm.at[:, x], work.at[:, :, row], sem_it.at[n]))
        for f, ref in enumerate(sources):
            copies.append(pltpu.make_async_copy(ref.at[x], fields.at[f, :, row], sem_field.at[f, n]))
    for copy in copies:
        copy.start()
    copies[0].wait()
    spread_rows = iota((16, nx), 0)
    spot = jnp.where(spread_rows < 8, spread_rows, spread_rows + nx - 16) == iota((16, nx), 1)
    ones = jnp.ones((nx, nz), jnp.bfloat16)
    marks = labels[...].astype(F32)
    for copy in copies[1:]:
        copy.wait()
    even = lax.rem(lax.axis_index("gx"), 2) == 0
    sub = iota((8, nz), 0)
    roll = lambda v, n: pltpu.roll(v, n, 0)
    for y in range(ny):
        row = jnp.where(spot, marks[y : y + 1], 0.0).astype(jnp.bfloat16)
        lb = jnp.dot(row, ones, preferred_element_type=F32)
        total = work[0, y]
        for j in range(1, ENLARGE):
            total = total + work[j, y]
        src, dg, fx, fy, fz = [fields[f, y] for f in range(5)]

        def first(at, is_low):
            if is_low:
                return jnp.where(sub < 3, total[at], jnp.where(sub >= 6, roll(lb[at], 6), roll(fx[at], 3)))
            return jnp.where(sub >= 5, total[at], jnp.where(sub < 2, roll(lb[at], 2), roll(fx[at], 5)))

        def second(at, start):
            values = src[at]
            for n, field in enumerate((dg, fy, fz)):
                begin = (start + 2 * n + 2) % 8
                inside = jnp.logical_or(sub == begin, sub == begin + 1)
                values = jnp.where(inside, roll(field[at], 2 * n + 2), values)
            return values

        lo, hi = slice(0, 8), slice(8, 16)
        for part, high, low in ((0, first(hi, False), first(lo, True)), (1, second(hi, 6), second(lo, 0))):
            even_out[part, y] = jnp.where(even, high, low)
            odd_out[part, y] = jnp.where(even, low, high)


def x_edges(arrays):
    _, nx, ny, nz = arrays[0].shape
    edge = array(2, ny, 8, nz)
    return pl.pallas_call(
        edges_kernel,
        in_specs=hbm(7),
        out_specs=vmem(2),
        out_shape=[edge] * 2,
        scratch_shapes=[
            pltpu.VMEM((ENLARGE, ny, 16, nz), F32),
            pltpu.VMEM((5, ny, 16, nz), F32),
            pltpu.VMEM((ny, nx), jnp.int32),
            pltpu.SemaphoreType.DMA((6,)),
            pltpu.SemaphoreType.DMA((5, 6)),
            pltpu.SemaphoreType.DMA,
        ],
        compiler_params=params(),
        name="x_edges",
    )(*arrays)


def partial_layers(ny, pitch, rows, t, s, src_at, dg, fx, fy, fz):
    nz = t.shape[-1]

    def layer(y, down=True, up=True):
        base = y * pitch
        for r in rows:
            at = base + r
            here = eight(at)
            value, face, fzs = s[here], fx[here], fz[here]
            last = -1 if r == 0 else (1 if r == pitch - 8 else 0)
            total = dg[here] * value - face * edge_near(s, at, 1, last)
            total = total - edge_near(fx, at, -1, last) * edge_near(s, at, -1, last)
            if up:
                total = total - fy[here] * s[eight(at + pitch)]
            if down:
                total = total - fy[eight(at - pitch)] * s[eight(at - pitch)]
            total = total - fzs * pltpu.roll(value, nz - 1, 1) - pltpu.roll(fzs * value, 1, 1)
            t[here] = src_at(y, r) - total

    layer(0, down=False)
    layer(ny - 1, up=False)
    loop(ny - 2, lambda i: layer(i + 1))


def inside_rows(nx):
    return range(PAD + 8, PAD + nx - 8, 8)


def deep_rows(nx):
    return range(PAD + 16, PAD + nx - 16, 8)


def first_power(ny, pitch, rows, p_out, t, fx, fy, dg, fz, lb):
    def layer(i):
        base = (i + 2) * pitch
        for r in rows:
            at = base + r
            last = -1 if r == 0 else (1 if r == pitch - 8 else 0)
            here, below, above = eight(at), eight(at - pitch), eight(at + pitch)
            value = t[here]
            parts = [
                ((dg[here] - SHIFT) * value - along_z(fz[here], value), lb[here]),
                (-fx[here] * edge_near(t, at, 1, last), edge_near(lb, at, 1, last)),
                (-edge_near(fx, at, -1, last) * edge_near(t, at, -1, last), edge_near(lb, at, -1, last)),
                (-fy[here] * t[above], lb[above]),
                (-fy[below] * t[below], lb[below]),
            ]
            for j, values in enumerate(spread(parts)):
                p_out[j, eight(i * pitch + r)] = values

    loop(ny - 4, layer)


def load_kernel(
    gx, gy,
    it_ref, src_in, dg_in, fx_in, fy_in, fz_in, label_hbm,
    t_out, s_out, fx_out, fy_out, dg_out, fz_out, lb_out, src_out, p_out,
    label_ref, sem_label,
):
    _, nx, ny, nz = it_ref.shape
    pitch = nx + 2 * PAD
    label_copy = pltpu.make_async_copy(label_hbm, label_ref, sem_label)
    label_copy.start()

    last_x = lax.axis_index("gx") == gx - 1
    last_y = lax.axis_index("gy") == gy - 1
    top = jnp.logical_and(last_y, iota((8, nz), 0) == 7)
    end = iota((8, nz), 1) == nz - 1

    def add(c):
        for x in range(8):
            for y in range(0, ny, 8):
                place = pl.ds(y * pitch + PAD + c * 8 + x, 8, stride=pitch)
                at = (c * 8 + x, slice(y, y + 8))
                total = it_ref[(0,) + at]
                for j in range(1, ENLARGE):
                    total = total + it_ref[(j,) + at]
                s_out[place, :] = total
                src_out[place, :] = src_in[at]
                dg_out[place, :] = dg_in[at]
                face = fx_in[at]
                if x == 7:
                    face = jnp.where(jnp.logical_and(last_x, c == nx // 8 - 1), 0.0, face)
                fx_out[place, :] = face
                face = fy_in[at]
                fy_out[place, :] = jnp.where(top, 0.0, face) if y == ny - 8 else face
                fz_out[place, :] = jnp.where(end, 0.0, fz_in[at])

    loop(nx // 8, add)
    label_copy.wait()

    spot = iota((nx, nx), 0) == iota((nx, nx), 1)
    ones = jnp.ones((nx, nz), jnp.bfloat16)
    labels = label_ref[...].astype(F32)
    for y in range(ny):
        row = jnp.where(spot, labels[y : y + 1], 0.0).astype(jnp.bfloat16)
        lb_out[y * pitch + PAD : y * pitch + PAD + nx] = jnp.dot(row, ones, preferred_element_type=F32)

    src_at = lambda y, r: src_out[eight(y * pitch + r)]
    partial_layers(ny, pitch, inside_rows(nx), t_out, s_out, src_at, dg_out, fx_out, fy_out, fz_out)
    first_power(ny, pitch, deep_rows(nx), p_out, t_out, fx_out, fy_out, dg_out, fz_out, lb_out)


def load(arrays, labels, gx, gy):
    _, nx, ny, nz = arrays[0].shape
    return pl.pallas_call(
        functools.partial(load_kernel, gx, gy),
        in_specs=vmem(6) + hbm(1),
        out_specs=vmem(9),
        out_shape=[array(ny * (nx + 2 * PAD), nz)] * 8 + [array(ENLARGE, (ny - 4) * (nx + 2 * PAD), nz)],
        scratch_shapes=[
            pltpu.VMEM((ny, nx), jnp.int32),
            pltpu.SemaphoreType.DMA,
        ],
        compiler_params=params(),
        cost_estimate=pl.CostEstimate(flops=4_000_000, bytes_accessed=16_000_000, transcendentals=0),
        name="load",
    )(*arrays, labels)


def blocks_of(nx):
    wide = nx + PAD
    sizes = (wide, wide, wide, wide, nx, nx, nx, 8)
    starts = [sum(sizes[:i]) for i in range(len(sizes) + 1)]
    return wide, starts


def pack_y_edge(ny, nx, dest, is_high, t, s, fy, fx, dg, fz, lb):
    pitch = nx + 2 * PAD
    nz = t.shape[-1]
    wide, starts = blocks_of(nx)
    first = jnp.where(is_high, ny - 1, 0) * pitch
    second = jnp.where(is_high, ny - 2, 1) * pitch
    between = jnp.where(is_high, ny - 2, 0) * pitch

    def line(ref, base):
        return ref[pl.ds(base + (PAD - SENT), wide)]

    def inner(ref, base):
        return ref[pl.ds(pl.multiple_of(base + PAD, 8), nx)]

    parts = (
        line(t, first),
        line(s, first),
        line(fy, first),
        line(fx, first),
        inner(fy, between) * inner(t, second),
        inner(dg, first),
        inner(fz, first),
    )
    for b, values in enumerate(parts):
        dest[starts[b] : starts[b + 1]] = values
    spot = iota((wide, nz), 0) == iota((wide, nz), 1)
    one = jnp.sum(jnp.where(spot, line(lb, first), 0.0), axis=0, keepdims=True)
    two = jnp.sum(jnp.where(spot, line(lb, second), 0.0), axis=0, keepdims=True)
    which = iota((8, nz), 0)
    dest[starts[7] : starts[8]] = jnp.where(which == 0, one, jnp.where(which == 1, two, 0.0))


def partial_kernel(
    gy, nx, ny,
    t_in, s_in, fx_in, fy_in, dg_in, fz_in, lb_in, src_ref, xe_ref, xo_ref,
    t_out, s_out, fx_out, fy_out, dg_out, fz_out, lb_out, ye_ref,
    src_ghost,
):
    nz = t_in.shape[-1]
    pitch = nx + 2 * PAD
    end = iota((8, nz), 1) == nz - 1
    even_x = lax.rem(lax.axis_index("gx"), 2) == 0
    last_y = lax.axis_index("gy") == gy - 1
    roll = lambda v, n: pltpu.roll(v, n, 0)

    def fill(y):
        top = jnp.logical_and(last_y, y == ny - 1)
        for at, is_low in ((0, True), (PAD + nx, False)):
            one, two = [
                jnp.where(even_x == is_low, xo_ref[part, y], xe_ref[part, y]) for part in range(2)
            ]
            here = eight(y * pitch + at)
            s_out[here] = one
            fx_out[here] = roll(one, 3 if is_low else 5)
            lb_out[here] = roll(one, 6 if is_low else 2)
            src_ghost[0 if is_low else 1, y] = two
            dg_out[here] = roll(two, 6)
            fy_out[here] = jnp.where(top, 0.0, roll(two, 4))
            fz_out[here] = jnp.where(end, 0.0, roll(two, 2))

    loop(ny, fill, unroll=2)

    def src_at(y, r):
        if r == 0 or r == pitch - 8:
            return src_ghost[0 if r == 0 else 1, y]
        return src_ref[eight(y * pitch + r)]

    rows = [r for r in range(0, pitch, 8) if r not in inside_rows(nx)]
    partial_layers(ny, pitch, rows, t_out, s_out, src_at, dg_out, fx_out, fy_out, fz_out)
    even_y = lax.rem(lax.axis_index("gy"), 2) == 0
    pack_y_edge(ny, nx, ye_ref, even_y, t_out, s_out, fy_out, fx_out, dg_out, fz_out, lb_out)


def partial_residual(fields, xe, xo, gy, nx, ny):
    nz = xe.shape[-1]
    return pl.pallas_call(
        functools.partial(partial_kernel, gy, nx, ny),
        in_specs=vmem(10),
        out_specs=vmem(8),
        out_shape=[array(*a.shape) for a in fields[:7]] + [array(blocks_of(nx)[1][-1], nz)],
        input_output_aliases={i: i for i in range(7)},
        scratch_shapes=[pltpu.VMEM((2, ny, 8, nz), F32)],
        compiler_params=params(),
        name="partial_residual",
    )(*fields, xe, xo)


def spread(parts):
    fields = []
    for j in range(ENLARGE):
        total = None
        for values, label in parts:
            term = jnp.where(label == float(j), values, 0.0)
            total = term if total is None else total + term
        fields.append(total)
    return fields


def along_z(fz, values):
    nz = values.shape[-1]
    return fz * pltpu.roll(values, nz - 1, 1) + pltpu.roll(fz * values, 1, 1)


def edge_near(ref, at, shift, last):
    if last == shift:
        return pltpu.roll(ref[eight(at)], 1 if shift < 0 else 7, 0)
    return ref[near(at + shift)]


def zeros_like_pairs(nz, count):
    return tuple(jnp.zeros((8, nz), F32) for _ in range(count))


def dot_own(sums, r, label, p):
    b = [jnp.where(label == float(j), r, 0.0) for j in range(ENLARGE)]
    n = len(PAIRS)
    own = tuple(t + v * v for t, v in zip(sums[n:], b))
    return tuple(t + b[j] * p[k] for t, (j, k) in zip(sums, PAIRS)) + own


def dot_pairs(sums, p, q):
    return tuple(t + p[j] * q[k] for t, (j, k) in zip(sums, PAIRS))


def clean_first_kernel(
    ny, nx,
    t_ref, s_ref, fx_ref, fy_ref, dg_ref, fz_ref, lb_ref, p_in,
    p_out, acc_out, yo_ref,
):
    nz = t_ref.shape[-1]
    pitch = nx + 2 * PAD

    rows = [r for r in range(0, pitch, 8) if r not in deep_rows(nx)]
    first_power(ny, pitch, rows, p_out, t_ref, fx_ref, fy_ref, dg_ref, fz_ref, lb_ref)

    def p_dots(i, sums):
        for r in range(PAD, PAD + nx, 8):
            p = [p_out[j, eight(i * pitch + r)] for j in range(ENLARGE)]
            sums = dot_pairs(sums, p, p)
        return sums

    sums = lax.fori_loop(0, ny - 4, p_dots, zeros_like_pairs(nz, len(PAIRS)))
    for n, values in enumerate(sums):
        acc_out[n] = values
    odd_y = lax.rem(lax.axis_index("gy"), 2) == 1
    pack_y_edge(ny, nx, yo_ref, odd_y, t_ref, s_ref, fy_ref, fx_ref, dg_ref, fz_ref, lb_ref)


def clean_second_kernel(
    ny, nx,
    t_ref, fx_ref, fy_ref, dg_ref, fz_ref, lb_ref, p_out,
    q_out, acc_out,
):
    nz = t_ref.shape[-1]
    pitch = nx + 2 * PAD
    chunks = nx // 8

    def second(i):
        for c in range(chunks):
            at = (i + 3) * pitch + PAD + c * 8
            own = (i + 1) * pitch + PAD + c * 8
            here = eight(at)
            dg, fz, fxp, fxm = dg_ref[here], fz_ref[here], fx_ref[here], fx_ref[near(at - 1)]
            fyp, fym = fy_ref[here], fy_ref[eight(at - pitch)]
            for j in range(ENLARGE):
                p = p_out[j, eight(own)]
                q = dg * p - fxp * p_out[j, near(own + 1)] - fxm * p_out[j, near(own - 1)]
                q = q - fyp * p_out[j, eight(own + pitch)] - fym * p_out[j, eight(own - pitch)]
                q_out[j, eight(i * nx + c * 8)] = q - along_z(fz, p)

    loop(ny - 6, second)

    def fields_at(ref, at):
        return [ref[j, eight(at)] for j in range(ENLARGE)]

    def own_dots(i, sums):
        for c in range(chunks):
            row = i * pitch + PAD + c * 8
            shifted = eight(row + 2 * pitch)
            sums = dot_own(sums, t_ref[shifted], lb_ref[shifted], fields_at(p_out, row))
        return sums

    def q_dots(i, sums):
        for c in range(chunks):
            p = fields_at(p_out, (i + 1) * pitch + PAD + c * 8)
            sums = dot_pairs(sums, p, fields_at(q_out, i * nx + c * 8))
        return sums

    slot = 0
    for dots, layers, count in ((own_dots, ny - 4, len(PAIRS) + ENLARGE), (q_dots, ny - 6, len(PAIRS))):
        sums = lax.fori_loop(0, layers, dots, zeros_like_pairs(nz, count))
        for values in sums:
            acc_out[slot] = values
            slot += 1


def clean_first(ext, inner, ny, nx):
    nz = ext[0].shape[-1]
    return pl.pallas_call(
        functools.partial(clean_first_kernel, ny, nx),
        in_specs=vmem(8),
        out_specs=vmem(3),
        out_shape=[
            array(ENLARGE, (ny - 4) * (nx + 2 * PAD), nz),
            array(len(PAIRS), 8, nz),
            array(blocks_of(nx)[1][-1], nz),
        ],
        input_output_aliases={7: 0},
        compiler_params=params(),
        cost_estimate=pl.CostEstimate(flops=20_000_000, bytes_accessed=8_000_000, transcendentals=0),
        name="clean_first",
    )(*ext, inner)


def clean_second(ext, pc, ny, nx):
    t, _, fx, fy, dg, fz, lb = ext
    nz = t.shape[-1]
    return pl.pallas_call(
        functools.partial(clean_second_kernel, ny, nx),
        in_specs=vmem(7),
        out_specs=vmem(2),
        out_shape=[array(ENLARGE, (ny - 6) * nx, nz), array(2 * len(PAIRS) + ENLARGE, 8, nz)],
        compiler_params=params(),
        cost_estimate=pl.CostEstimate(flops=40_000_000, bytes_accessed=12_000_000, transcendentals=0),
        name="clean_second",
    )(t, fx, fy, dg, fz, lb, pc)


def side_of(phase):
    odd = lax.rem(lax.axis_index("gy"), 2)
    return odd if phase else 1 - odd


def edge_kernel(
    ny, nx, phase, devices,
    t_ref, s_ref, fx_ref, fy_ref, dg_ref, fz_ref, lb_ref, pc_ref, acc_pp, acc_ref, pack,
    p_out, q_out, r_out, *rest,
):
    outs, (lb, fx, fy, dg, fz, rows_acc) = rest[:-6], rest[-6:]
    nz = t_ref.shape[-1]
    pitch = nx + 2 * PAD
    chunks = nx // 8
    wide, starts = blocks_of(nx)
    left = PAD - SENT
    side = side_of(phase)

    def packed(b):
        return pack[starts[b] : starts[b + 1]]

    def setup(which):
        first, skip = (0, 2) if which == 0 else (ny - 4, 0)
        for i in range(4):
            source, dest = (first + i) * pitch, (skip + i) * pitch
            for ref, out in ((t_ref, r_out), (lb_ref, lb), (fx_ref, fx), (fy_ref, fy), (dg_ref, dg), (fz_ref, fz)):
                out[dest : dest + pitch] = ref[source : source + pitch]
        first, skip = (0, 4) if which == 0 else (ny - 6, 0)
        for i in range(2):
            source, dest = (first + i) * pitch, (skip + i) * pitch
            p_out[:, dest : dest + pitch] = pc_ref[:, source : source + pitch]
        inner, ghost, far = (2, 1, 0) if which == 0 else (3, 4, 5)
        at = lambda slot, start=left, size=wide: pl.ds(slot * pitch + start, size)
        base = pl.ds((0 if which == 0 else ny - 1) * pitch + left, wide)
        face = packed(2) if which == 0 else fy_ref[base]
        r_out[at(ghost)] = packed(0) + face * s_ref[base]
        r_out[at(inner)] = t_ref[base] + face * packed(1)
        if which == 0:
            fy[at(ghost)] = face
        fy[at(far if which == 0 else ghost)] = jnp.ones((wide, nz), F32)
        r_out[at(far, PAD, nx)] = packed(4)
        fx[at(ghost)] = packed(3)
        dg[at(ghost, PAD, nx)] = packed(5)
        fz[at(ghost, PAD, nx)] = packed(6)
        labels = packed(7)
        spot = iota((wide, nz), 0) == iota((wide, nz), 1)
        for r, slot in ((0, ghost), (1, far)):
            column = jnp.sum(jnp.where(spot, labels[r : r + 1], 0.0), axis=1, keepdims=True)
            lb[at(slot)] = jnp.broadcast_to(column, (wide, nz))

    for which in range(2):
        pl.when(side == which)(functools.partial(setup, which))

    def first(i):
        base = (i + 1 + side) * pitch
        for r in range(0, pitch, 8):
            at = base + r
            here, below, above = eight(at), eight(at - pitch), eight(at + pitch)
            value = r_out[here]
            parts = [
                ((dg[here] - SHIFT) * value - along_z(fz[here], value), lb[here]),
                (-fx[here] * r_out[near(at + 1)], lb[near(at + 1)]),
                (-fx[near(at - 1)] * r_out[near(at - 1)], lb[near(at - 1)]),
                (-fy[here] * r_out[above], lb[above]),
                (-fy[below] * r_out[below], lb[below]),
            ]
            for j, values in enumerate(spread(parts)):
                p_out[j, here] = values

    loop(3, first)

    def second(i):
        for c in range(chunks):
            at = (i + 2 - side) * pitch + PAD + c * 8
            here, below, above = eight(at), eight(at - pitch), eight(at + pitch)
            d, z, fxp, fxm, fyp, fym = dg[here], fz[here], fx[here], fx[near(at - 1)], fy[here], fy[below]
            for j in range(ENLARGE):
                p = p_out[j, here]
                q = d * p - fxp * p_out[j, near(at + 1)] - fxm * p_out[j, near(at - 1)]
                q = q - fyp * p_out[j, above] - fym * p_out[j, below]
                q_out[j, eight(i * nx + c * 8)] = q - along_z(z, p)

    loop(3, second)

    def fields_at(ref, at):
        return [ref[j, eight(at)] for j in range(ENLARGE)]

    def own_dots(i, sums):
        for c in range(chunks):
            at = (i + 2) * pitch + PAD + c * 8
            sums = dot_own(sums, r_out[eight(at)], lb[eight(at)], fields_at(p_out, at))
        return sums

    def p_dots(i, sums):
        for c in range(chunks):
            p = fields_at(p_out, (i + 2) * pitch + PAD + c * 8)
            sums = dot_pairs(sums, p, p)
        return sums

    def q_dots(i, sums):
        for c in range(chunks):
            p = fields_at(p_out, (i + 2 - side) * pitch + PAD + c * 8)
            sums = dot_pairs(sums, p, fields_at(q_out, i * nx + c * 8))
        return sums

    pairs = len(PAIRS)
    span = ENLARGE * ENLARGE
    groups = (
        (0, own_dots, 2, [(acc_ref, i) for i in range(pairs + ENLARGE)]),
        (1, p_dots, 2, [(acc_pp, i) for i in range(pairs)]),
        (2, q_dots, 3, [(acc_ref, pairs + ENLARGE + i) for i in range(pairs)]),
    )
    if phase:
        rows_acc[...] = jnp.zeros_like(rows_acc)

    def put(slot, values):
        rows_acc[slot : slot + 1] = jnp.sum(values, axis=0, keepdims=True)

    for which, dots, layers, stored in groups:
        sums = tuple(ref[i] for ref, i in stored)
        sums = lax.fori_loop(0, layers, dots, sums)
        if not phase:
            out = outs[0] if which == 1 else outs[1]
            for (_, i), values in zip(stored, sums):
                out[i] = values
            continue
        for (j, k), values in zip(PAIRS, sums):
            put(which * span + j * ENLARGE + k, values)
            if j != k:
                put(which * span + k * ENLARGE + j, values)
        for j, values in enumerate(sums[pairs:]):
            put(3 * span + j * ENLARGE + j, values)
    if phase:
        ones = jnp.ones((8, nz), F32)
        flat = lax.dot_general(
            ones, rows_acc[...], (((1,), (1,)), ((), ())), precision=HIGHEST, preferred_element_type=F32
        )
        half = 2 * span
        pair = jnp.where(iota((2, half), 0) == 0, flat[0:2, 0:half], flat[0:2, half : 2 * half])
        for d in range(devices):
            outs[0][d] = pair


def edge_powers(phase, ext, pc, acc_pp, acc, pack, ny, nx, devices):
    nz = pc.shape[-1]
    rows = 6 * (nx + 2 * PAD)
    half = 2 * ENLARGE * ENLARGE
    result = [array(devices, 2, half)] if phase else [array(*acc_pp.shape), array(*acc.shape)]
    return pl.pallas_call(
        functools.partial(edge_kernel, ny, nx, phase, devices),
        in_specs=vmem(11),
        out_specs=vmem(3 + len(result)),
        out_shape=[array(ENLARGE, rows, nz), array(ENLARGE, 3 * nx, nz), array(rows, nz)] + result,
        scratch_shapes=[pltpu.VMEM((rows, nz), F32)] * 5 + [pltpu.VMEM((2 * half, nz), F32)],
        compiler_params=params(),
        cost_estimate=pl.CostEstimate(flops=20_000_000, bytes_accessed=8_000_000, transcendentals=0),
        name=f"edge_powers_{phase}",
    )(*ext, pc, acc_pp, acc, pack)


def solve_columns(parts):
    nz = parts.shape[-1]
    span = ENLARGE * ENLARGE
    v = jnp.sum(parts, axis=0)
    lhs = jnp.concatenate([jnp.broadcast_to(v[0:1], (8, nz)), jnp.broadcast_to(v[1:2], (8, nz))], axis=1)
    source = iota((8, 2 * nz), 1)
    lhs = jnp.where(iota((8, 2 * nz), 0) == lax.rem(source, span) // ENLARGE, lhs, 0.0)
    k = iota((2 * nz, nz), 0)
    n = iota((2 * nz, nz), 1)
    which = k // span
    column = lax.rem(k, ENLARGE)

    def place(block, offset, scale):
        return jnp.where(jnp.logical_and(which == block, n == column + offset), scale, 0.0)

    upper = place(0, 0, 1.0) + place(3, 0, SHIFT) + place(1, 8, 1.0) + place(0, 8, SHIFT) + place(3, 16, 1.0)
    lower = place(1, 0, 1.0) + place(0, 0, SHIFT) + place(2, 8, 1.0) + place(0, 16, 1.0)
    dot = functools.partial(jnp.dot, precision=HIGHEST, preferred_element_type=F32)
    m = jnp.concatenate([dot(lhs, upper), dot(lhs, lower)], axis=0)
    row = iota(m.shape, 0)
    two = 2 * ENLARGE
    columns = [jnp.broadcast_to(m[:, i : i + 1], m.shape) for i in range(two + ENLARGE)]
    for i in range(two):
        inverse = 1.0 / columns[i][i : i + 1]
        for n in range(i + 1, two + ENLARGE):
            scaled = jnp.broadcast_to(columns[n][i : i + 1] * inverse, m.shape)
            columns[n] = jnp.where(row == i, scaled, columns[n] - columns[i] * scaled)
    return columns[two:]


def update_kernel(
    parts_ref, pc_ref, qc_ref, p0_ref, q0_ref, r0_ref, p1_ref, q1_ref, r1_ref, t_ref, lb_ref, it_hbm,
    it_out, r_out, it_ref,
    table, weights, onehot, own, work, r_work, sem_in, sem_out, sem_r,
):
    _, ny, nx, nz = it_ref.shape
    pitch = nx + 2 * PAD
    two = 2 * ENLARGE
    square = ENLARGE * ENLARGE
    chunks = nx // 8

    def copy_in(y):
        return pltpu.make_async_copy(it_hbm.at[:, :, y], it_ref.at[:, y], sem_in.at[y])

    loop(ny, lambda y: copy_in(y).start())

    def copy_out(half, c):
        span, rows = pl.ds(half * 4, 4), pl.ds(pl.multiple_of(c * 8 * ny, 8 * ny), 8 * ny)
        return pltpu.make_async_copy(work.at[span, rows], it_out.at[span, rows], sem_out.at[half, c])

    def copy_r(c):
        rows = pl.ds(pl.multiple_of(c * 8 * ny, 8 * ny), 8 * ny)
        return pltpu.make_async_copy(r_work.at[rows], r_out.at[rows], sem_r.at[c])

    def mark(y):
        lane = iota((nx, nz), 1)
        labels = lb_ref[pl.ds(pl.multiple_of(y * pitch + PAD, 8), nx)]
        chosen = jnp.logical_and(lane < 3 * ENLARGE, lax.rem(lane, ENLARGE).astype(F32) == labels)
        onehot[pl.ds(pl.multiple_of(y * nx, nx), nx)] = jnp.where(chosen, 1.0, 0.0).astype(jnp.bfloat16)

    loop(ny, mark)

    columns = solve_columns(parts_ref[...])
    carried = columns[0]
    for column in columns[1:]:
        carried = carried + column
    weights[...] = jnp.zeros_like(weights)
    for j, column in enumerate(columns + [carried]):
        for k in range(two):
            if j < ENLARGE and k < ENLARGE:
                continue
            slot = j * ENLARGE + k - ENLARGE if j < ENLARGE else square + k
            table[slot] = jnp.broadcast_to(column[k : k + 1], (8, nz))
        mine = column[0:ENLARGE]
        high = mine.astype(jnp.bfloat16).astype(F32)
        mid = (mine - high).astype(jnp.bfloat16).astype(F32)
        at = slice(j * nz, (j + 1) * nz)
        weights[0:8, at] = high
        weights[8:16, at] = mid
        weights[16:24, at] = mine - high - mid
    spread_weights = weights[...].astype(jnp.bfloat16)

    def coefficients(n):
        here = pl.ds(pl.multiple_of(n * 128, 128), 128)
        own[here] = jnp.dot(onehot[here], spread_weights, preferred_element_type=F32)

    loop(ny * nx // 128, coefficients, unroll=2)

    def spots(c, visit):
        x = PAD + c * 8
        for i in range(ny - 6):
            visit(i + 3, pc_ref, (i + 1) * pitch + x, qc_ref, i * nx + c * 8, t_ref, (i + 3) * pitch + x)
        for phase, p_ref, q_ref, r_ref in ((0, p0_ref, q0_ref, r0_ref), (1, p1_ref, q1_ref, r1_ref)):
            for side in range(2):

                def visit_side(side=side, p_ref=p_ref, q_ref=q_ref, r_ref=r_ref):
                    for i in range(3):
                        at = (i + 2 - side) * pitch + x
                        visit(i + side * (ny - 3), p_ref, at, q_ref, i * nx + c * 8, r_ref, at)

                pl.when(side_of(phase) == side)(visit_side)

    def place(c, y):
        return pl.ds(c * 8 * ny + y, 8, stride=ny)

    def updates(half):
        js = range(half * 4, half * 4 + 4)
        scales = [[table[j * ENLARGE + k] for k in range(ENLARGE)] for j in js]

        def block(c):
            def visit(y, p_ref, p_at, q_ref, q_at, r_ref, r_at):
                r = r_ref[eight(r_at)]
                at = eight(y * nx + c * 8)
                totals = [it_ref[j, y, eight(c * 8)] + own[at, j * nz : (j + 1) * nz] * r for j in js]
                for k in range(ENLARGE):
                    p = p_ref[k, eight(p_at)]
                    totals = [t + scale[k] * p for t, scale in zip(totals, scales)]
                for j, t in zip(js, totals):
                    work[j, place(c, y), :] = t

            spots(c, visit)
            copy_out(half, c).start()

        loop(chunks, block)

    def residuals():
        scales = [table[square + k] for k in range(two)]

        def block(c):
            def visit(y, p_ref, p_at, q_ref, q_at, r_ref, r_at):
                r = r_ref[eight(r_at)]
                total = r - (SHIFT * own[eight(y * nx + c * 8), ENLARGE * nz : (ENLARGE + 1) * nz]) * r
                for k in range(ENLARGE):
                    total = total - scales[k] * p_ref[k, eight(p_at)]
                    total = total - scales[ENLARGE + k] * q_ref[k, eight(q_at)]
                r_work[place(c, y), :] = total

            spots(c, visit)
            copy_r(c).start()

        loop(chunks, block)

    residuals()
    loop(ny, lambda y: copy_in(y).wait())
    updates(0)
    updates(1)
    for half in range(2):
        loop(chunks, lambda c, half=half: copy_out(half, c).wait())
    loop(chunks, lambda c: copy_r(c).wait())


def update(parts, pc, qc, edges, t, labels, iterates):
    _, nx, ny, nz = iterates.shape
    rows = nx * ny
    return pl.pallas_call(
        update_kernel,
        in_specs=vmem(11) + hbm(1),
        out_specs=hbm(2),
        out_shape=[array(ENLARGE, rows, nz), array(rows, nz)],
        scratch_shapes=[
            pltpu.VMEM((ENLARGE, ny, nx, nz), F32),
            pltpu.VMEM((ENLARGE * ENLARGE + 2 * ENLARGE, 8, nz), F32),
            pltpu.VMEM((nz, (ENLARGE + 1) * nz), F32),
            pltpu.VMEM((rows, nz), jnp.bfloat16),
            pltpu.VMEM((rows, (ENLARGE + 1) * nz), F32),
            pltpu.VMEM((ENLARGE, rows, nz), F32),
            pltpu.VMEM((rows, nz), F32),
            pltpu.SemaphoreType.DMA((ny,)),
            pltpu.SemaphoreType.DMA((2, nx // 8)),
            pltpu.SemaphoreType.DMA((nx // 8,)),
        ],
        compiler_params=params(),
        name="update",
    )(parts, pc, qc, *edges, t, labels, iterates)


def shards(gx, gy, source, diagonal, face_x, face_y, face_z, iterates, labels):
    _, nx, ny, nz = iterates.shape
    arrays = [pinned(a) for a in (iterates, source, diagonal, face_x, face_y, face_z, labels.T)]
    xe, xo = x_edges(arrays)
    xo = lax.ppermute(xo, "gx", odd_pairs(gx))
    xe = lax.ppermute(xe, "gx", even_pairs(gx))
    direct = [iterates, source, diagonal, face_x, face_y, face_z]
    *fields, inner = load(direct, arrays[6], gx, gy)
    *ext, ye = partial_residual(fields, xe, xo, gy, nx, ny)
    ye = lax.ppermute(ye, "gy", even_pairs(gy))
    pc, acc_pp, yo = clean_first(ext, inner, ny, nx)
    yo = lax.ppermute(yo, "gy", odd_pairs(gy))
    qc, acc = clean_second(ext, pc, ny, nx)
    p0, q0, r0, acc_pp, acc = edge_powers(0, ext, pc, acc_pp, acc, ye, ny, nx, gx * gy)
    p1, q1, r1, gram = edge_powers(1, ext, pc, acc_pp, acc, yo, ny, nx, gx * gy)
    parts = lax.all_to_all(gram, ("gx", "gy"), 0, 0, tiled=True)
    edges = (p0, q0, r0, p1, q1, r1)
    new_iterates, new_residual = update(parts, pc, qc, edges, ext[0], ext[-1], arrays[0])
    return new_iterates.reshape(iterates.shape), new_residual.reshape(source.shape)


def solution(mesh):
    placed = (
        P("gx", "gy", None),
        P("gx", "gy", None),
        P("gx", "gy", None),
        P("gx", "gy", None),
        P("gx", "gy", None),
        P(None, "gx", "gy", None),
        P("gx", "gy"),
    )
    return jax.shard_map(
        functools.partial(shards, mesh.shape["gx"], mesh.shape["gy"]),
        mesh=mesh,
        in_specs=placed,
        out_specs=(P(None, "gx", "gy", None), P("gx", "gy", None)),
        check_vma=False,
    )
```

```python
import functools

import jax
import jax.numpy as jnp
from jax import lax
from jax.experimental import pallas as pl
from jax.experimental.pallas import tpu as pltpu
from jax.sharding import PartitionSpec as P

ENLARGE = 8
SHIFT = 6.5
F32 = jnp.float32
HIGHEST = lax.Precision.HIGHEST
PAIRS = [(j, k) for j in range(ENLARGE) for k in range(j, ENLARGE)]
VMEM_LIMIT = 20 * 1024 * 1024
PAD = 8
SENT = 2


def iota(shape, dim):
    return lax.broadcasted_iota(jnp.int32, shape, dim)


def even_pairs(count):
    return [(i, i ^ 1) for i in range(count) if (i ^ 1) < count]


def odd_pairs(count):
    return [(i, ((i - 1) ^ 1) + 1) for i in range(1, count) if ((i - 1) ^ 1) + 1 < count]


def vmem(count):
    return [pl.BlockSpec(memory_space=pltpu.VMEM)] * count


def hbm(count):
    return [pl.BlockSpec(memory_space=pltpu.HBM)] * count


def pinned(value):
    return pltpu.with_memory_space_constraint(value, pltpu.HBM)


def array(*shape):
    return jax.ShapeDtypeStruct(shape, F32)


def params():
    return pltpu.CompilerParams(vmem_limit_bytes=VMEM_LIMIT)


def aligned(value):
    return value if isinstance(value, int) else pl.multiple_of(value, 8)


def eight(start):
    return pl.ds(aligned(start), 8)


def near(start):
    return pl.ds(start, 8)


def loop(count, body, **kw):
    def wrapped(i, carry):
        body(i)
        return carry

    lax.fori_loop(0, count, wrapped, 0, **kw)


def edges_kernel(
    it_hbm, src_hbm, dg_hbm, fx_hbm, fy_hbm, fz_hbm, label_hbm,
    even_out, odd_out,
    work, fields, labels, sem_it, sem_field, sem_label,
):
    _, nx, ny, nz = it_hbm.shape
    sources = (src_hbm, dg_hbm, fx_hbm, fy_hbm, fz_hbm)
    lines = [(x, x) for x in range(3)] + [(nx - 3 + x, 13 + x) for x in range(3)]
    copies = [pltpu.make_async_copy(label_hbm, labels, sem_label)]
    for n, (x, row) in enumerate(lines):
        copies.append(pltpu.make_async_copy(it_hbm.at[:, x], work.at[:, :, row], sem_it.at[n]))
        for f, ref in enumerate(sources):
            copies.append(pltpu.make_async_copy(ref.at[x], fields.at[f, :, row], sem_field.at[f, n]))
    for copy in copies:
        copy.start()
    copies[0].wait()
    spread_rows = iota((16, nx), 0)
    spot = jnp.where(spread_rows < 8, spread_rows, spread_rows + nx - 16) == iota((16, nx), 1)
    ones = jnp.ones((nx, nz), jnp.bfloat16)
    marks = labels[...].astype(F32)
    for copy in copies[1:]:
        copy.wait()
    even = lax.rem(lax.axis_index("gx"), 2) == 0
    sub = iota((8, nz), 0)
    roll = lambda v, n: pltpu.roll(v, n, 0)
    for y in range(ny):
        row = jnp.where(spot, marks[y : y + 1], 0.0).astype(jnp.bfloat16)
        lb = jnp.dot(row, ones, preferred_element_type=F32)
        total = work[0, y]
        for j in range(1, ENLARGE):
            total = total + work[j, y]
        src, dg, fx, fy, fz = [fields[f, y] for f in range(5)]

        def first(at, is_low):
            if is_low:
                return jnp.where(sub < 3, total[at], jnp.where(sub >= 6, roll(lb[at], 6), roll(fx[at], 3)))
            return jnp.where(sub >= 5, total[at], jnp.where(sub < 2, roll(lb[at], 2), roll(fx[at], 5)))

        def second(at, start):
            values = src[at]
            for n, field in enumerate((dg, fy, fz)):
                begin = (start + 2 * n + 2) % 8
                inside = jnp.logical_or(sub == begin, sub == begin + 1)
                values = jnp.where(inside, roll(field[at], 2 * n + 2), values)
            return values

        lo, hi = slice(0, 8), slice(8, 16)
        for part, high, low in ((0, first(hi, False), first(lo, True)), (1, second(hi, 6), second(lo, 0))):
            even_out[part, y] = jnp.where(even, high, low)
            odd_out[part, y] = jnp.where(even, low, high)


def x_edges(arrays):
    _, nx, ny, nz = arrays[0].shape
    edge = array(2, ny, 8, nz)
    return pl.pallas_call(
        edges_kernel,
        in_specs=hbm(7),
        out_specs=vmem(2),
        out_shape=[edge] * 2,
        scratch_shapes=[
            pltpu.VMEM((ENLARGE, ny, 16, nz), F32),
            pltpu.VMEM((5, ny, 16, nz), F32),
            pltpu.VMEM((ny, nx), jnp.int32),
            pltpu.SemaphoreType.DMA((6,)),
            pltpu.SemaphoreType.DMA((5, 6)),
            pltpu.SemaphoreType.DMA,
        ],
        compiler_params=params(),
        name="x_edges",
    )(*arrays)


def partial_layers(ny, pitch, rows, t, s, src_at, dg, fx, fy, fz):
    nz = t.shape[-1]

    def layer(y, down=True, up=True):
        base = y * pitch
        for r in rows:
            at = base + r
            here = eight(at)
            value, face, fzs = s[here], fx[here], fz[here]
            last = -1 if r == 0 else (1 if r == pitch - 8 else 0)
            total = dg[here] * value - face * edge_near(s, at, 1, last)
            total = total - edge_near(fx, at, -1, last) * edge_near(s, at, -1, last)
            if up:
                total = total - fy[here] * s[eight(at + pitch)]
            if down:
                total = total - fy[eight(at - pitch)] * s[eight(at - pitch)]
            total = total - fzs * pltpu.roll(value, nz - 1, 1) - pltpu.roll(fzs * value, 1, 1)
            t[here] = src_at(y, r) - total

    layer(0, down=False)
    layer(ny - 1, up=False)
    loop(ny - 2, lambda i: layer(i + 1))


def inside_rows(nx):
    return range(PAD + 8, PAD + nx - 8, 8)


def deep_rows(nx):
    return range(PAD + 16, PAD + nx - 16, 8)


def first_power(ny, pitch, rows, p_out, t, fx, fy, dg, fz, lb):
    def layer(i):
        base = (i + 2) * pitch
        for r in rows:
            at = base + r
            last = -1 if r == 0 else (1 if r == pitch - 8 else 0)
            here, below, above = eight(at), eight(at - pitch), eight(at + pitch)
            value = t[here]
            parts = [
                ((dg[here] - SHIFT) * value - along_z(fz[here], value), lb[here]),
                (-fx[here] * edge_near(t, at, 1, last), edge_near(lb, at, 1, last)),
                (-edge_near(fx, at, -1, last) * edge_near(t, at, -1, last), edge_near(lb, at, -1, last)),
                (-fy[here] * t[above], lb[above]),
                (-fy[below] * t[below], lb[below]),
            ]
            for j, values in enumerate(spread(parts)):
                p_out[j, eight(i * pitch + r)] = values

    loop(ny - 4, layer)


def load_kernel(
    gx, gy,
    it_ref, src_in, dg_in, fx_in, fy_in, fz_in, label_hbm,
    t_out, s_out, fx_out, fy_out, dg_out, fz_out, lb_out, src_out, p_out,
    label_ref, sem_label,
):
    _, nx, ny, nz = it_ref.shape
    pitch = nx + 2 * PAD
    label_copy = pltpu.make_async_copy(label_hbm, label_ref, sem_label)
    label_copy.start()

    last_x = lax.axis_index("gx") == gx - 1
    last_y = lax.axis_index("gy") == gy - 1
    top = jnp.logical_and(last_y, iota((8, nz), 0) == 7)
    end = iota((8, nz), 1) == nz - 1

    def add(c):
        for x in range(8):
            for y in range(0, ny, 8):
                place = pl.ds(y * pitch + PAD + c * 8 + x, 8, stride=pitch)
                at = (c * 8 + x, slice(y, y + 8))
                total = it_ref[(0,) + at]
                for j in range(1, ENLARGE):
                    total = total + it_ref[(j,) + at]
                s_out[place, :] = total
                src_out[place, :] = src_in[at]
                dg_out[place, :] = dg_in[at]
                face = fx_in[at]
                if x == 7:
                    face = jnp.where(jnp.logical_and(last_x, c == nx // 8 - 1), 0.0, face)
                fx_out[place, :] = face
                face = fy_in[at]
                fy_out[place, :] = jnp.where(top, 0.0, face) if y == ny - 8 else face
                fz_out[place, :] = jnp.where(end, 0.0, fz_in[at])

    loop(nx // 8, add)
    label_copy.wait()

    spot = iota((nx, nx), 0) == iota((nx, nx), 1)
    ones = jnp.ones((nx, nz), jnp.bfloat16)
    labels = label_ref[...].astype(F32)
    for y in range(ny):
        row = jnp.where(spot, labels[y : y + 1], 0.0).astype(jnp.bfloat16)
        lb_out[y * pitch + PAD : y * pitch + PAD + nx] = jnp.dot(row, ones, preferred_element_type=F32)

    src_at = lambda y, r: src_out[eight(y * pitch + r)]
    partial_layers(ny, pitch, inside_rows(nx), t_out, s_out, src_at, dg_out, fx_out, fy_out, fz_out)
    first_power(ny, pitch, deep_rows(nx), p_out, t_out, fx_out, fy_out, dg_out, fz_out, lb_out)


def load(arrays, labels, gx, gy):
    _, nx, ny, nz = arrays[0].shape
    return pl.pallas_call(
        functools.partial(load_kernel, gx, gy),
        in_specs=vmem(6) + hbm(1),
        out_specs=vmem(9),
        out_shape=[array(ny * (nx + 2 * PAD), nz)] * 8 + [array(ENLARGE, (ny - 4) * (nx + 2 * PAD), nz)],
        scratch_shapes=[
            pltpu.VMEM((ny, nx), jnp.int32),
            pltpu.SemaphoreType.DMA,
        ],
        compiler_params=params(),
        cost_estimate=pl.CostEstimate(flops=4_000_000, bytes_accessed=16_000_000, transcendentals=0),
        name="load",
    )(*arrays, labels)


def blocks_of(nx):
    wide = nx + PAD
    sizes = (wide, wide, wide, wide, nx, nx, nx, 8)
    starts = [sum(sizes[:i]) for i in range(len(sizes) + 1)]
    return wide, starts


def pack_y_edge(ny, nx, dest, is_high, t, s, fy, fx, dg, fz, lb):
    pitch = nx + 2 * PAD
    nz = t.shape[-1]
    wide, starts = blocks_of(nx)
    first = jnp.where(is_high, ny - 1, 0) * pitch
    second = jnp.where(is_high, ny - 2, 1) * pitch
    between = jnp.where(is_high, ny - 2, 0) * pitch

    def line(ref, base):
        return ref[pl.ds(base + (PAD - SENT), wide)]

    def inner(ref, base):
        return ref[pl.ds(pl.multiple_of(base + PAD, 8), nx)]

    parts = (
        line(t, first),
        line(s, first),
        line(fy, first),
        line(fx, first),
        inner(fy, between) * inner(t, second),
        inner(dg, first),
        inner(fz, first),
    )
    for b, values in enumerate(parts):
        dest[starts[b] : starts[b + 1]] = values
    spot = iota((wide, nz), 0) == iota((wide, nz), 1)
    one = jnp.sum(jnp.where(spot, line(lb, first), 0.0), axis=0, keepdims=True)
    two = jnp.sum(jnp.where(spot, line(lb, second), 0.0), axis=0, keepdims=True)
    which = iota((8, nz), 0)
    dest[starts[7] : starts[8]] = jnp.where(which == 0, one, jnp.where(which == 1, two, 0.0))


def partial_kernel(
    gy, nx, ny,
    t_in, s_in, fx_in, fy_in, dg_in, fz_in, lb_in, src_ref, xe_ref, xo_ref,
    t_out, s_out, fx_out, fy_out, dg_out, fz_out, lb_out, ye_ref,
    src_ghost,
):
    nz = t_in.shape[-1]
    pitch = nx + 2 * PAD
    end = iota((8, nz), 1) == nz - 1
    even_x = lax.rem(lax.axis_index("gx"), 2) == 0
    last_y = lax.axis_index("gy") == gy - 1
    roll = lambda v, n: pltpu.roll(v, n, 0)

    def fill(y):
        top = jnp.logical_and(last_y, y == ny - 1)
        for at, is_low in ((0, True), (PAD + nx, False)):
            one, two = [
                jnp.where(even_x == is_low, xo_ref[part, y], xe_ref[part, y]) for part in range(2)
            ]
            here = eight(y * pitch + at)
            s_out[here] = one
            fx_out[here] = roll(one, 3 if is_low else 5)
            lb_out[here] = roll(one, 6 if is_low else 2)
            src_ghost[0 if is_low else 1, y] = two
            dg_out[here] = roll(two, 6)
            fy_out[here] = jnp.where(top, 0.0, roll(two, 4))
            fz_out[here] = jnp.where(end, 0.0, roll(two, 2))

    loop(ny, fill, unroll=2)

    def src_at(y, r):
        if r == 0 or r == pitch - 8:
            return src_ghost[0 if r == 0 else 1, y]
        return src_ref[eight(y * pitch + r)]

    rows = [r for r in range(0, pitch, 8) if r not in inside_rows(nx)]
    partial_layers(ny, pitch, rows, t_out, s_out, src_at, dg_out, fx_out, fy_out, fz_out)
    even_y = lax.rem(lax.axis_index("gy"), 2) == 0
    pack_y_edge(ny, nx, ye_ref, even_y, t_out, s_out, fy_out, fx_out, dg_out, fz_out, lb_out)


def partial_residual(fields, xe, xo, gy, nx, ny):
    nz = xe.shape[-1]
    return pl.pallas_call(
        functools.partial(partial_kernel, gy, nx, ny),
        in_specs=vmem(10),
        out_specs=vmem(8),
        out_shape=[array(*a.shape) for a in fields[:7]] + [array(blocks_of(nx)[1][-1], nz)],
        input_output_aliases={i: i for i in range(7)},
        scratch_shapes=[pltpu.VMEM((2, ny, 8, nz), F32)],
        compiler_params=params(),
        name="partial_residual",
    )(*fields, xe, xo)


def spread(parts):
    fields = []
    for j in range(ENLARGE):
        total = None
        for values, label in parts:
            term = jnp.where(label == float(j), values, 0.0)
            total = term if total is None else total + term
        fields.append(total)
    return fields


def along_z(fz, values):
    nz = values.shape[-1]
    return fz * pltpu.roll(values, nz - 1, 1) + pltpu.roll(fz * values, 1, 1)


def edge_near(ref, at, shift, last):
    if last == shift:
        return pltpu.roll(ref[eight(at)], 1 if shift < 0 else 7, 0)
    return ref[near(at + shift)]


def zeros_like_pairs(nz, count):
    return tuple(jnp.zeros((8, nz), F32) for _ in range(count))


def dot_own(sums, r, label, p):
    b = [jnp.where(label == float(j), r, 0.0) for j in range(ENLARGE)]
    n = len(PAIRS)
    own = tuple(t + v * v for t, v in zip(sums[n:], b))
    return tuple(t + b[j] * p[k] for t, (j, k) in zip(sums, PAIRS)) + own


def dot_pairs(sums, p, q):
    return tuple(t + p[j] * q[k] for t, (j, k) in zip(sums, PAIRS))


def clean_first_kernel(
    ny, nx,
    t_ref, s_ref, fx_ref, fy_ref, dg_ref, fz_ref, lb_ref, p_in,
    p_out, acc_out, yo_ref,
):
    nz = t_ref.shape[-1]
    pitch = nx + 2 * PAD

    rows = [r for r in range(0, pitch, 8) if r not in deep_rows(nx)]
    first_power(ny, pitch, rows, p_out, t_ref, fx_ref, fy_ref, dg_ref, fz_ref, lb_ref)

    def p_dots(i, sums):
        for r in range(PAD, PAD + nx, 8):
            p = [p_out[j, eight(i * pitch + r)] for j in range(ENLARGE)]
            sums = dot_pairs(sums, p, p)
        return sums

    sums = lax.fori_loop(0, ny - 4, p_dots, zeros_like_pairs(nz, len(PAIRS)))
    for n, values in enumerate(sums):
        acc_out[n] = values
    odd_y = lax.rem(lax.axis_index("gy"), 2) == 1
    pack_y_edge(ny, nx, yo_ref, odd_y, t_ref, s_ref, fy_ref, fx_ref, dg_ref, fz_ref, lb_ref)


def clean_second_kernel(
    ny, nx,
    t_ref, fx_ref, fy_ref, dg_ref, fz_ref, lb_ref, p_out,
    q_out, acc_out,
):
    nz = t_ref.shape[-1]
    pitch = nx + 2 * PAD
    chunks = nx // 8

    def second(i):
        for c in range(chunks):
            at = (i + 3) * pitch + PAD + c * 8
            own = (i + 1) * pitch + PAD + c * 8
            here = eight(at)
            dg, fz, fxp, fxm = dg_ref[here], fz_ref[here], fx_ref[here], fx_ref[near(at - 1)]
            fyp, fym = fy_ref[here], fy_ref[eight(at - pitch)]
            for j in range(ENLARGE):
                p = p_out[j, eight(own)]
                q = dg * p - fxp * p_out[j, near(own + 1)] - fxm * p_out[j, near(own - 1)]
                q = q - fyp * p_out[j, eight(own + pitch)] - fym * p_out[j, eight(own - pitch)]
                q_out[j, eight(i * nx + c * 8)] = q - along_z(fz, p)

    loop(ny - 6, second)

    def fields_at(ref, at):
        return [ref[j, eight(at)] for j in range(ENLARGE)]

    def own_dots(i, sums):
        for c in range(chunks):
            row = i * pitch + PAD + c * 8
            shifted = eight(row + 2 * pitch)
            sums = dot_own(sums, t_ref[shifted], lb_ref[shifted], fields_at(p_out, row))
        return sums

    def q_dots(i, sums):
        for c in range(chunks):
            p = fields_at(p_out, (i + 1) * pitch + PAD + c * 8)
            sums = dot_pairs(sums, p, fields_at(q_out, i * nx + c * 8))
        return sums

    slot = 0
    for dots, layers, count in ((own_dots, ny - 4, len(PAIRS) + ENLARGE), (q_dots, ny - 6, len(PAIRS))):
        sums = lax.fori_loop(0, layers, dots, zeros_like_pairs(nz, count))
        for values in sums:
            acc_out[slot] = values
            slot += 1


def clean_first(ext, inner, ny, nx):
    nz = ext[0].shape[-1]
    return pl.pallas_call(
        functools.partial(clean_first_kernel, ny, nx),
        in_specs=vmem(8),
        out_specs=vmem(3),
        out_shape=[
            array(ENLARGE, (ny - 4) * (nx + 2 * PAD), nz),
            array(len(PAIRS), 8, nz),
            array(blocks_of(nx)[1][-1], nz),
        ],
        input_output_aliases={7: 0},
        compiler_params=params(),
        cost_estimate=pl.CostEstimate(flops=20_000_000, bytes_accessed=8_000_000, transcendentals=0),
        name="clean_first",
    )(*ext, inner)


def clean_second(ext, pc, ny, nx):
    t, _, fx, fy, dg, fz, lb = ext
    nz = t.shape[-1]
    return pl.pallas_call(
        functools.partial(clean_second_kernel, ny, nx),
        in_specs=vmem(7),
        out_specs=vmem(2),
        out_shape=[array(ENLARGE, (ny - 6) * nx, nz), array(2 * len(PAIRS) + ENLARGE, 8, nz)],
        compiler_params=params(),
        cost_estimate=pl.CostEstimate(flops=40_000_000, bytes_accessed=12_000_000, transcendentals=0),
        name="clean_second",
    )(t, fx, fy, dg, fz, lb, pc)


def side_of(phase):
    odd = lax.rem(lax.axis_index("gy"), 2)
    return odd if phase else 1 - odd


def edge_kernel(
    ny, nx, phase, devices,
    t_ref, s_ref, fx_ref, fy_ref, dg_ref, fz_ref, lb_ref, pc_ref, acc_pp, acc_ref, pack,
    p_out, q_out, r_out, *rest,
):
    outs, (lb, fx, fy, dg, fz, rows_acc) = rest[:-6], rest[-6:]
    nz = t_ref.shape[-1]
    pitch = nx + 2 * PAD
    chunks = nx // 8
    wide, starts = blocks_of(nx)
    left = PAD - SENT
    side = side_of(phase)

    def packed(b):
        return pack[starts[b] : starts[b + 1]]

    def setup(which):
        first, skip = (0, 2) if which == 0 else (ny - 4, 0)
        for i in range(4):
            source, dest = (first + i) * pitch, (skip + i) * pitch
            for ref, out in ((t_ref, r_out), (lb_ref, lb), (fx_ref, fx), (fy_ref, fy), (dg_ref, dg), (fz_ref, fz)):
                out[dest : dest + pitch] = ref[source : source + pitch]
        first, skip = (0, 4) if which == 0 else (ny - 6, 0)
        for i in range(2):
            source, dest = (first + i) * pitch, (skip + i) * pitch
            p_out[:, dest : dest + pitch] = pc_ref[:, source : source + pitch]
        inner, ghost, far = (2, 1, 0) if which == 0 else (3, 4, 5)
        at = lambda slot, start=left, size=wide: pl.ds(slot * pitch + start, size)
        base = pl.ds((0 if which == 0 else ny - 1) * pitch + left, wide)
        face = packed(2) if which == 0 else fy_ref[base]
        r_out[at(ghost)] = packed(0) + face * s_ref[base]
        r_out[at(inner)] = t_ref[base] + face * packed(1)
        if which == 0:
            fy[at(ghost)] = face
        fy[at(far if which == 0 else ghost)] = jnp.ones((wide, nz), F32)
        r_out[at(far, PAD, nx)] = packed(4)
        fx[at(ghost)] = packed(3)
        dg[at(ghost, PAD, nx)] = packed(5)
        fz[at(ghost, PAD, nx)] = packed(6)
        labels = packed(7)
        spot = iota((wide, nz), 0) == iota((wide, nz), 1)
        for r, slot in ((0, ghost), (1, far)):
            column = jnp.sum(jnp.where(spot, labels[r : r + 1], 0.0), axis=1, keepdims=True)
            lb[at(slot)] = jnp.broadcast_to(column, (wide, nz))

    for which in range(2):
        pl.when(side == which)(functools.partial(setup, which))

    def first(i):
        base = (i + 1 + side) * pitch
        for r in range(0, pitch, 8):
            at = base + r
            here, below, above = eight(at), eight(at - pitch), eight(at + pitch)
            value = r_out[here]
            parts = [
                ((dg[here] - SHIFT) * value - along_z(fz[here], value), lb[here]),
                (-fx[here] * r_out[near(at + 1)], lb[near(at + 1)]),
                (-fx[near(at - 1)] * r_out[near(at - 1)], lb[near(at - 1)]),
                (-fy[here] * r_out[above], lb[above]),
                (-fy[below] * r_out[below], lb[below]),
            ]
            for j, values in enumerate(spread(parts)):
                p_out[j, here] = values

    loop(3, first)

    def second(i):
        for c in range(chunks):
            at = (i + 2 - side) * pitch + PAD + c * 8
            here, below, above = eight(at), eight(at - pitch), eight(at + pitch)
            d, z, fxp, fxm, fyp, fym = dg[here], fz[here], fx[here], fx[near(at - 1)], fy[here], fy[below]
            for j in range(ENLARGE):
                p = p_out[j, here]
                q = d * p - fxp * p_out[j, near(at + 1)] - fxm * p_out[j, near(at - 1)]
                q = q - fyp * p_out[j, above] - fym * p_out[j, below]
                q_out[j, eight(i * nx + c * 8)] = q - along_z(z, p)

    loop(3, second)

    def fields_at(ref, at):
        return [ref[j, eight(at)] for j in range(ENLARGE)]

    def own_dots(i, sums):
        for c in range(chunks):
            at = (i + 2) * pitch + PAD + c * 8
            sums = dot_own(sums, r_out[eight(at)], lb[eight(at)], fields_at(p_out, at))
        return sums

    def p_dots(i, sums):
        for c in range(chunks):
            p = fields_at(p_out, (i + 2) * pitch + PAD + c * 8)
            sums = dot_pairs(sums, p, p)
        return sums

    def q_dots(i, sums):
        for c in range(chunks):
            p = fields_at(p_out, (i + 2 - side) * pitch + PAD + c * 8)
            sums = dot_pairs(sums, p, fields_at(q_out, i * nx + c * 8))
        return sums

    pairs = len(PAIRS)
    span = ENLARGE * ENLARGE
    groups = (
        (0, own_dots, 2, [(acc_ref, i) for i in range(pairs + ENLARGE)]),
        (1, p_dots, 2, [(acc_pp, i) for i in range(pairs)]),
        (2, q_dots, 3, [(acc_ref, pairs + ENLARGE + i) for i in range(pairs)]),
    )
    if phase:
        rows_acc[...] = jnp.zeros_like(rows_acc)

    def put(slot, values):
        rows_acc[slot : slot + 1] = jnp.sum(values, axis=0, keepdims=True)

    for which, dots, layers, stored in groups:
        sums = tuple(ref[i] for ref, i in stored)
        sums = lax.fori_loop(0, layers, dots, sums)
        if not phase:
            out = outs[0] if which == 1 else outs[1]
            for (_, i), values in zip(stored, sums):
                out[i] = values
            continue
        for (j, k), values in zip(PAIRS, sums):
            put(which * span + j * ENLARGE + k, values)
            if j != k:
                put(which * span + k * ENLARGE + j, values)
        for j, values in enumerate(sums[pairs:]):
            put(3 * span + j * ENLARGE + j, values)
    if phase:
        ones = jnp.ones((8, nz), F32)
        flat = lax.dot_general(
            ones, rows_acc[...], (((1,), (1,)), ((), ())), precision=HIGHEST, preferred_element_type=F32
        )
        half = 2 * span
        pair = jnp.where(iota((2, half), 0) == 0, flat[0:2, 0:half], flat[0:2, half : 2 * half])
        for d in range(devices):
            outs[0][d] = pair


def edge_powers(phase, ext, pc, acc_pp, acc, pack, ny, nx, devices):
    nz = pc.shape[-1]
    rows = 6 * (nx + 2 * PAD)
    half = 2 * ENLARGE * ENLARGE
    result = [array(devices, 2, half)] if phase else [array(*acc_pp.shape), array(*acc.shape)]
    return pl.pallas_call(
        functools.partial(edge_kernel, ny, nx, phase, devices),
        in_specs=vmem(11),
        out_specs=vmem(3 + len(result)),
        out_shape=[array(ENLARGE, rows, nz), array(ENLARGE, 3 * nx, nz), array(rows, nz)] + result,
        scratch_shapes=[pltpu.VMEM((rows, nz), F32)] * 5 + [pltpu.VMEM((2 * half, nz), F32)],
        compiler_params=params(),
        cost_estimate=pl.CostEstimate(flops=20_000_000, bytes_accessed=8_000_000, transcendentals=0),
        name=f"edge_powers_{phase}",
    )(*ext, pc, acc_pp, acc, pack)


def solve_columns(parts):
    nz = parts.shape[-1]
    span = ENLARGE * ENLARGE
    v = jnp.sum(parts, axis=0)
    lhs = jnp.concatenate([jnp.broadcast_to(v[0:1], (8, nz)), jnp.broadcast_to(v[1:2], (8, nz))], axis=1)
    source = iota((8, 2 * nz), 1)
    lhs = jnp.where(iota((8, 2 * nz), 0) == lax.rem(source, span) // ENLARGE, lhs, 0.0)
    k = iota((2 * nz, nz), 0)
    n = iota((2 * nz, nz), 1)
    which = k // span
    column = lax.rem(k, ENLARGE)

    def place(block, offset, scale):
        return jnp.where(jnp.logical_and(which == block, n == column + offset), scale, 0.0)

    upper = place(0, 0, 1.0) + place(3, 0, SHIFT) + place(1, 8, 1.0) + place(0, 8, SHIFT) + place(3, 16, 1.0)
    lower = place(1, 0, 1.0) + place(0, 0, SHIFT) + place(2, 8, 1.0) + place(0, 16, 1.0)
    dot = functools.partial(jnp.dot, precision=HIGHEST, preferred_element_type=F32)
    m = jnp.concatenate([dot(lhs, upper), dot(lhs, lower)], axis=0)
    row = iota(m.shape, 0)
    two = 2 * ENLARGE
    columns = [jnp.broadcast_to(m[:, i : i + 1], m.shape) for i in range(two + ENLARGE)]
    for i in range(two):
        inverse = 1.0 / columns[i][i : i + 1]
        for n in range(i + 1, two + ENLARGE):
            scaled = jnp.broadcast_to(columns[n][i : i + 1] * inverse, m.shape)
            columns[n] = jnp.where(row == i, scaled, columns[n] - columns[i] * scaled)
    return columns[two:]


def update_kernel(
    parts_ref, pc_ref, qc_ref, p0_ref, q0_ref, r0_ref, p1_ref, q1_ref, r1_ref, t_ref, lb_ref, it_hbm,
    it_out, r_out, it_ref,
    table, weights, onehot, own, work, r_work, sem_in, sem_out, sem_r,
):
    _, ny, nx, nz = it_ref.shape
    pitch = nx + 2 * PAD
    two = 2 * ENLARGE
    square = ENLARGE * ENLARGE
    chunks = nx // 8

    def copy_in(y):
        return pltpu.make_async_copy(it_hbm.at[:, :, y], it_ref.at[:, y], sem_in.at[y])

    loop(ny, lambda y: copy_in(y).start())

    def copy_out(half, c):
        span, rows = pl.ds(half * 4, 4), pl.ds(pl.multiple_of(c * 8 * ny, 8 * ny), 8 * ny)
        return pltpu.make_async_copy(work.at[span, rows], it_out.at[span, rows], sem_out.at[half, c])

    def copy_r(c):
        rows = pl.ds(pl.multiple_of(c * 8 * ny, 8 * ny), 8 * ny)
        return pltpu.make_async_copy(r_work.at[rows], r_out.at[rows], sem_r.at[c])

    def mark(y):
        lane = iota((nx, nz), 1)
        labels = lb_ref[pl.ds(pl.multiple_of(y * pitch + PAD, 8), nx)]
        chosen = jnp.logical_and(lane < 3 * ENLARGE, lax.rem(lane, ENLARGE).astype(F32) == labels)
        onehot[pl.ds(pl.multiple_of(y * nx, nx), nx)] = jnp.where(chosen, 1.0, 0.0).astype(jnp.bfloat16)

    loop(ny, mark)

    columns = solve_columns(parts_ref[...])
    carried = columns[0]
    for column in columns[1:]:
        carried = carried + column
    weights[...] = jnp.zeros_like(weights)
    for j, column in enumerate(columns + [carried]):
        for k in range(two):
            if j < ENLARGE and k < ENLARGE:
                continue
            slot = j * ENLARGE + k - ENLARGE if j < ENLARGE else square + k
            table[slot] = jnp.broadcast_to(column[k : k + 1], (8, nz))
        mine = column[0:ENLARGE]
        high = mine.astype(jnp.bfloat16).astype(F32)
        mid = (mine - high).astype(jnp.bfloat16).astype(F32)
        at = slice(j * nz, (j + 1) * nz)
        weights[0:8, at] = high
        weights[8:16, at] = mid
        weights[16:24, at] = mine - high - mid
    spread_weights = weights[...].astype(jnp.bfloat16)

    def coefficients(n):
        here = pl.ds(pl.multiple_of(n * 128, 128), 128)
        own[here] = jnp.dot(onehot[here], spread_weights, preferred_element_type=F32)

    loop(ny * nx // 128, coefficients, unroll=2)

    def spots(c, odd, visit):
        x = PAD + c * 8
        for i in range(ny - 6):
            visit(i + 3, pc_ref, (i + 1) * pitch + x, qc_ref, i * nx + c * 8, t_ref, (i + 3) * pitch + x)
        for phase, p_ref, q_ref, r_ref in ((0, p0_ref, q0_ref, r0_ref), (1, p1_ref, q1_ref, r1_ref)):
            side = odd if phase else 1 - odd
            for i in range(3):
                at = (i + 2 - side) * pitch + x
                visit(i + side * (ny - 3), p_ref, at, q_ref, i * nx + c * 8, r_ref, at)

    def place(c, y):
        return pl.ds(c * 8 * ny + y, 8, stride=ny)

    def updates(odd, half):
        js = range(half * 4, half * 4 + 4)
        scales = [[table[j * ENLARGE + k] for k in range(ENLARGE)] for j in js]

        def block(c):
            def visit(y, p_ref, p_at, q_ref, q_at, r_ref, r_at):
                r = r_ref[eight(r_at)]
                at = eight(y * nx + c * 8)
                totals = [it_ref[j, y, eight(c * 8)] + own[at, j * nz : (j + 1) * nz] * r for j in js]
                for k in range(ENLARGE):
                    p = p_ref[k, eight(p_at)]
                    totals = [t + scale[k] * p for t, scale in zip(totals, scales)]
                for j, t in zip(js, totals):
                    work[j, place(c, y), :] = t

            spots(c, odd, visit)
            copy_out(half, c).start()

        loop(chunks, block)

    def residuals(odd):
        scales = [table[square + k] for k in range(two)]

        def block(c):
            def visit(y, p_ref, p_at, q_ref, q_at, r_ref, r_at):
                r = r_ref[eight(r_at)]
                total = r - (SHIFT * own[eight(y * nx + c * 8), ENLARGE * nz : (ENLARGE + 1) * nz]) * r
                for k in range(ENLARGE):
                    total = total - scales[k] * p_ref[k, eight(p_at)]
                    total = total - scales[ENLARGE + k] * q_ref[k, eight(q_at)]
                r_work[place(c, y), :] = total

            spots(c, odd, visit)
            copy_r(c).start()

        loop(chunks, block)

    def run(odd):
        residuals(odd)
        loop(ny, lambda y: copy_in(y).wait())
        updates(odd, 0)
        updates(odd, 1)

    for odd in range(2):
        pl.when(side_of(1) == odd)(functools.partial(run, odd))
    for half in range(2):
        loop(chunks, lambda c, half=half: copy_out(half, c).wait())
    loop(chunks, lambda c: copy_r(c).wait())


def update(parts, pc, qc, edges, t, labels, iterates):
    _, nx, ny, nz = iterates.shape
    rows = nx * ny
    return pl.pallas_call(
        update_kernel,
        in_specs=vmem(11) + hbm(1),
        out_specs=hbm(2),
        out_shape=[array(ENLARGE, rows, nz), array(rows, nz)],
        scratch_shapes=[
            pltpu.VMEM((ENLARGE, ny, nx, nz), F32),
            pltpu.VMEM((ENLARGE * ENLARGE + 2 * ENLARGE, 8, nz), F32),
            pltpu.VMEM((nz, (ENLARGE + 1) * nz), F32),
            pltpu.VMEM((rows, nz), jnp.bfloat16),
            pltpu.VMEM((rows, (ENLARGE + 1) * nz), F32),
            pltpu.VMEM((ENLARGE, rows, nz), F32),
            pltpu.VMEM((rows, nz), F32),
            pltpu.SemaphoreType.DMA((ny,)),
            pltpu.SemaphoreType.DMA((2, nx // 8)),
            pltpu.SemaphoreType.DMA((nx // 8,)),
        ],
        compiler_params=params(),
        name="update",
    )(parts, pc, qc, *edges, t, labels, iterates)


def shards(gx, gy, source, diagonal, face_x, face_y, face_z, iterates, labels):
    _, nx, ny, nz = iterates.shape
    arrays = [pinned(a) for a in (iterates, source, diagonal, face_x, face_y, face_z, labels.T)]
    xe, xo = x_edges(arrays)
    xo = lax.ppermute(xo, "gx", odd_pairs(gx))
    xe = lax.ppermute(xe, "gx", even_pairs(gx))
    direct = [iterates, source, diagonal, face_x, face_y, face_z]
    *fields, inner = load(direct, arrays[6], gx, gy)
    *ext, ye = partial_residual(fields, xe, xo, gy, nx, ny)
    ye = lax.ppermute(ye, "gy", even_pairs(gy))
    pc, acc_pp, yo = clean_first(ext, inner, ny, nx)
    yo = lax.ppermute(yo, "gy", odd_pairs(gy))
    qc, acc = clean_second(ext, pc, ny, nx)
    p0, q0, r0, acc_pp, acc = edge_powers(0, ext, pc, acc_pp, acc, ye, ny, nx, gx * gy)
    p1, q1, r1, gram = edge_powers(1, ext, pc, acc_pp, acc, yo, ny, nx, gx * gy)
    parts = lax.all_to_all(gram, ("gx", "gy"), 0, 0, tiled=True)
    edges = (p0, q0, r0, p1, q1, r1)
    new_iterates, new_residual = update(parts, pc, qc, edges, ext[0], ext[-1], arrays[0])
    return new_iterates.reshape(iterates.shape), new_residual.reshape(source.shape)


def solution(mesh):
    placed = (
        P("gx", "gy", None),
        P("gx", "gy", None),
        P("gx", "gy", None),
        P("gx", "gy", None),
        P("gx", "gy", None),
        P(None, "gx", "gy", None),
        P("gx", "gy"),
    )
    return jax.shard_map(
        functools.partial(shards, mesh.shape["gx"], mesh.shape["gy"]),
        mesh=mesh,
        in_specs=placed,
        out_specs=(P(None, "gx", "gy", None), P("gx", "gy", None)),
        check_vma=False,
    )
```
